512 devices in a mesh: prow: 16 (over y, core), pcol: 32 (over z, x).
Axes of the slice: x: 4, y: 8, z: 8, core: 2. Of those that a mesh axis runs over, the one named last changes fastest.
Arguments:
- matrix: bfloat16 [2, 16, 512, 2, 32, 512], P(None, 'prow', None, None, 'pcol'), may hold values from -6 to 6
- pivots: int32 [2, 512], replicated, may hold values from 0 to 16383, as said below
- lower_inverse: bfloat16 [2, 512, 512], replicated, as said below
- upper_inverse: bfloat16 [2, 512, 512], replicated, as said below
Outputs:
- factored: bfloat16 [2, 16, 512, 2, 32, 512], P(None, 'prow', None, None, 'pcol')
The draws below stay inside these ranges and needn't reach their ends.
Inputs may be any that keep to these rules, and one draw needn't show every extreme that they name: Each row of pivots holds 512 distinct row indices; those of panel k are k * 512 or more. lower_inverse[k] is unit lower triangular. upper_inverse[k] is upper triangular with a positive diagonal.
All inputs are finite; a program needn't handle non-finite values.
Results may differ from the reference program's by a relative error of at most 0.0084.
Values may be sent and summed in bfloat16 or wider, within the bound.
A program may use at most 64 MiB of HBM per device.

```python
import math
import jax
import jax.numpy as jnp
from jax import lax

NB = 512
PANELS = 2
CB_DEV = 2
RB_DEV = 2
ROWS = 16384
COLS = 32768
N_PROW = 16
N_PCOL = 32


def draw_pivots(key, part):
    lists = []
    for step_index in range(PANELS):
        first_row = step_index * NB
        span_rows = ROWS - first_row
        order_rows = jax.random.permutation(jax.random.fold_in(key, step_index), span_rows).astype(jnp.int32)
        if step_index == 0:
            places = jnp.arange(span_rows, dtype=jnp.int32)
            position = jnp.argmax(order_rows == span_rows - 1).astype(jnp.int32)
            slot_index = jax.random.randint(jax.random.fold_in(key, 101), (), 0, NB).astype(jnp.int32)
            held_value = order_rows[slot_index]
            order_rows = jnp.where(places == slot_index, span_rows - 1, jnp.where(places == position, held_value, order_rows))
            offset_two = jax.random.randint(jax.random.fold_in(key, 202), (), 1, NB).astype(jnp.int32)
            slot_two = (slot_index + offset_two) % NB
            position_two = jnp.argmax(order_rows == 0).astype(jnp.int32)
            held_two = order_rows[slot_two]
            order_rows = jnp.where(places == slot_two, 0, jnp.where(places == position_two, held_two, order_rows))
        lists.append(order_rows[:NB] + first_row)
    return jnp.stack(lists).astype(jnp.int32)


def draw_lower_inverse(key, part):
    noise = jax.random.normal(key, (PANELS, NB, NB), jnp.float32)
    row_ids = jnp.arange(NB)[:, None]
    col_ids = jnp.arange(NB)[None, :]
    lower_part = jnp.where(row_ids > col_ids, noise * (0.7 / math.sqrt(NB)), 0.0)
    lower_part = jnp.where(row_ids == col_ids, 1.0, lower_part)
    return lower_part.astype(jnp.bfloat16)


def draw_upper_inverse(key, part):
    noise = jax.random.normal(key, (PANELS, NB, NB), jnp.float32)
    scales = jnp.exp(jax.random.uniform(jax.random.fold_in(key, 3), (PANELS, 1, NB), jnp.float32, math.log(0.5), math.log(1.5))) / math.sqrt(NB)
    row_ids = jnp.arange(NB)[:, None]
    col_ids = jnp.arange(NB)[None, :]
    upper_part = jnp.where(row_ids < col_ids, noise / NB, 0.0)
    upper_part = jnp.where(row_ids == col_ids, scales, upper_part)
    return upper_part.astype(jnp.bfloat16)


def levels(key, extent, pieces, smallest, high):
    def one(dim, blocks):
        steps = jax.random.uniform(jax.random.fold_in(jax.random.fold_in(key, 6), dim), (blocks,), jnp.float32, smallest / len(pieces), high / len(pieces))
        return jnp.repeat(jnp.exp(steps), extent[dim] // blocks).reshape((-1,) + (1,) * (len(extent) - dim - 1))

    factor_of = one(*pieces[0])
    for cut in pieces[1:]:
        factor_of = factor_of * one(*cut)
    return factor_of


def centred(stream_key, dims, deviation, limit, cuts=(), kind=jnp.bfloat16):
    entries = deviation * jax.random.normal(stream_key, dims, jnp.float32)
    if cuts:
        entries = entries * levels(stream_key, dims, cuts, -0.22, 0.18)
    return jnp.clip(entries, -limit, limit).astype(kind)


def setup_inputs(seed: int = 0) -> dict:
    arg_keys = jax.random.split(jax.random.key(seed), 5)
    matrix = centred(arg_keys[0], (RB_DEV, N_PROW, NB, CB_DEV, N_PCOL, NB), 1.0, 6.0, ((1, 16), (4, 32)))
    pivots = draw_pivots(jax.random.fold_in(arg_keys[4], 71), 0)
    lower_inverse = draw_lower_inverse(jax.random.fold_in(arg_keys[4], 71), 0)
    upper_inverse = draw_upper_inverse(jax.random.fold_in(arg_keys[4], 71), 0)
    return {"matrix": matrix, "pivots": pivots, "lower_inverse": lower_inverse, "upper_inverse": upper_inverse}


def interchange(full_matrix, sources, first_row):
    top_ids = first_row + jnp.arange(NB, dtype=jnp.int32)
    chosen = jnp.any(sources[None, :] == top_ids[:, None], axis=1)
    leftover = jnp.logical_not(chosen)
    left_rank = (jnp.cumsum(leftover.astype(jnp.int32)) - 1).astype(jnp.int32)
    vacated = sources >= first_row + NB
    vac_rank = (jnp.cumsum(vacated.astype(jnp.int32)) - 1).astype(jnp.int32)
    match_table = leftover[None, :] & (left_rank[None, :] == vac_rank[:, None])
    receive = jnp.sum(jnp.where(match_table, top_ids[None, :], 0), axis=1).astype(jnp.int32)
    new_top = full_matrix[sources]
    moved_rows = full_matrix[receive]
    full_matrix = full_matrix.at[sources].set(jnp.where(vacated[:, None], moved_rows, new_top))
    return full_matrix.at[top_ids].set(new_top)


def reference(matrix, pivots, lower_inverse, upper_inverse):
    full_matrix = matrix.reshape(ROWS, COLS)
    rows_id = jnp.arange(ROWS, dtype=jnp.int32)
    cols_id = jnp.arange(COLS, dtype=jnp.int32)
    for step_index in range(PANELS):
        first_row = step_index * NB
        past_row = first_row + NB
        full_matrix = interchange(full_matrix, pivots[step_index], first_row)
        below_rows = rows_id >= past_row
        factor = jnp.dot(full_matrix[:, first_row:past_row], upper_inverse[step_index], preferred_element_type=jnp.float32).astype(jnp.bfloat16)
        factor = jnp.where(below_rows[:, None], factor, jnp.zeros_like(factor))
        top_rows = full_matrix[first_row:past_row]
        upper_rows = jnp.dot(lower_inverse[step_index], top_rows, preferred_element_type=jnp.float32).astype(jnp.bfloat16)
        right_cols = cols_id >= past_row
        row_block = jnp.where(right_cols[None, :], upper_rows, top_rows)
        update = jnp.where(right_cols[None, :], upper_rows, jnp.zeros_like(upper_rows))

        def column_block(block_index, current):
            first_col = block_index * NB
            column_slab = lax.dynamic_slice_in_dim(current, first_col, NB, 1)
            update_part = lax.dynamic_slice_in_dim(update, first_col, NB, 1)
            column_slab = (column_slab.astype(jnp.float32) - jnp.dot(factor, update_part, preferred_element_type=jnp.float32)).astype(current.dtype)
            return lax.dynamic_update_slice_in_dim(current, column_slab, first_col, 1)

        full_matrix = lax.fori_loop(0, COLS // NB, column_block, full_matrix)
        panel_cols = jnp.where(below_rows[:, None], factor, full_matrix[:, first_row:past_row])
        full_matrix = full_matrix.at[:, first_row:past_row].set(panel_cols)
        full_matrix = full_matrix.at[first_row:past_row].set(row_block)
    return full_matrix.reshape(matrix.shape)
```

```python
import jax
import jax.numpy as jnp
from jax import lax
from jax.experimental import pallas as pl
from jax.experimental.pallas import tpu as pltpu
from jax.sharding import PartitionSpec as P

NB = 512
CORES = 2
NX = 4
CAP = 96
DCAP = 56
PA = 16
PB = 24
MESH = pl.DeviceIdType.MESH
ANY = pl.BlockSpec(memory_space=pl.ANY)


class Ring:
    def __init__(self, n, pos, goto, item, send, recv, fresh=None, arrived=None):
        self.n, self.pos, self.goto, self.item = n, pos, goto, item
        self.send, self.recv = send, recv
        self.fresh, self.arrived = fresh, arrived
        self.got = [0, 0]

    def carries(self, way, hop, half):
        return hop < self.n // 2 or (hop == self.n // 2 and half == way)

    def copy(self, way, hop, half):
        step = 1 if way == 0 else -1
        index = lax.rem(self.pos + self.n - step * (hop - 1), self.n)
        target = lax.rem(self.pos + self.n + step, self.n)
        src = self.item(index, half)
        if hop == 1 and self.fresh is not None:
            src = self.fresh(half)
        return pltpu.make_async_remote_copy(
            src_ref=src,
            dst_ref=self.item(index, half),
            send_sem=self.send.at[way, hop - 1, half],
            recv_sem=self.recv.at[way, hop - 1, half],
            device_id=self.goto(target),
            device_id_type=MESH,
        )

    def landed(self, way, hop, half):
        step = 1 if way == 0 else -1
        index = lax.rem(self.pos + self.n - step * hop, self.n)
        ref = self.item(index, half)
        return index, ref, pltpu.make_async_remote_copy(
            src_ref=ref,
            dst_ref=ref,
            send_sem=self.send.at[way, hop - 1, half],
            recv_sem=self.recv.at[way, hop - 1, half],
            device_id=self.goto(lax.rem(self.pos + 1, self.n)),
            device_id_type=MESH,
        )

    def start(self, half):
        for way in (0, 1):
            self.copy(way, 1, half).start()

    def step(self, way, hop, half):
        index, ref, arrival = self.landed(way, hop, half)
        arrival.wait_recv()
        if self.carries(way, hop + 1, half):
            self.copy(way, hop + 1, half).start()
        self.got[half] += 1
        if self.arrived is not None:
            self.arrived(index, ref, way, hop, half)

    def events(self, t0, dt):
        out = []
        for half in (0, 1):
            for hop in range(1, self.n // 2 + 1):
                for way in (0, 1):
                    if self.carries(way, hop, half):
                        when = t0[half] + dt * hop
                        out.append((when, lambda w=way, h=hop, f=half: self.step(w, h, f)))
        return out

    def complete(self, half):
        assert self.got[half] == self.n - 1

    def drain(self):
        for half in (0, 1):
            for hop in range(1, self.n // 2 + 1):
                for way in (0, 1):
                    if self.carries(way, hop, half):
                        self.copy(way, hop, half).wait_send()


def run_events(events):
    for _, act in sorted(events, key=lambda e: e[0]):
        act()


class RowExchange:
    def __init__(self, ny, sent, spread, rows, moved, sems):
        self.ny, self.sent, self.spread, self.rows, self.moved = ny, sent, spread, rows, moved
        (self.rs, self.rr, self.fs, self.fr, self.os, self.orr, self.ls, self.es, self.er) = sems
        prow = lax.axis_index("prow")
        self.y, self.c = lax.div(prow, CORES), lax.rem(prow, CORES)
        self.partner = {"prow": self.y * CORES + 1 - self.c}
        self.ring = Ring(
            ny, self.y,
            lambda i: {"prow": i * CORES + self.c},
            lambda i, half: rows.at[i * CORES + self.c, half],
            self.rs, self.rr,
            fresh=lambda half: sent.at[half],
            arrived=self.forward,
        )
        self.forwards = []

    def barrier_peers(self):
        ids = [{"prow": lax.rem(self.y + k, self.ny) * CORES + c} for k in range(1, self.ny) for c in (0, 1)]
        return ids + [self.partner]

    def forward_copy(self, index, way, hop, half):
        return pltpu.make_async_remote_copy(
            src_ref=self.rows.at[index * CORES + self.c, half],
            dst_ref=self.rows.at[index * CORES + self.c, half],
            send_sem=self.fs.at[way, hop - 1, half],
            recv_sem=self.fr.at[way, hop - 1, half],
            device_id=self.partner,
            device_id_type=MESH,
        )

    def forward(self, index, ref, way, hop, half):
        copy = self.forward_copy(index, way, hop, half)
        copy.start()
        self.forwards.append((copy, index, way, hop, half))

    def own_copies(self):
        mine = self.rows.at[self.y * CORES + self.c]
        local = pltpu.make_async_copy(self.sent, mine, self.ls.at[0])
        across = pltpu.make_async_remote_copy(
            src_ref=self.sent, dst_ref=mine, send_sem=self.os, recv_sem=self.orr,
            device_id=self.partner, device_id_type=MESH,
        )
        return local, across

    def spread_copy(self, k, core):
        to = lax.rem(self.y + k, self.ny) * CORES + core
        return pltpu.make_async_remote_copy(
            src_ref=self.spread.at[to], dst_ref=self.moved.at[self.c],
            send_sem=self.es.at[k, core], recv_sem=self.er.at[self.c],
            device_id={"prow": to}, device_id_type=MESH,
        )

    def spread_partner(self):
        to = 1 - self.c
        return pltpu.make_async_remote_copy(
            src_ref=self.spread.at[to], dst_ref=self.moved.at[self.c],
            send_sem=self.es.at[0, 0], recv_sem=self.er.at[self.c],
            device_id=self.partner, device_id_type=MESH,
        )

    def spread_own(self):
        return pltpu.make_async_copy(self.spread.at[self.c], self.moved.at[self.c], self.er.at[self.c])

    def begin(self):
        for half in (0, 1):
            self.ring.start(half)
        for copy in self.own_copies():
            copy.start()

    def spread_some(self, ks):
        @pl.when(self.y == 0)
        def _():
            for k in ks:
                for core in (0, 1):
                    self.spread_copy(k, core).start()

    def spread_near(self):
        @pl.when(self.y == 0)
        def _():
            self.spread_partner().start()
            self.spread_own().start()

    def events(self, dt):
        half_n = self.ny // 2
        out = [(-1.0, self.begin), (3.9 * dt, self.spread_near)]
        order = [half_n] + [k for d in range(half_n - 1, 0, -1) for k in (d, self.ny - d)]
        for i, k in enumerate(order):
            out.append((0.1 + i * 0.5 * dt, lambda k=k: self.spread_some([k])))
        return out + self.ring.events([0.0, 0.3 * dt], dt)

    def finish(self):
        local, across = self.own_copies()
        local.wait()
        across.wait()
        self.ring.drain()
        for copy, index, way, hop, half in self.forwards:
            copy.wait_send()
        for copy, index, way, hop, half in self.forwards:
            ref = self.rows.at[index * CORES + 1 - self.c, half]
            pltpu.make_async_remote_copy(
                src_ref=ref, dst_ref=ref,
                send_sem=self.fs.at[way, hop - 1, half], recv_sem=self.fr.at[way, hop - 1, half],
                device_id=self.partner, device_id_type=MESH,
            ).wait_recv()
        for core in (0, 1):
            ref = self.moved.at[core]
            pltpu.make_async_copy(ref, ref, self.er.at[core]).wait()

        @pl.when(self.y == 0)
        def _():
            for k in range(1, self.ny):
                for core in (0, 1):
                    self.spread_copy(k, core).wait_send()
            self.spread_partner().wait_send()


def exchange_sems(ny):
    dma = pltpu.SemaphoreType.DMA
    return [
        dma((2, ny // 2, 2)), dma((2, ny // 2, 2)),
        dma((2, ny // 2, 2)), dma((2, ny // 2, 2)),
        dma, dma, dma((1,)), dma((ny, CORES)), dma((CORES,)),
    ]


def meet(peers):
    barrier = pltpu.get_barrier_semaphore()
    for peer in peers:
        pl.semaphore_signal(barrier, inc=1, device_id=peer, device_id_type=MESH)
    pl.semaphore_wait(barrier, len(peers))


def exchange_kernel(ny, sent, spread, rows, moved, *sems):
    ex = RowExchange(ny, sent, spread, rows, moved, sems)
    meet(ex.barrier_peers())
    run_events(ex.events(3.8))
    ex.finish()


def row_exchange(sent, spread, ny, cid):
    width = sent.shape[-1]
    return pl.pallas_call(
        lambda *refs: exchange_kernel(ny, *refs),
        out_shape=(
            jax.ShapeDtypeStruct((ny * CORES, 2, CAP // 2, width), jnp.bfloat16),
            jax.ShapeDtypeStruct((CORES, DCAP, width), jnp.bfloat16),
        ),
        in_specs=[ANY, ANY],
        out_specs=(ANY, ANY),
        scratch_shapes=exchange_sems(ny),
        compiler_params=pltpu.CompilerParams(collective_id=cid, has_side_effects=True),
        name="row_exchange_%d" % cid,
    )(sent, spread)


def spread_kernel(ny, nz, nexch, *refs):
    src_a, src_b, sent, spread, buf_a, buf_b, other, rows, moved = refs[:9]
    sems = refs[9 : 9 + nexch]
    (axs, axr, azs, azr, bzs, bzr, bxs, bxr, ss, sr, ts, tr) = refs[9 + nexch :]
    ex = RowExchange(ny, sent, spread, rows, moved, sems)
    pcol = lax.axis_index("pcol")
    n = nz * NX
    z, x = lax.div(pcol, NX), lax.rem(pcol, NX)

    barrier = pltpu.get_barrier_semaphore()

    def signal(peer):
        pl.semaphore_signal(barrier, inc=1, device_id=peer, device_id_type=MESH)

    near = ex.barrier_peers()
    near += [{"pcol": z * NX + lax.rem(x + d, NX)} for d in (1, NX - 1)]
    near += [{"pcol": lax.rem(z + d, nz) * NX + x} for d in (1, nz - 1)]
    for peer in near:
        signal(peer)
    for root in (0, 1):
        @pl.when(pcol == root)
        def _():
            for k in range(1, n):
                signal({"pcol": lax.rem(pcol + k, n)})

        @pl.when(pcol != root)
        def _():
            signal({"pcol": root})

    @pl.when(pcol < 2)
    def _():
        pl.semaphore_wait(barrier, len(near) + n)

    @pl.when(pcol >= 2)
    def _():
        pl.semaphore_wait(barrier, len(near) + 2)

    def scatter_copies(k):
        to = lax.rem(pcol + k, n)
        tz, tx = lax.div(to, NX), lax.rem(to, NX)
        args = dict(device_id={"pcol": to}, device_id_type=MESH)
        a = pltpu.make_async_remote_copy(
            src_ref=src_a.at[tz, tx], dst_ref=buf_a.at[pcol, tz, tx],
            send_sem=ss.at[k, 0], recv_sem=sr.at[0, pcol], **args)
        b = pltpu.make_async_remote_copy(
            src_ref=src_b.at[tx, tz], dst_ref=buf_b.at[pcol, tx, tz],
            send_sem=ss.at[k, 1], recv_sem=sr.at[1, pcol], **args)
        return a, b

    def scatter():
        @pl.when(pcol < 2)
        def _():
            for which in (0, 1):
                for k in range(1, n):
                    scatter_copies(k)[which].start()
            pltpu.make_async_copy(src_a.at[z, x], buf_a.at[pcol, z, x], sr.at[0, pcol]).start()
            pltpu.make_async_copy(src_b.at[x, z], buf_b.at[pcol, x, z], sr.at[1, pcol]).start()

    def to_x(i):
        return {"pcol": z * NX + i}

    def to_z(i):
        return {"pcol": i * NX + x}

    ax = Ring(NX, x, to_x, lambda i, h: buf_a.at[h, z, i], axs, axr)
    az = Ring(nz, z, to_z, lambda i, h: buf_a.at[h, i], azs, azr)
    bz = Ring(nz, z, to_z, lambda i, h: buf_b.at[h, x, i], bzs, bzr)
    bx = Ring(NX, x, to_x, lambda i, h: buf_b.at[h, i], bxs, bxr)

    def own(which, half):
        ref = buf_a.at[half, z, x] if which == 0 else buf_b.at[half, x, z]
        pltpu.make_async_copy(ref, ref, sr.at[which, half]).wait()

    def begin(ring, half, which=None, after=None):
        if which is not None:
            own(which, half)
        if after is not None:
            after.complete(half)
        ring.start(half)

    def across(half):
        return pltpu.make_async_remote_copy(
            src_ref=buf_a.at[half, pl.ds(0, nz // 2)], dst_ref=other.at[half],
            send_sem=ts.at[half], recv_sem=tr.at[half],
            device_id=ex.partner, device_id_type=MESH)

    def send_other(half):
        az.complete(half)
        across(half).start()

    events = [(-0.5, scatter)]
    events += ex.events(3.8)
    events += [(5.0 + h * 0.1, lambda h=h: begin(ax, h, which=0)) for h in (0, 1)]
    events += ax.events([5.0, 5.2], 1.8)
    events += [(7.0 + h * 0.1, lambda h=h: begin(bz, h, which=1)) for h in (0, 1)]
    events += bz.events([7.2, 7.4], 2.2)
    events += [(9.0 + h * 0.1, lambda h=h: begin(az, h, after=ax)) for h in (0, 1)]
    events += az.events([9.2, 9.5], 3.4)
    events += [(16.5 + h * 0.1, lambda h=h: begin(bx, h, after=bz)) for h in (0, 1)]
    events += bx.events([17.0, 18.0], 6.0)
    events += [(25.0 + h * 0.1, lambda h=h: send_other(h)) for h in (0, 1)]
    run_events(events)
    ex.finish()
    for ring in (ax, az, bz, bx):
        for half in (0, 1):
            ring.complete(half)
        ring.drain()
    for half in (0, 1):
        across(half).wait()

    @pl.when(pcol < 2)
    def _():
        for k in range(1, n):
            for copy in scatter_copies(k):
                copy.wait_send()


def panel_spread(src_a, src_b, sent, spread, ny, nz, cid):
    width = sent.shape[-1]
    dma = pltpu.SemaphoreType.DMA
    sems = exchange_sems(ny)
    return pl.pallas_call(
        lambda *refs: spread_kernel(ny, nz, len(sems), *refs),
        out_shape=(
            jax.ShapeDtypeStruct((2, nz, NX, PA, NB), jnp.bfloat16),
            jax.ShapeDtypeStruct((2, NX, nz, PB, NB), jnp.bfloat16),
            jax.ShapeDtypeStruct((2, nz // 2, NX, PA, NB), jnp.bfloat16),
            jax.ShapeDtypeStruct((ny * CORES, 2, CAP // 2, width), jnp.bfloat16),
            jax.ShapeDtypeStruct((CORES, DCAP, width), jnp.bfloat16),
        ),
        in_specs=[ANY] * 4,
        out_specs=(ANY,) * 5,
        scratch_shapes=sems
        + [dma((2, NX // 2, 2)), dma((2, NX // 2, 2)), dma((2, nz // 2, 2)), dma((2, nz // 2, 2))]
        + [dma((2, nz // 2, 2)), dma((2, nz // 2, 2)), dma((2, NX // 2, 2)), dma((2, NX // 2, 2))]
        + [dma((nz * NX, 2)), dma((2, 2)), dma((2,)), dma((2,))],
        compiler_params=pltpu.CompilerParams(collective_id=cid, has_side_effects=True),
        name="panel_spread_%d" % cid,
    )(src_a, src_b, sent, spread)


def count_before(flags):
    n = flags.shape[0]
    ahead = jnp.arange(n)[None, :] < jnp.arange(n)[:, None]
    return jnp.sum((ahead & flags[None, :]).astype(jnp.int32), axis=1)


def pairing(sources, first_row):
    top_ids = first_row + jnp.arange(NB, dtype=jnp.int32)
    leftover = jnp.logical_not(jnp.any(sources[None, :] == top_ids[:, None], axis=1))
    left_rank = count_before(leftover)
    vacated = sources >= first_row + NB
    vac_rank = count_before(vacated)
    table = leftover[None, :] & (left_rank[None, :] == vac_rank[:, None])
    return jnp.sum(jnp.where(table, top_ids[None, :], 0), axis=1)


def lookup(keys, names, values):
    hit = keys[:, None] == names[None, :]
    found = jnp.sum(jnp.where(hit, values[None, :], 0), axis=1)
    return jnp.where(jnp.any(hit, axis=1), found, keys)


def rank_in(group):
    n = group.shape[0]
    ahead = jnp.arange(n)[None, :] < jnp.arange(n)[:, None]
    same = group[None, :] == group[:, None]
    return jnp.sum((same & ahead).astype(jnp.int32), axis=1)


def slot_values(keys, values, wanted):
    hit = wanted[:, None] == keys[None, :]
    return jnp.sum(jnp.where(hit, values[None, :] + 1, 0), axis=1) - 1


def one_hot(index, n):
    return (index[:, None] == jnp.arange(n, dtype=jnp.int32)[None, :]).astype(jnp.bfloat16)


def dot(a, b):
    return jnp.dot(a, b, preferred_element_type=jnp.float32)


def bdot(a, b):
    return dot(a, b).astype(jnp.bfloat16)


def per_device(matrix, pivots, lower_inverse, upper_inverse):
    nprow, npcol = lax.axis_size("prow"), lax.axis_size("pcol")
    ny, nz = nprow // CORES, npcol // NX
    prow, pcol = lax.axis_index("prow"), lax.axis_index("pcol")
    core = lax.rem(prow, CORES)
    tiles = [matrix[:, 0, :, d, 0, :].reshape(2 * NB, NB) for d in (0, 1)]

    s0, s1 = pivots[0], pivots[1]
    receive0, receive1 = pairing(s0, 0), pairing(s1, NB)
    src1 = lookup(s1, s0, receive0)
    from1 = lookup(receive1, s0, receive0)
    again = jnp.any(s0[:, None] == s1[None, :], axis=1)
    big = jnp.int32(1 << 20)

    def owner(rows):
        return lax.rem(rows // NB, nprow)

    def local(rows):
        return rows // (NB * nprow) * NB + lax.rem(rows, NB)

    t_src = jnp.concatenate([s0, src1])
    t_owner = owner(t_src)
    t_rank = rank_in(t_owner)
    t_local = local(t_src)
    d_dst = jnp.concatenate([s0, s1])
    d_src = jnp.concatenate([receive0, from1])
    d_valid = (d_dst >= 2 * NB) & jnp.concatenate([jnp.logical_not(again), jnp.ones((NB,), jnp.bool_)])
    d_core = d_src // NB
    d_owner = owner(d_dst)
    d_rank = rank_in(jnp.where(d_valid, d_owner * CORES + d_core, -1))
    d_local = local(d_dst)
    rounds = jnp.maximum(
        jnp.max(t_rank) // CAP, jnp.max(jnp.where(d_valid, d_rank, 0)) // DCAP
    ) + 1

    def plan(r):
        t_in = (t_rank // CAP) == r
        t_slot = t_owner * CAP + lax.rem(t_rank, CAP)
        d_in = d_valid & ((d_rank // DCAP) == r)
        d_slot = (d_owner * CORES + d_core) * DCAP + lax.rem(d_rank, DCAP)
        t_key = jnp.where(t_in, t_slot, big)
        d_key = jnp.where(d_in, d_slot, big)
        send_sel = one_hot(slot_values(t_key, t_local, prow * CAP + jnp.arange(CAP, dtype=jnp.int32)), 2 * NB)
        place = one_hot(jnp.where(t_in, t_slot, -1), nprow * CAP)
        every = jnp.arange(nprow * DCAP, dtype=jnp.int32)
        wanted = (every // DCAP * CORES + core) * DCAP + lax.rem(every, DCAP)
        spread_sel = one_hot(lax.rem(slot_values(d_key, d_src + NB, wanted), NB + 0) * 1, NB)
        have = slot_values(d_key, d_src, wanted) >= 0
        spread_sel = jnp.where(have[:, None], spread_sel, jnp.zeros_like(spread_sel))
        mine = prow * CORES * DCAP + jnp.arange(CORES * DCAP, dtype=jnp.int32)
        into = slot_values(d_key, d_local, mine)
        insert = (jnp.arange(2 * NB, dtype=jnp.int32)[:, None] == into[None, :]).astype(jnp.bfloat16)
        hit = jnp.any(insert > 0, axis=1)
        return send_sel, place, spread_sel, insert, hit

    def pack(sel, spread_sel, tile):
        width = tile.shape[1]
        sent = bdot(sel, tile).reshape(2, CAP // 2, width)
        spread = lax.cond(
            prow < CORES,
            lambda: bdot(spread_sel, tile[:NB]),
            lambda: jnp.zeros((nprow * DCAP, width), jnp.bfloat16),
        ).reshape(nprow, DCAP, width)
        return sent, spread

    def unpack_rows(place, rows):
        return bdot(place, rows.reshape(nprow * CAP, rows.shape[-1]))

    def unpack_moved(insert, hit, moved, tile):
        new = bdot(insert, moved.reshape(CORES * DCAP, moved.shape[-1]))
        return jnp.where(hit[:, None], new, tile)

    send_sel, place, spread_sel, insert, hit = plan(0)
    packs = [pack(send_sel, spread_sel, tile) for tile in tiles]
    rows0, moved0 = row_exchange(*packs[0], ny, 0)
    top0 = unpack_rows(place, rows0)
    tile0 = unpack_moved(insert, hit, moved0, tiles[0])

    def more(top0, tile0):
        whole = jnp.concatenate(tiles, axis=1)

        def body(state):
            r, top, tile = state
            send_sel, place, spread_sel, insert, hit = plan(r)
            rows, moved = row_exchange(*pack(send_sel, spread_sel, whole), ny, 1)
            return r + 1, top + unpack_rows(place, rows), unpack_moved(insert, hit, moved, tile)

        start = jnp.concatenate([top0, jnp.zeros_like(top0)], axis=1), jnp.concatenate([tile0, tiles[1]], axis=1)
        _, top, tile = lax.while_loop(lambda s: s[0] < rounds, body, (jnp.int32(1),) + start)
        return top[:, :NB], top[:, NB:], tile[:, :NB], tile[:, NB:]

    def none(top0, tile0):
        return top0, jnp.zeros_like(top0), tile0, tiles[1]

    top0, extra, tile0, tile1 = lax.cond(rounds > 1, more, none, top0, tile0)

    panel_top = jnp.where(pcol == 0, top0[NB:], top0[:NB])
    quarter = NB // CORES
    part = lax.dynamic_slice_in_dim(panel_top, core * quarter, quarter, 0)
    src_a = jnp.concatenate([part, tile0[:quarter]], axis=0).reshape(nz, NX, PA, NB)
    src_b = tile0[quarter:].reshape(NX, nz, PB, NB)
    buf_a, buf_b, other, rows1, moved1 = panel_spread(src_a, src_b, *packs[1], ny, nz, 2)

    top1 = unpack_rows(place, rows1) + extra
    tile1 = unpack_moved(insert, hit, moved1, tile1)
    flat_a = buf_a.reshape(2, NB, NB)
    flat_b = buf_b.reshape(2, 2 * NB - quarter, NB)
    other = other.reshape(2, quarter, NB)
    raw = [jnp.concatenate([flat_a[k, quarter:], flat_b[k]], axis=0) for k in (0, 1)]
    first = jnp.where(core == 0, flat_a[:, :quarter], other)
    second = jnp.where(core == 0, other, flat_a[:, :quarter])
    tops = jnp.concatenate([first, second], axis=1)

    l0, l1, u0, u1 = lower_inverse[0], lower_inverse[1], upper_inverse[0], upper_inverse[1]
    factor0 = bdot(raw[0], u0)
    corner = bdot(tops[0], u0)
    upper_panel = bdot(l0, tops[1])
    panel1 = (raw[1].astype(jnp.float32) - dot(factor0, upper_panel)).astype(jnp.bfloat16)
    factor1 = bdot(panel1, u1)
    out = []
    for d, (top, tile) in enumerate(((top0, tile0), (top1, tile1))):
        up0 = bdot(l0, top[:NB])
        low = (top[NB:].astype(jnp.float32) - dot(corner, up0)).astype(jnp.bfloat16)
        up1 = bdot(l1, low)
        new = (tile.astype(jnp.float32) - dot(factor0, up0)).astype(jnp.bfloat16)
        new = (new.astype(jnp.float32) - dot(factor1, up1)).astype(jnp.bfloat16)
        row0, row1 = up0, up1
        if d == 0:
            new = jnp.where(pcol == 0, factor0, jnp.where(pcol == 1, factor1, new))
            row0 = jnp.where(pcol == 0, top[:NB], up0)
            row1 = jnp.where(pcol == 0, corner, jnp.where(pcol == 1, low, up1))
        head = jnp.where(prow == 0, row0, jnp.where(prow == 1, row1, new[:NB]))
        out.append(jnp.concatenate([head, new[NB:]], axis=0).reshape(2, NB, NB))
    return jnp.stack(out, axis=2).reshape(matrix.shape)


def solution(mesh):
    return jax.shard_map(
        per_device,
        mesh=mesh,
        in_specs=(P(None, "prow", None, None, "pcol", None), P(), P(), P()),
        out_specs=P(None, "prow", None, None, "pcol", None),
        check_vma=False,
    )
```

```python
import jax
import jax.numpy as jnp
from jax import lax
from jax.experimental import pallas as pl
from jax.experimental.pallas import tpu as pltpu
from jax.sharding import PartitionSpec as P

NB = 512
CORES = 2
NX = 4
CAP = 96
DCAP = 56
MOVED = CORES * DCAP
HALF = NB // CORES
PA = 32
PB = 16
MESH = pl.DeviceIdType.MESH
ANY = pl.BlockSpec(memory_space=pl.ANY)


class Ring:
    def __init__(self, n, pos, goto, item, send, recv, fresh=None, arrived=None):
        self.n, self.pos, self.goto, self.item = n, pos, goto, item
        self.send, self.recv = send, recv
        self.fresh, self.arrived = fresh, arrived
        self.got = [0, 0]

    def carries(self, way, hop, half):
        return hop < self.n // 2 or (hop == self.n // 2 and half == way)

    def copy(self, way, hop, half):
        step = 1 if way == 0 else -1
        index = lax.rem(self.pos + self.n - step * (hop - 1), self.n)
        target = lax.rem(self.pos + self.n + step, self.n)
        src = self.item(index, half)
        if hop == 1 and self.fresh is not None:
            src = self.fresh(half)
        return pltpu.make_async_remote_copy(
            src_ref=src,
            dst_ref=self.item(index, half),
            send_sem=self.send.at[way, hop - 1, half],
            recv_sem=self.recv.at[way, hop - 1, half],
            device_id=self.goto(target),
            device_id_type=MESH,
        )

    def landed(self, way, hop, half):
        step = 1 if way == 0 else -1
        index = lax.rem(self.pos + self.n - step * hop, self.n)
        ref = self.item(index, half)
        return index, ref, pltpu.make_async_remote_copy(
            src_ref=ref,
            dst_ref=ref,
            send_sem=self.send.at[way, hop - 1, half],
            recv_sem=self.recv.at[way, hop - 1, half],
            device_id=self.goto(lax.rem(self.pos + 1, self.n)),
            device_id_type=MESH,
        )

    def start(self, half):
        for way in (0, 1):
            self.copy(way, 1, half).start()

    def step(self, way, hop, half):
        index, ref, arrival = self.landed(way, hop, half)
        arrival.wait_recv()
        if self.carries(way, hop + 1, half):
            self.copy(way, hop + 1, half).start()
        self.got[half] += 1
        if self.arrived is not None:
            self.arrived(index, ref, way, hop, half)

    def events(self, t0, dt):
        out = []
        for half in (0, 1):
            for hop in range(1, self.n // 2 + 1):
                for way in (0, 1):
                    if self.carries(way, hop, half):
                        when = t0[half] + dt * hop
                        out.append((when, lambda w=way, h=hop, f=half: self.step(w, h, f)))
        return out

    def complete(self, half):
        assert self.got[half] == self.n - 1

    def drain(self):
        for half in (0, 1):
            for hop in range(1, self.n // 2 + 1):
                for way in (0, 1):
                    if self.carries(way, hop, half):
                        self.copy(way, hop, half).wait_send()


def run_events(events):
    for _, act in sorted(events, key=lambda e: e[0]):
        act()


class RowExchange:
    def __init__(self, ny, sent, spread, rows, moved, sems):
        self.ny, self.sent, self.spread, self.rows, self.moved = ny, sent, spread, rows, moved
        (self.rs, self.rr, self.fs, self.fr, self.os, self.orr, self.ls, self.es, self.er) = sems
        prow = lax.axis_index("prow")
        self.y, self.c = lax.div(prow, CORES), lax.rem(prow, CORES)
        self.partner = {"prow": self.y * CORES + 1 - self.c}
        self.ring = Ring(
            ny, self.y,
            lambda i: {"prow": i * CORES + self.c},
            lambda i, half: rows.at[i * CORES + self.c, half],
            self.rs, self.rr,
            fresh=lambda half: sent.at[half],
            arrived=self.forward,
        )
        self.forwards = []

    def barrier_peers(self):
        ids = [{"prow": lax.rem(self.y + k, self.ny) * CORES + c} for k in range(1, self.ny) for c in (0, 1)]
        return ids + [self.partner]

    def forward_copy(self, index, way, hop, half):
        return pltpu.make_async_remote_copy(
            src_ref=self.rows.at[index * CORES + self.c, half],
            dst_ref=self.rows.at[index * CORES + self.c, half],
            send_sem=self.fs.at[way, hop - 1, half],
            recv_sem=self.fr.at[way, hop - 1, half],
            device_id=self.partner,
            device_id_type=MESH,
        )

    def forward(self, index, ref, way, hop, half):
        copy = self.forward_copy(index, way, hop, half)
        copy.start()
        self.forwards.append((copy, index, way, hop, half))

    def own_copies(self):
        mine = self.rows.at[self.y * CORES + self.c]
        local = pltpu.make_async_copy(self.sent, mine, self.ls.at[0])
        across = pltpu.make_async_remote_copy(
            src_ref=self.sent, dst_ref=mine, send_sem=self.os, recv_sem=self.orr,
            device_id=self.partner, device_id_type=MESH,
        )
        return local, across

    def spread_copy(self, k, core):
        to = lax.rem(self.y + k, self.ny) * CORES + core
        return pltpu.make_async_remote_copy(
            src_ref=self.spread.at[to], dst_ref=self.moved.at[self.c],
            send_sem=self.es.at[k, core], recv_sem=self.er.at[self.c],
            device_id={"prow": to}, device_id_type=MESH,
        )

    def spread_partner(self):
        to = 1 - self.c
        return pltpu.make_async_remote_copy(
            src_ref=self.spread.at[to], dst_ref=self.moved.at[self.c],
            send_sem=self.es.at[0, 0], recv_sem=self.er.at[self.c],
            device_id=self.partner, device_id_type=MESH,
        )

    def spread_own(self):
        return pltpu.make_async_copy(self.spread.at[self.c], self.moved.at[self.c], self.er.at[self.c])

    def begin(self):
        for half in (0, 1):
            self.ring.start(half)
        for copy in self.own_copies():
            copy.start()

    def spread_some(self, ks):
        @pl.when(self.y == 0)
        def _():
            for k in ks:
                for core in (0, 1):
                    self.spread_copy(k, core).start()

    def spread_near(self):
        @pl.when(self.y == 0)
        def _():
            self.spread_partner().start()
            self.spread_own().start()

    def events(self, dt):
        half_n = self.ny // 2
        out = [(-1.0, self.begin), (3.9 * dt, self.spread_near)]
        order = [half_n] + [k for d in range(half_n - 1, 0, -1) for k in (d, self.ny - d)]
        for i, k in enumerate(order):
            out.append((0.1 + i * 0.5 * dt, lambda k=k: self.spread_some([k])))
        return out + self.ring.events([0.0, 0.3 * dt], dt)

    def finish(self):
        local, across = self.own_copies()
        local.wait()
        across.wait()
        self.ring.drain()
        for copy, index, way, hop, half in self.forwards:
            copy.wait_send()
        for copy, index, way, hop, half in self.forwards:
            ref = self.rows.at[index * CORES + 1 - self.c, half]
            pltpu.make_async_remote_copy(
                src_ref=ref, dst_ref=ref,
                send_sem=self.fs.at[way, hop - 1, half], recv_sem=self.fr.at[way, hop - 1, half],
                device_id=self.partner, device_id_type=MESH,
            ).wait_recv()
        for core in (0, 1):
            ref = self.moved.at[core]
            pltpu.make_async_copy(ref, ref, self.er.at[core]).wait()

        @pl.when(self.y == 0)
        def _():
            for k in range(1, self.ny):
                for core in (0, 1):
                    self.spread_copy(k, core).wait_send()
            self.spread_partner().wait_send()


def exchange_sems(ny):
    dma = pltpu.SemaphoreType.DMA
    return [
        dma((2, ny // 2, 2)), dma((2, ny // 2, 2)),
        dma((2, ny // 2, 2)), dma((2, ny // 2, 2)),
        dma, dma, dma((1,)), dma((ny, CORES)), dma((CORES,)),
    ]


def meet(peers):
    barrier = pltpu.get_barrier_semaphore()
    for peer in peers:
        pl.semaphore_signal(barrier, inc=1, device_id=peer, device_id_type=MESH)
    pl.semaphore_wait(barrier, len(peers))


def exchange_kernel(ny, sent, spread, rows, moved, *sems):
    ex = RowExchange(ny, sent, spread, rows, moved, sems)
    meet(ex.barrier_peers())
    run_events(ex.events(3.8))
    ex.finish()


def row_exchange(sent, spread, ny, cid):
    width = sent.shape[-1]
    return pl.pallas_call(
        lambda *refs: exchange_kernel(ny, *refs),
        out_shape=(
            jax.ShapeDtypeStruct((ny * CORES, 2, CAP // 2, width), jnp.bfloat16),
            jax.ShapeDtypeStruct((CORES, DCAP, width), jnp.bfloat16),
        ),
        in_specs=[ANY, ANY],
        out_specs=(ANY, ANY),
        scratch_shapes=exchange_sems(ny),
        compiler_params=pltpu.CompilerParams(collective_id=cid, has_side_effects=True),
        name="row_exchange",
    )(sent, spread)


def meet_with_roots(near, pcol, n):
    barrier = pltpu.get_barrier_semaphore()

    def signal(peer):
        pl.semaphore_signal(barrier, inc=1, device_id=peer, device_id_type=MESH)

    for root in (0, 1):
        @pl.when(pcol == root)
        def _():
            for k in range(1, n):
                signal({"pcol": lax.rem(pcol + k, n)})

        @pl.when(pcol != root)
        def _():
            signal({"pcol": root})

    for peer in near:
        signal(peer)

    @pl.when(pcol < 2)
    def _():
        pl.semaphore_wait(barrier, len(near) + n)

    @pl.when(pcol >= 2)
    def _():
        pl.semaphore_wait(barrier, len(near) + 2)


class Scatter:
    def __init__(self, pcol, n, piece, slot, send, recv):
        self.pcol, self.n, self.piece, self.slot, self.send, self.recv = pcol, n, piece, slot, send, recv

    def copy(self, k):
        to = lax.rem(self.pcol + k, self.n)
        return pltpu.make_async_remote_copy(
            src_ref=self.piece(to), dst_ref=self.slot(self.pcol, to),
            send_sem=self.send.at[k], recv_sem=self.recv.at[self.pcol],
            device_id={"pcol": to}, device_id_type=MESH)

    def start(self):
        @pl.when(self.pcol < 2)
        def _():
            for k in range(1, self.n):
                self.copy(k).start()
            pltpu.make_async_copy(
                self.piece(self.pcol), self.slot(self.pcol, self.pcol), self.recv.at[self.pcol]
            ).start()

    def landed(self, panel):
        ref = self.slot(panel, self.pcol)
        pltpu.make_async_copy(ref, ref, self.recv.at[panel]).wait()

    def drain(self):
        @pl.when(self.pcol < 2)
        def _():
            for k in range(1, self.n):
                self.copy(k).wait_send()


def first_kernel(ny, nz, nexch, *refs):
    tile, sent, spread, piece, rows, moved = refs[:6]
    ex = RowExchange(ny, sent, spread, rows, moved, refs[6 : 6 + nexch])
    ss, sr = refs[6 + nexch :]
    pcol = lax.axis_index("pcol")
    n = nz * NX
    scatter = Scatter(
        pcol, n,
        lambda to: tile.at[pl.ds(pl.multiple_of(to * PA, PA), PA), pl.ds(0, NB)],
        lambda panel, to: piece.at[panel], ss, sr)
    meet_with_roots(ex.barrier_peers(), pcol, n)
    run_events(ex.events(3.8) + [(0.0, scatter.start)])
    ex.finish()
    for panel in (0, 1):
        scatter.landed(panel)
    scatter.drain()


def first_exchange(tile, sent, spread, ny, nz, cid):
    width = sent.shape[-1]
    sems = exchange_sems(ny)
    dma = pltpu.SemaphoreType.DMA
    return pl.pallas_call(
        lambda *refs: first_kernel(ny, nz, len(sems), *refs),
        out_shape=(
            jax.ShapeDtypeStruct((2, PA, NB), jnp.bfloat16),
            jax.ShapeDtypeStruct((ny * CORES, 2, CAP // 2, width), jnp.bfloat16),
            jax.ShapeDtypeStruct((CORES, DCAP, width), jnp.bfloat16),
        ),
        in_specs=[ANY] * 3,
        out_specs=(ANY,) * 3,
        scratch_shapes=sems + [dma((nz * NX,)), dma((2,))],
        compiler_params=pltpu.CompilerParams(collective_id=cid, has_side_effects=True),
        name="first_exchange",
    )(tile, sent, spread)


class Direct:
    def __init__(self, n, pos, goto, item, fresh, send, recv):
        self.n, self.pos, self.goto, self.item, self.fresh, self.send, self.recv = n, pos, goto, item, fresh, send, recv

    def copy(self, k, half):
        to = lax.rem(self.pos + k, self.n)
        return pltpu.make_async_remote_copy(
            src_ref=self.fresh(half), dst_ref=self.item(self.pos, half),
            send_sem=self.send.at[k, half], recv_sem=self.recv.at[k, half],
            device_id=self.goto(to), device_id_type=MESH)

    def start(self):
        for half in (0, 1):
            for k in range(1, self.n):
                self.copy(k, half).start()
            pltpu.make_async_copy(
                self.fresh(half), self.item(self.pos, half), self.recv.at[0, half]).start()

    def wait(self, half):
        for k in range(self.n):
            ref = self.item(lax.rem(self.pos + self.n - k, self.n), half)
            pltpu.make_async_copy(ref, ref, self.recv.at[k, half]).wait()

    def drain(self):
        for half in (0, 1):
            for k in range(1, self.n):
                self.copy(k, half).wait_send()


def second_kernel(ny, nz, nexch, *refs):
    piece, small, sent, spread, raw, extra, other, rows, moved = refs[:9]
    ex = RowExchange(ny, sent, spread, rows, moved, refs[9 : 9 + nexch])
    (axs, axr, azs, azr, bzs, bzr, bxs, bxr, ss, sr, ts, tr, to_s, to_r) = refs[9 + nexch :]
    pcol = lax.axis_index("pcol")
    n = nz * NX
    z, x = lax.div(pcol, NX), lax.rem(pcol, NX)

    def to_x(i):
        return {"pcol": z * NX + i}

    def to_z(i):
        return {"pcol": i * NX + x}

    near = ex.barrier_peers()
    near += [to_x(lax.rem(x + d, NX)) for d in range(1, NX)]
    near += [to_z(lax.rem(z + d, nz)) for d in (1, nz - 1)]
    meet_with_roots(near, pcol, n)

    tops = nz // 2

    def across(index, way, hop, half, sems=None):
        s, r = (ts.at[way, hop - 1, half], tr.at[way, hop - 1, half]) if hop else (to_s.at[half], to_r.at[half])
        return pltpu.make_async_remote_copy(
            src_ref=extra.at[half, index, pl.ds(0, tops)], dst_ref=other.at[half, index],
            send_sem=s, recv_sem=r, device_id=ex.partner, device_id_type=MESH)

    crossing = []

    def cross(index, ref, way, hop, half):
        copy = across(index, way, hop, half)
        copy.start()
        crossing.append(copy)

    scatter = Scatter(
        pcol, n,
        lambda to: small.at[lax.rem(to, NX), lax.div(to, NX)],
        lambda panel, to: extra.at[panel, lax.rem(to, NX), lax.div(to, NX)], ss, sr)
    ax = Direct(NX, x, to_x, lambda i, h: raw.at[h, z, i], lambda h: piece.at[h], axs, axr)
    az = Ring(nz, z, to_z, lambda i, h: raw.at[h, i], azs, azr)
    bz = Ring(nz, z, to_z, lambda i, h: extra.at[h, x, i], bzs, bzr)
    bx = Ring(NX, x, to_x, lambda i, h: extra.at[h, i], bxs, bxr, arrived=cross)

    def begin_az(half):
        ax.wait(half)
        az.start(half)

    def begin_bz(half):
        scatter.landed(half)
        bz.start(half)

    def begin_bx(half):
        bz.complete(half)
        bx.start(half)
        cross(x, None, 0, 0, half)

    events = [(-0.6, scatter.start), (-0.5, ax.start)]
    events += ex.events(4.5)
    events += [(3.5 + h * 0.3, lambda h=h: begin_az(h)) for h in (0, 1)]
    events += az.events([3.5, 5.5], 5.0)
    events += [(5.0 + h * 0.1, lambda h=h: begin_bz(h)) for h in (0, 1)]
    events += bz.events([5.2, 5.4], 3.0)
    events += [(17.6 + h * 0.1, lambda h=h: begin_bx(h)) for h in (0, 1)]
    events += bx.events([18.0, 19.5], 3.5)
    run_events(events)
    ex.finish()
    for ring in (az, bz, bx):
        for half in (0, 1):
            ring.complete(half)
        ring.drain()
    ax.drain()
    scatter.drain()
    for copy in crossing:
        copy.wait()


def second_exchange(piece, small, sent, spread, ny, nz, cid):
    width = sent.shape[-1]
    dma = pltpu.SemaphoreType.DMA
    sems = exchange_sems(ny)
    zring, xring = dma((2, nz // 2, 2)), dma((2, NX // 2, 2))
    direct = dma((NX, 2))
    return pl.pallas_call(
        lambda *refs: second_kernel(ny, nz, len(sems), *refs),
        out_shape=(
            jax.ShapeDtypeStruct((2, nz, NX, PA, NB), jnp.bfloat16),
            jax.ShapeDtypeStruct((2, NX, nz, PB, NB), jnp.bfloat16),
            jax.ShapeDtypeStruct((2, NX, nz // 2, PB, NB), jnp.bfloat16),
            jax.ShapeDtypeStruct((ny * CORES, 2, CAP // 2, width), jnp.bfloat16),
            jax.ShapeDtypeStruct((CORES, DCAP, width), jnp.bfloat16),
        ),
        in_specs=[ANY] * 4,
        out_specs=(ANY,) * 5,
        scratch_shapes=sems
        + [direct, direct, zring, zring, zring, zring, xring, xring]
        + [dma((nz * NX,)), dma((2,)), xring, xring, dma((2,)), dma((2,))],
        compiler_params=pltpu.CompilerParams(collective_id=cid, has_side_effects=True),
        name="second_exchange",
    )(piece, small, sent, spread)


def dot(a, b):
    return jnp.dot(a, b, preferred_element_type=jnp.float32)


def bdot(a, b):
    return dot(a, b).astype(jnp.bfloat16)


def ids(shape, axis):
    return lax.broadcasted_iota(jnp.int32, shape, axis).astype(jnp.float32)


def to_row(col):
    n = col.shape[0]
    return jnp.sum(jnp.where(ids((n, n), 0) == ids((n, n), 1), col, 0.0), axis=0, keepdims=True)


def to_col(row):
    n = row.shape[1]
    return jnp.sum(jnp.where(ids((n, n), 0) == ids((n, n), 1), row, 0.0), axis=1, keepdims=True)


def along(table):
    return jnp.sum(table, axis=1, keepdims=True)


def down(table):
    return jnp.sum(table, axis=0, keepdims=True)


def hot(mask):
    return jnp.where(mask, 1.0, 0.0).astype(jnp.bfloat16)


def index_kernel(nprow, piv, tile, sent0, sent1, spread0, spread1, slot_out, into_out, rounds_out):
    prow = lax.axis_index("prow")
    core = lax.rem(prow, CORES).astype(jnp.float32)
    prow_f = prow.astype(jnp.float32)
    rows = [piv[k : k + 1, :].astype(jnp.float32) for k in (0, 1)]
    cols = [to_col(r) for r in rows]
    i0, i1 = ids((NB, NB), 0), ids((NB, NB), 1)
    receive = []
    for k in (0, 1):
        first = float(k * NB)
        top_c, top_r = ids((NB, 1), 0) + first, ids((1, NB), 1) + first
        left_c = 1.0 - along(jnp.where(rows[k] == top_c, 1.0, 0.0))
        left_r = 1.0 - down(jnp.where(cols[k] == top_r, 1.0, 0.0))
        rank_r = down(jnp.where(i0 < i1, left_c, 0.0))
        vac_r = jnp.where(rows[k] >= first + NB, 1.0, 0.0)
        vac_c = along(jnp.where(i1 < i0, vac_r, 0.0))
        receive.append(along(jnp.where((rank_r == vac_c) & (left_r > 0.5), top_r, 0.0)))
    receive0_r = to_row(receive[0])

    def lookup(keys):
        hit = keys == rows[0]
        found = along(jnp.where(hit, 1.0, 0.0))
        return jnp.where(found > 0.5, along(jnp.where(hit, receive0_r, 0.0)), keys)

    src1, from1 = lookup(cols[1]), lookup(receive[1])
    again = along(jnp.where(cols[0] == rows[1], 1.0, 0.0))

    def owner(v):
        return (lax.shift_right_logical(v.astype(jnp.int32), 9) & (nprow - 1)).astype(jnp.float32)

    def local(v):
        v = v.astype(jnp.int32)
        return (lax.shift_right_logical(v, 13) * NB + (v & (NB - 1))).astype(jnp.float32)

    n = 2 * NB
    e0, e1 = ids((n, n), 0), ids((n, n), 1)

    def rank(group_c):
        group_r = to_row(group_c)
        same = group_c == group_r
        rank_c = along(jnp.where(same & (e1 < e0), 1.0, 0.0))
        rank_r = down(jnp.where(same & (e0 < e1), 1.0, 0.0))
        return group_r, rank_c, rank_r

    t_c = jnp.concatenate([cols[0], src1], axis=0)
    t_group = owner(t_c)
    t_group_r, t_rank_c, t_rank_r = rank(t_group)
    slot_c = jnp.where(t_rank_c < CAP, t_group * CAP + t_rank_c, -1.0)
    slot_r = jnp.where(t_rank_r < CAP, t_group_r * CAP + t_rank_r, -1.0)
    slot_out[...] = slot_c.astype(jnp.int32)
    mine = ids((CAP, 1), 0) + prow_f * CAP
    pick = along(jnp.where(slot_r == mine, local(to_row(t_c)) + 1.0, 0.0)) - 1.0
    sent = bdot(hot(pick == ids((CAP, n), 1)), tile[...])
    sent0[...] = sent[:, :NB]
    sent1[...] = sent[:, NB:]

    d_dst = jnp.concatenate([cols[0], cols[1]], axis=0)
    d_src = jnp.concatenate([receive[0], from1], axis=0)
    fresh = jnp.concatenate([again, jnp.zeros_like(again)], axis=0)
    valid = (d_dst >= 2.0 * NB) & (fresh < 0.5)
    group = jnp.where(valid, owner(d_dst) * CORES + jnp.where(d_src >= NB, 1.0, 0.0), -1.0)
    group_r, rank_c, rank_r = rank(group)
    key_c = jnp.where(valid & (rank_c < DCAP), group * DCAP + rank_c, -1.0)
    lane = ids((1, 128), 1)
    wanted = jnp.where(lane < MOVED, lane + prow_f * MOVED, -2.0)
    into = down(jnp.where(key_c == wanted, local(d_dst) + 1.0, 0.0)) - 1.0
    into_out[...] = into.astype(jnp.int32)
    most_t = jnp.max(t_rank_c) * (1.0 / CAP)
    most_d = jnp.max(jnp.where(valid, rank_c, 0.0)) * (1.0 / DCAP)
    rounds_out[0, 0] = jnp.where(jnp.maximum(most_t, most_d) > 1.0 - 0.25 / CAP, 2, 1).astype(jnp.int32)

    @pl.when(prow < CORES)
    def _():
        key_r = jnp.where((group_r > -0.5) & (rank_r < DCAP), group_r * DCAP + rank_r, -1.0)
        src_r = to_row(d_src)
        s = ids((MOVED, 1), 0)

        def one_chip(q, _):
            second = jnp.where(s >= DCAP, 1.0, 0.0)
            want = (2.0 * q.astype(jnp.float32) + second) * MOVED + core * DCAP + s - second * DCAP
            src = along(jnp.where(key_r == want, src_r + 1.0, 0.0)) - 1.0 - core * NB
            out = bdot(hot(src == ids((MOVED, NB), 1)), tile[:NB, :])
            here = pl.ds(pl.multiple_of(q * MOVED, MOVED), MOVED)
            spread0[here, :] = out[:, :NB]
            spread1[here, :] = out[:, NB:]
            return 0

        lax.fori_loop(0, nprow // 2, one_chip, 0)


def index_and_pack(pivots, tile, nprow):
    n = 2 * NB
    bf16 = jnp.bfloat16
    vmem = pl.BlockSpec(memory_space=pltpu.VMEM)
    return pl.pallas_call(
        lambda *refs: index_kernel(nprow, *refs),
        out_shape=(
            jax.ShapeDtypeStruct((CAP, NB), bf16), jax.ShapeDtypeStruct((CAP, NB), bf16),
            jax.ShapeDtypeStruct((nprow * DCAP, NB), bf16), jax.ShapeDtypeStruct((nprow * DCAP, NB), bf16),
            jax.ShapeDtypeStruct((n, 1), jnp.int32), jax.ShapeDtypeStruct((1, 128), jnp.int32),
            jax.ShapeDtypeStruct((1, 1), jnp.int32),
        ),
        in_specs=[vmem, vmem],
        out_specs=(vmem,) * 6 + (pl.BlockSpec(memory_space=pltpu.SMEM),),
        name="index_and_pack",
    )(pivots, tile)


def panel_tops_kernel(rows, moved, slot, small):
    pcol, prow = lax.axis_index("pcol"), lax.axis_index("prow")
    first = jnp.where(pcol == 0, NB, 0) + lax.rem(prow, CORES) * HALF
    first = pl.multiple_of(first, HALF)
    keys = slot[pl.ds(first, HALF), :]
    total = rows.shape[0]
    place = jnp.where(keys == lax.broadcasted_iota(jnp.int32, (HALF, total), 1), 1.0, 0.0).astype(jnp.bfloat16)
    part = bdot(place, rows[...])
    step = HALF // NX
    for x in range(NX):
        small[x, pl.ds(0, step), :] = part[x * step : (x + 1) * step]
    small[0, pl.ds(step, step), :] = moved[pl.ds(0, step), :]
    small[1, pl.ds(step, MOVED - step), :] = moved[pl.ds(step, MOVED - step), :]
    for x, start in ((1, MOVED), (2, step), (3, step)):
        size = 2 * step - start if x > 1 else 2 * step - MOVED
        small[x, pl.ds(2 * step - size, size), :] = jnp.zeros((size, NB), jnp.bfloat16)


def panel_tops(rows, moved, slot, nz):
    vmem = pl.BlockSpec(memory_space=pltpu.VMEM)
    return pl.pallas_call(
        panel_tops_kernel,
        out_shape=jax.ShapeDtypeStruct((NX, nz * PB, NB), jnp.bfloat16),
        in_specs=[vmem] * 3,
        out_specs=vmem,
        name="panel_tops",
    )(rows, moved, slot)


def update_kernel(raw, extra, other, rows0, rows1, moved0, moved1, slot, into, tile, low_inv, up_inv,
                  out, top, low, up0, up1):
    pcol, prow = lax.axis_index("pcol"), lax.axis_index("prow")
    core = lax.rem(prow, CORES)
    f32 = jnp.float32
    step = NB // 2
    halves = (pl.ds(0, NB), pl.ds(NB, NB))
    total = rows0.shape[0]

    def spot(i):
        return pl.ds(pl.multiple_of(i * step, step), step)

    def place_rows(i, _):
        keys = slot[spot(i), :]
        place = jnp.where(keys == lax.broadcasted_iota(jnp.int32, (step, total), 1), 1.0, 0.0).astype(jnp.bfloat16)
        top[spot(i), halves[0]] = bdot(place, rows0[...])
        top[spot(i), halves[1]] = bdot(place, rows1[...])
        return 0

    lax.fori_loop(0, 4, place_rows, 0)
    l0, l1, u0, u1 = low_inv[0], low_inv[1], up_inv[0], up_inv[1]
    panel_tops = []
    half = HALF // NX
    for k in (0, 1):
        own = jnp.concatenate([extra[k, x, :half, :] for x in range(NX)], axis=0)
        far = jnp.concatenate([other[k, x] for x in range(NX)], axis=0)
        panel_tops.append(jnp.concatenate(
            [jnp.where(core == 0, own, far), jnp.where(core == 0, far, own)], axis=0))
    corner = bdot(panel_tops[0], u0)
    upper = bdot(l0, panel_tops[1])
    moved_panel = [
        jnp.concatenate([extra[k, 0, half:, :], extra[k, 1, half : half + MOVED - half, :]], axis=0) for k in (0, 1)
    ]
    for cols in halves:
        up0[:, cols] = bdot(l0, top[pl.ds(0, NB), cols])
        low[:, cols] = (top[pl.ds(NB, NB), cols].astype(f32) - dot(corner, up0[:, cols])).astype(jnp.bfloat16)
        up1[:, cols] = bdot(l1, low[:, cols])

    def update(i, _):
        here = spot(i)
        ids_c = lax.broadcasted_iota(jnp.int32, (step, MOVED), 0) + i * step
        match = jnp.where(ids_c == into[:, :MOVED], 1.0, 0.0)
        hit = jnp.max(match, axis=1, keepdims=True) > 0.5
        insert = match.astype(jnp.bfloat16)

        def with_moved(new, old):
            return jnp.where(hit, dot(insert, new), old.astype(f32)).astype(jnp.bfloat16)

        factor0 = bdot(with_moved(moved_panel[0], raw[0, here, :]), u0)
        panel1 = (with_moved(moved_panel[1], raw[1, here, :]).astype(f32) - dot(factor0, upper)).astype(jnp.bfloat16)
        factor1 = bdot(panel1, u1)
        for d, (cols, moved) in enumerate(zip(halves, (moved0, moved1))):
            new = with_moved(moved[...], tile[here, cols]).astype(f32)
            new = (new - dot(factor0, up0[:, cols])).astype(jnp.bfloat16).astype(f32)
            new = (new - dot(factor1, up1[:, cols])).astype(jnp.bfloat16)
            if d == 0:
                new = jnp.where(pcol == 0, factor0, jnp.where(pcol == 1, factor1, new))
            out[here, cols] = new
        return 0

    lax.fori_loop(0, 4, update, 0)
    heads = pl.ds(0, NB)

    @pl.when(prow == 0)
    def _():
        out[heads, halves[0]] = jnp.where(pcol == 0, top[heads, halves[0]], up0[:, halves[0]])
        out[heads, halves[1]] = up0[:, halves[1]]

    @pl.when(prow == 1)
    def _():
        out[heads, halves[0]] = jnp.where(
            pcol == 0, corner, jnp.where(pcol == 1, low[:, halves[0]], up1[:, halves[0]]))
        out[heads, halves[1]] = up1[:, halves[1]]


def update(*args):
    n = 2 * NB
    vmem = pl.BlockSpec(memory_space=pltpu.VMEM)
    bf16 = jnp.bfloat16
    return pl.pallas_call(
        update_kernel,
        out_shape=jax.ShapeDtypeStruct((n, n), bf16),
        in_specs=[vmem] * len(args),
        out_specs=vmem,
        scratch_shapes=[pltpu.VMEM((n, n), bf16)] + [pltpu.VMEM((NB, n), bf16)] * 3,
        name="update",
    )(*args)


def count_before(flags):
    n = flags.shape[0]
    ahead = jnp.arange(n)[None, :] < jnp.arange(n)[:, None]
    return jnp.sum((ahead & flags[None, :]).astype(jnp.int32), axis=1)


def pairing(sources, first_row):
    top_ids = first_row + jnp.arange(NB, dtype=jnp.int32)
    leftover = jnp.logical_not(jnp.any(sources[None, :] == top_ids[:, None], axis=1))
    left_rank = count_before(leftover)
    vacated = sources >= first_row + NB
    vac_rank = count_before(vacated)
    table = leftover[None, :] & (left_rank[None, :] == vac_rank[:, None])
    return jnp.sum(jnp.where(table, top_ids[None, :], 0), axis=1)


def lookup(keys, names, values):
    hit = keys[:, None] == names[None, :]
    found = jnp.sum(jnp.where(hit, values[None, :], 0), axis=1)
    return jnp.where(jnp.any(hit, axis=1), found, keys)


def rank_in(group):
    n = group.shape[0]
    ahead = jnp.arange(n)[None, :] < jnp.arange(n)[:, None]
    same = group[None, :] == group[:, None]
    return jnp.sum((same & ahead).astype(jnp.int32), axis=1)


def slot_values(keys, values, wanted):
    hit = wanted[:, None] == keys[None, :]
    return jnp.sum(jnp.where(hit, values[None, :] + 1, 0), axis=1) - 1


def one_hot(index, n):
    return (index[:, None] == jnp.arange(n, dtype=jnp.int32)[None, :]).astype(jnp.bfloat16)


def collect_rounds(tile, pivots, nprow, ny):
    prow = lax.axis_index("prow")
    core = lax.rem(prow, CORES)
    s0, s1 = pivots[0], pivots[1]
    receive0, receive1 = pairing(s0, 0), pairing(s1, NB)
    src1 = lookup(s1, s0, receive0)
    from1 = lookup(receive1, s0, receive0)
    again = jnp.any(s0[:, None] == s1[None, :], axis=1)
    big = jnp.int32(1 << 20)

    def owner(rows):
        return lax.rem(rows // NB, nprow)

    def local(rows):
        return rows // (NB * nprow) * NB + lax.rem(rows, NB)

    t_src = jnp.concatenate([s0, src1])
    t_owner = owner(t_src)
    t_rank = rank_in(t_owner)
    t_local = local(t_src)
    d_dst = jnp.concatenate([s0, s1])
    d_src = jnp.concatenate([receive0, from1])
    d_valid = (d_dst >= 2 * NB) & jnp.concatenate([jnp.logical_not(again), jnp.ones((NB,), jnp.bool_)])
    d_core = d_src // NB
    d_owner = owner(d_dst)
    d_rank = rank_in(jnp.where(d_valid, d_owner * CORES + d_core, -1))
    d_local = local(d_dst)
    rounds = jnp.maximum(jnp.max(t_rank) // CAP, jnp.max(jnp.where(d_valid, d_rank, 0)) // DCAP) + 1

    def body(state):
        r, top, now = state
        t_in = (t_rank // CAP) == r
        t_slot = t_owner * CAP + lax.rem(t_rank, CAP)
        t_key = jnp.where(t_in, t_slot, big)
        d_in = d_valid & ((d_rank // DCAP) == r)
        d_key = jnp.where(d_in, (d_owner * CORES + d_core) * DCAP + lax.rem(d_rank, DCAP), big)
        pick = one_hot(slot_values(t_key, t_local, prow * CAP + jnp.arange(CAP, dtype=jnp.int32)), 2 * NB)
        every = jnp.arange(nprow * DCAP, dtype=jnp.int32)
        wanted = (every // DCAP * CORES + core) * DCAP + lax.rem(every, DCAP)
        spread_sel = one_hot(slot_values(d_key, d_src - core * NB, wanted), NB)
        mine = prow * MOVED + jnp.arange(MOVED, dtype=jnp.int32)
        into = slot_values(d_key, d_local, mine)
        insert = (jnp.arange(2 * NB, dtype=jnp.int32)[:, None] == into[None, :]).astype(jnp.bfloat16)
        rows, moved = row_exchange(
            bdot(pick, tile).reshape(2, CAP // 2, 2 * NB),
            bdot(spread_sel, tile[:NB]).reshape(nprow, DCAP, 2 * NB), ny, 1)
        place = one_hot(jnp.where(t_in, t_slot, -1), nprow * CAP)
        top = top + bdot(place, rows.reshape(nprow * CAP, 2 * NB))
        new = bdot(insert, moved.reshape(MOVED, 2 * NB))
        return r + 1, top, jnp.where(jnp.any(insert > 0, axis=1)[:, None], new, now)

    _, top, now = lax.while_loop(
        lambda s: s[0] < rounds, body, (jnp.int32(0), jnp.zeros_like(tile), tile))
    return top, now


def per_device(matrix, pivots, lower_inverse, upper_inverse):
    nprow, npcol = lax.axis_size("prow"), lax.axis_size("pcol")
    ny, nz = nprow // CORES, npcol // NX
    n = 2 * NB
    tile = matrix.reshape(n, n)
    *packed, slot, into, rounds = index_and_pack(pivots, tile, nprow)

    def finish(tile, packed, slot, into, known, cids):
        sents = [v.reshape(2, CAP // 2, NB) for v in packed[:2]]
        spreads = [v.reshape(nprow, DCAP, NB) for v in packed[2:]]
        piece, rows0, moved0 = first_exchange(tile, sents[0], spreads[0], ny, nz, cids[0])
        rows0, moved0 = rows0.reshape(nprow * CAP, NB), moved0.reshape(MOVED, NB)
        if known is not None:
            rows0, moved0 = known[0], jnp.zeros_like(moved0)
        small = panel_tops(rows0, moved0, slot, nz).reshape(NX, nz, PB, NB)
        raw, extra, other, rows1, moved1 = second_exchange(piece, small, sents[1], spreads[1], ny, nz, cids[1])
        rows1, moved1 = rows1.reshape(nprow * CAP, NB), moved1.reshape(MOVED, NB)
        if known is not None:
            rows1, moved1 = known[1], jnp.zeros_like(moved1)
        return update(
            raw.reshape(2, n, NB), extra.reshape(2, NX, nz * PB, NB), other.reshape(2, NX, nz * PB // 2, NB),
            rows0, rows1, moved0, moved1, slot, into, tile, lower_inverse, upper_inverse)

    def one_round(tile):
        return finish(tile, packed, slot, into, None, (0, 2))

    def many_rounds(tile):
        top, now = collect_rounds(tile, pivots, nprow, ny)
        top = jnp.pad(top, ((0, nprow * CAP - n), (0, 0)))
        empty = [jnp.zeros_like(v) for v in packed]
        order = jnp.arange(n, dtype=jnp.int32)[:, None]
        return finish(now, empty, order, jnp.full_like(into, -1), (top[:, :NB], top[:, NB:]), (3, 4))

    out = lax.cond(rounds[0, 0] > 1, many_rounds, one_round, tile)
    return out.reshape(matrix.shape)


def solution(mesh):
    return jax.shard_map(
        per_device,
        mesh=mesh,
        in_specs=(P(None, "prow", None, None, "pcol", None), P(), P(), P()),
        out_specs=P(None, "prow", None, None, "pcol", None),
        check_vma=False,
    )
```

```python
import jax
import jax.numpy as jnp
from jax import lax
from jax.experimental import pallas as pl
from jax.experimental.pallas import tpu as pltpu
from jax.sharding import PartitionSpec as P

NB = 512
CORES = 2
NX = 4
CAP = 96
DCAP = 56
MOVED = CORES * DCAP
HALF = NB // CORES
LANES = NB // NX
PA = 32
PB = 48
MESH = pl.DeviceIdType.MESH
T_Y, T_A0, T_A1, T_AD, T_BZ, T_BX, T_BXD = 4.5, 0.0, 2.5, 5.8, 4.5, 13.0, 4.0
ANY = pl.BlockSpec(memory_space=pl.ANY)


class Ring:
    def __init__(self, n, pos, goto, item, send, recv, fresh=None, arrived=None):
        self.n, self.pos, self.goto, self.item = n, pos, goto, item
        self.send, self.recv = send, recv
        self.fresh, self.arrived = fresh, arrived
        self.got = [0, 0]

    def carries(self, way, hop, half):
        return hop < self.n // 2 or (hop == self.n // 2 and half == way)

    def copy(self, way, hop, half):
        step = 1 if way == 0 else -1
        index = lax.rem(self.pos + self.n - step * (hop - 1), self.n)
        target = lax.rem(self.pos + self.n + step, self.n)
        src = self.item(index, half)
        if hop == 1 and self.fresh is not None:
            src = self.fresh(half)
        return pltpu.make_async_remote_copy(
            src_ref=src,
            dst_ref=self.item(index, half),
            send_sem=self.send.at[way, hop - 1, half],
            recv_sem=self.recv.at[way, hop - 1, half],
            device_id=self.goto(target),
            device_id_type=MESH,
        )

    def landed(self, way, hop, half):
        step = 1 if way == 0 else -1
        index = lax.rem(self.pos + self.n - step * hop, self.n)
        ref = self.item(index, half)
        return index, ref, pltpu.make_async_remote_copy(
            src_ref=ref,
            dst_ref=ref,
            send_sem=self.send.at[way, hop - 1, half],
            recv_sem=self.recv.at[way, hop - 1, half],
            device_id=self.goto(lax.rem(self.pos + 1, self.n)),
            device_id_type=MESH,
        )

    def start(self, half):
        for way in (0, 1):
            self.copy(way, 1, half).start()

    def step(self, way, hop, half):
        index, ref, arrival = self.landed(way, hop, half)
        arrival.wait_recv()
        if self.carries(way, hop + 1, half):
            self.copy(way, hop + 1, half).start()
        self.got[half] += 1
        if self.arrived is not None:
            self.arrived(index, ref, way, hop, half)

    def events(self, t0, dt):
        out = []
        for half in (0, 1):
            for hop in range(1, self.n // 2 + 1):
                for way in (0, 1):
                    if self.carries(way, hop, half):
                        when = t0[half] + dt * hop
                        out.append((when, lambda w=way, h=hop, f=half: self.step(w, h, f)))
        return out

    def complete(self, half):
        assert self.got[half] == self.n - 1

    def drain(self):
        for half in (0, 1):
            for hop in range(1, self.n // 2 + 1):
                for way in (0, 1):
                    if self.carries(way, hop, half):
                        self.copy(way, hop, half).wait_send()


def run_events(events):
    for _, act in sorted(events, key=lambda e: e[0]):
        act()


class RowExchange:
    def __init__(self, ny, sent, spread, rows, moved, sems):
        self.ny, self.sent, self.spread, self.rows, self.moved = ny, sent, spread, rows, moved
        (self.rs, self.rr, self.fs, self.fr, self.os, self.orr, self.ls, self.es, self.er) = sems
        prow = lax.axis_index("prow")
        self.y, self.c = lax.div(prow, CORES), lax.rem(prow, CORES)
        self.partner = {"prow": self.y * CORES + 1 - self.c}
        self.ring = Ring(
            ny, self.y,
            lambda i: {"prow": i * CORES + self.c},
            lambda i, half: rows.at[i * CORES + self.c, half],
            self.rs, self.rr,
            fresh=lambda half: sent.at[half],
            arrived=self.forward,
        )
        self.forwards = []

    def barrier_peers(self):
        ids = [{"prow": lax.rem(self.y + k, self.ny) * CORES + c} for k in range(1, self.ny) for c in (0, 1)]
        return ids + [self.partner]

    def forward_copy(self, index, way, hop, half):
        return pltpu.make_async_remote_copy(
            src_ref=self.rows.at[index * CORES + self.c, half],
            dst_ref=self.rows.at[index * CORES + self.c, half],
            send_sem=self.fs.at[way, hop - 1, half],
            recv_sem=self.fr.at[way, hop - 1, half],
            device_id=self.partner,
            device_id_type=MESH,
        )

    def forward(self, index, ref, way, hop, half):
        copy = self.forward_copy(index, way, hop, half)
        copy.start()
        self.forwards.append((copy, index, way, hop, half))

    def own_copies(self):
        mine = self.rows.at[self.y * CORES + self.c]
        local = pltpu.make_async_copy(self.sent, mine, self.ls.at[0])
        across = pltpu.make_async_remote_copy(
            src_ref=self.sent, dst_ref=mine, send_sem=self.os, recv_sem=self.orr,
            device_id=self.partner, device_id_type=MESH,
        )
        return local, across

    def spread_copy(self, k, core):
        to = lax.rem(self.y + k, self.ny) * CORES + core
        return pltpu.make_async_remote_copy(
            src_ref=self.spread.at[to], dst_ref=self.moved.at[self.c],
            send_sem=self.es.at[k, core], recv_sem=self.er.at[self.c],
            device_id={"prow": to}, device_id_type=MESH,
        )

    def spread_partner(self):
        to = 1 - self.c
        return pltpu.make_async_remote_copy(
            src_ref=self.spread.at[to], dst_ref=self.moved.at[self.c],
            send_sem=self.es.at[0, 0], recv_sem=self.er.at[self.c],
            device_id=self.partner, device_id_type=MESH,
        )

    def spread_own(self):
        return pltpu.make_async_copy(self.spread.at[self.c], self.moved.at[self.c], self.er.at[self.c])

    def begin(self):
        for half in (0, 1):
            self.ring.start(half)
        for copy in self.own_copies():
            copy.start()

    def spread_some(self, ks):
        @pl.when(self.y == 0)
        def _():
            for k in ks:
                for core in (0, 1):
                    self.spread_copy(k, core).start()

    def spread_near(self):
        @pl.when(self.y == 0)
        def _():
            self.spread_partner().start()
            self.spread_own().start()

    def events(self, dt):
        half_n = self.ny // 2
        out = [(-1.0, self.begin), (3.9 * dt, self.spread_near)]
        order = [half_n] + [k for d in range(half_n - 1, 0, -1) for k in (d, self.ny - d)]
        for i, k in enumerate(order):
            out.append((0.1 + i * 0.5 * dt, lambda k=k: self.spread_some([k])))
        return out + self.ring.events([0.0, 0.3 * dt], dt)

    def finish(self):
        local, across = self.own_copies()
        local.wait()
        across.wait()
        self.ring.drain()
        for copy, index, way, hop, half in self.forwards:
            copy.wait_send()
        for copy, index, way, hop, half in self.forwards:
            ref = self.rows.at[index * CORES + 1 - self.c, half]
            pltpu.make_async_remote_copy(
                src_ref=ref, dst_ref=ref,
                send_sem=self.fs.at[way, hop - 1, half], recv_sem=self.fr.at[way, hop - 1, half],
                device_id=self.partner, device_id_type=MESH,
            ).wait_recv()
        for core in (0, 1):
            ref = self.moved.at[core]
            pltpu.make_async_copy(ref, ref, self.er.at[core]).wait()

        @pl.when(self.y == 0)
        def _():
            for k in range(1, self.ny):
                for core in (0, 1):
                    self.spread_copy(k, core).wait_send()
            self.spread_partner().wait_send()


def exchange_sems(ny):
    dma = pltpu.SemaphoreType.DMA
    return [
        dma((2, ny // 2, 2)), dma((2, ny // 2, 2)),
        dma((2, ny // 2, 2)), dma((2, ny // 2, 2)),
        dma, dma, dma((1,)), dma((ny, CORES)), dma((CORES,)),
    ]


def meet(peers):
    barrier = pltpu.get_barrier_semaphore()
    for peer in peers:
        pl.semaphore_signal(barrier, inc=1, device_id=peer, device_id_type=MESH)
    pl.semaphore_wait(barrier, len(peers))


def exchange_kernel(ny, sent, spread, rows, moved, *sems):
    ex = RowExchange(ny, sent, spread, rows, moved, sems)
    meet(ex.barrier_peers())
    run_events(ex.events(3.8))
    ex.finish()


def row_exchange(sent, spread, ny, cid):
    width = sent.shape[-1]
    return pl.pallas_call(
        lambda *refs: exchange_kernel(ny, *refs),
        out_shape=(
            jax.ShapeDtypeStruct((ny * CORES, 2, CAP // 2, width), jnp.bfloat16),
            jax.ShapeDtypeStruct((CORES, DCAP, width), jnp.bfloat16),
        ),
        in_specs=[ANY, ANY],
        out_specs=(ANY, ANY),
        scratch_shapes=exchange_sems(ny),
        compiler_params=pltpu.CompilerParams(collective_id=cid, has_side_effects=True),
        name="row_exchange",
    )(sent, spread)


def meet_with_roots(near, pcol, n):
    barrier = pltpu.get_barrier_semaphore()

    def signal(peer):
        pl.semaphore_signal(barrier, inc=1, device_id=peer, device_id_type=MESH)

    for root in (0, 1):
        @pl.when(pcol == root)
        def _():
            for k in range(1, n):
                signal({"pcol": lax.rem(pcol + k, n)})

        @pl.when(pcol != root)
        def _():
            signal({"pcol": root})

    for peer in near:
        signal(peer)

    @pl.when(pcol < 2)
    def _():
        pl.semaphore_wait(barrier, len(near) + n)

    @pl.when(pcol >= 2)
    def _():
        pl.semaphore_wait(barrier, len(near) + 2)


class Scatter:
    def __init__(self, pcol, n, piece, slot, send, recv):
        self.pcol, self.n, self.piece, self.slot, self.send, self.recv = pcol, n, piece, slot, send, recv

    def copy(self, k):
        to = lax.rem(self.pcol + k, self.n)
        return pltpu.make_async_remote_copy(
            src_ref=self.piece(to), dst_ref=self.slot(self.pcol, to),
            send_sem=self.send.at[k], recv_sem=self.recv.at[self.pcol],
            device_id={"pcol": to}, device_id_type=MESH)

    def start(self):
        @pl.when(self.pcol < 2)
        def _():
            for k in range(1, self.n):
                self.copy(k).start()
            pltpu.make_async_copy(
                self.piece(self.pcol), self.slot(self.pcol, self.pcol), self.recv.at[self.pcol]
            ).start()

    def landed(self, panel):
        ref = self.slot(panel, self.pcol)
        pltpu.make_async_copy(ref, ref, self.recv.at[panel]).wait()

    def drain(self):
        @pl.when(self.pcol < 2)
        def _():
            for k in range(1, self.n):
                self.copy(k).wait_send()


class Direct:
    def __init__(self, n, pos, goto, item, send, recv):
        self.n, self.pos, self.goto, self.item, self.send, self.recv = n, pos, goto, item, send, recv

    def copy(self, k, half):
        to = lax.rem(self.pos + k, self.n)
        return pltpu.make_async_remote_copy(
            src_ref=self.item(self.pos, half), dst_ref=self.item(self.pos, half),
            send_sem=self.send.at[k, half], recv_sem=self.recv.at[k, half],
            device_id=self.goto(to), device_id_type=MESH)

    def start(self):
        for half in (0, 1):
            self.start_half(half)

    def start_half(self, half):
        for k in sorted(range(1, self.n), key=lambda k: -min(k, self.n - k)):
            self.copy(k, half).start()

    def wait(self, half):
        for k in range(1, self.n):
            ref = self.item(lax.rem(self.pos + self.n - k, self.n), half)
            pltpu.make_async_copy(ref, ref, self.recv.at[k, half]).wait()

    def drain(self):
        for half in (0, 1):
            for k in range(1, self.n):
                self.copy(k, half).wait_send()


def first_kernel(ny, nz, nexch, *refs):
    tile, sent, spread, line, rows, moved = refs[:6]
    ex = RowExchange(ny, sent, spread, rows, moved, refs[6 : 6 + nexch])
    ss, sr, xs, xr = refs[6 + nexch :]
    pcol = lax.axis_index("pcol")
    n = nz * NX
    z, x = lax.div(pcol, NX), lax.rem(pcol, NX)
    scatter = Scatter(
        pcol, n,
        lambda to: tile.at[pl.ds(pl.multiple_of(to * PA, PA), PA), pl.ds(0, NB)],
        lambda panel, to: line.at[panel, lax.rem(to, NX)], ss, sr)
    gather = Direct(NX, x, lambda i: {"pcol": z * NX + i}, lambda i, h: line.at[h, i], xs, xr)
    near = ex.barrier_peers() + [{"pcol": z * NX + lax.rem(x + d, NX)} for d in range(1, NX)]
    meet_with_roots(near, pcol, n)

    def pass_on():
        for panel in (0, 1):
            scatter.landed(panel)
            gather.start_half(panel)

    run_events(ex.events(3.8) + [(-0.5, scatter.start), (13.0, pass_on)])
    ex.finish()
    for panel in (0, 1):
        gather.wait(panel)
    gather.drain()
    scatter.drain()


def first_exchange(tile, sent, spread, ny, nz, cid):
    width = sent.shape[-1]
    sems = exchange_sems(ny)
    dma = pltpu.SemaphoreType.DMA
    return pl.pallas_call(
        lambda *refs: first_kernel(ny, nz, len(sems), *refs),
        out_shape=(
            jax.ShapeDtypeStruct((2, NX, PA, NB), jnp.bfloat16),
            jax.ShapeDtypeStruct((ny * CORES, 2, CAP // 2, width), jnp.bfloat16),
            jax.ShapeDtypeStruct((CORES, DCAP, width), jnp.bfloat16),
        ),
        in_specs=[ANY] * 3,
        out_specs=(ANY,) * 3,
        scratch_shapes=sems + [dma((nz * NX,)), dma((2,)), dma((NX, 2)), dma((NX, 2))],
        compiler_params=pltpu.CompilerParams(collective_id=cid, has_side_effects=True),
        name="first_exchange",
    )(tile, sent, spread)


def second_kernel(ny, nz, nexch, *refs):
    line, small, sent, spread, raw, extra, other, rows, moved = refs[:9]
    ex = RowExchange(ny, sent, spread, rows, moved, refs[9 : 9 + nexch])
    (azs, azr, bzs, bzr, bxs, bxr, ss, sr, ts, tr, to_s, to_r, own) = refs[9 + nexch :]
    pcol = lax.axis_index("pcol")
    n = nz * NX
    z, x = lax.div(pcol, NX), lax.rem(pcol, NX)

    def to_x(i):
        return {"pcol": z * NX + i}

    def to_z(i):
        return {"pcol": i * NX + x}

    near = ex.barrier_peers()
    near += [to_x(lax.rem(x + d, NX)) for d in (1, NX - 1)]
    near += [to_z(lax.rem(z + d, nz)) for d in range(1, nz)]
    meet_with_roots(near, pcol, n)

    def across(index, way, hop, half):
        s, r = (ts.at[way, hop - 1, half], tr.at[way, hop - 1, half]) if hop else (to_s.at[half], to_r.at[half])
        return pltpu.make_async_remote_copy(
            src_ref=extra.at[half, index, pl.ds(0, HALF)], dst_ref=other.at[half, index],
            send_sem=s, recv_sem=r, device_id=ex.partner, device_id_type=MESH)

    crossing = []

    def cross(index, ref, way, hop, half):
        copy = across(index, way, hop, half)
        copy.start()
        crossing.append(copy)

    def band(i):
        return pl.ds(pl.multiple_of(i * PB, PB), PB)

    scatter = Scatter(
        pcol, n,
        lambda to: small.at[lax.rem(to, NX), band(lax.div(to, NX))],
        lambda panel, to: extra.at[panel, lax.rem(to, NX), band(lax.div(to, NX))], ss, sr)
    az = Ring(nz, z, to_z, lambda i, h: raw.at[h, i], azs, azr, fresh=lambda h: line.at[h])
    bz = Direct(nz, z, to_z, lambda i, h: extra.at[h, x, band(i)], bzs, bzr)
    bx = Ring(NX, x, to_x, lambda i, h: extra.at[h, i], bxs, bxr, arrived=cross)
    keep = [pltpu.make_async_copy(line.at[h], raw.at[h, z], own.at[h]) for h in (0, 1)]

    def begin_az():
        for half in (0, 1):
            az.start(half)
        for copy in keep:
            copy.start()

    def begin_bz():
        for half in (0, 1):
            scatter.landed(half)
            bz.start_half(half)

    def begin_bx(half):
        bz.wait(half)
        bx.start(half)
        cross(x, None, 0, 0, half)

    events = [(-2.0, scatter.start), (-0.9, begin_az)]
    events += ex.events(T_Y)
    events += az.events([T_A0, T_A1], T_AD)
    events += [(T_BZ, begin_bz)]
    events += [(T_BX + h * 0.4, lambda h=h: begin_bx(h)) for h in (0, 1)]
    events += bx.events([T_BX + 0.2, T_BX + 1.2], T_BXD)
    run_events(events)
    ex.finish()
    for ring in (az, bx):
        for half in (0, 1):
            ring.complete(half)
        ring.drain()
    bz.drain()
    scatter.drain()
    for copy in crossing:
        copy.wait()
    for copy in keep:
        copy.wait()


def second_exchange(line, small, sent, spread, ny, nz, cid):
    width = sent.shape[-1]
    dma = pltpu.SemaphoreType.DMA
    sems = exchange_sems(ny)
    zring, xring, zdirect = dma((2, nz // 2, 2)), dma((2, NX // 2, 2)), dma((nz, 2))
    return pl.pallas_call(
        lambda *refs: second_kernel(ny, nz, len(sems), *refs),
        out_shape=(
            jax.ShapeDtypeStruct((2, nz, NX, PA, NB), jnp.bfloat16),
            jax.ShapeDtypeStruct((2, NX, nz * PB, LANES), jnp.bfloat16),
            jax.ShapeDtypeStruct((2, NX, HALF, LANES), jnp.bfloat16),
            jax.ShapeDtypeStruct((ny * CORES, 2, CAP // 2, width), jnp.bfloat16),
            jax.ShapeDtypeStruct((CORES, DCAP, width), jnp.bfloat16),
        ),
        in_specs=[ANY] * 4,
        out_specs=(ANY,) * 5,
        scratch_shapes=sems
        + [zring, zring, zdirect, zdirect, xring, xring]
        + [dma((nz * NX,)), dma((2,)), xring, xring, dma((2,)), dma((2,)), dma((2,))],
        compiler_params=pltpu.CompilerParams(collective_id=cid, has_side_effects=True),
        name="second_exchange",
    )(line, small, sent, spread)


def dot(a, b):
    return jnp.dot(a, b, preferred_element_type=jnp.float32)


def bdot(a, b):
    return dot(a, b).astype(jnp.bfloat16)


def ids(shape, axis):
    return lax.broadcasted_iota(jnp.int32, shape, axis).astype(jnp.float32)


def to_row(col):
    n = col.shape[0]
    return jnp.sum(jnp.where(ids((n, n), 0) == ids((n, n), 1), col, 0.0), axis=0, keepdims=True)


def to_col(row):
    n = row.shape[1]
    return jnp.sum(jnp.where(ids((n, n), 0) == ids((n, n), 1), row, 0.0), axis=1, keepdims=True)


def along(table):
    return jnp.sum(table, axis=1, keepdims=True)


def down(table):
    return jnp.sum(table, axis=0, keepdims=True)


def hot(mask):
    return jnp.where(mask, 1.0, 0.0).astype(jnp.bfloat16)


def index_kernel(nprow, piv, tile, sent0, sent1, spread0, spread1, slot_out, into_out, rounds_out):
    prow = lax.axis_index("prow")
    core = lax.rem(prow, CORES).astype(jnp.float32)
    prow_f = prow.astype(jnp.float32)
    rows = [piv[k : k + 1, :].astype(jnp.float32) for k in (0, 1)]
    cols = [to_col(r) for r in rows]
    i0, i1 = ids((NB, NB), 0), ids((NB, NB), 1)
    receive = []
    for k in (0, 1):
        first = float(k * NB)
        top_c, top_r = ids((NB, 1), 0) + first, ids((1, NB), 1) + first
        left_c = 1.0 - along(jnp.where(rows[k] == top_c, 1.0, 0.0))
        left_r = 1.0 - down(jnp.where(cols[k] == top_r, 1.0, 0.0))
        rank_r = down(jnp.where(i0 < i1, left_c, 0.0))
        vac_r = jnp.where(rows[k] >= first + NB, 1.0, 0.0)
        vac_c = along(jnp.where(i1 < i0, vac_r, 0.0))
        receive.append(along(jnp.where((rank_r == vac_c) & (left_r > 0.5), top_r, 0.0)))
    receive0_r = to_row(receive[0])

    def lookup(keys):
        hit = keys == rows[0]
        found = along(jnp.where(hit, 1.0, 0.0))
        return jnp.where(found > 0.5, along(jnp.where(hit, receive0_r, 0.0)), keys)

    src1, from1 = lookup(cols[1]), lookup(receive[1])
    again = along(jnp.where(cols[0] == rows[1], 1.0, 0.0))

    def owner(v):
        return (lax.shift_right_logical(v.astype(jnp.int32), 9) & (nprow - 1)).astype(jnp.float32)

    def local(v):
        v = v.astype(jnp.int32)
        return (lax.shift_right_logical(v, 13) * NB + (v & (NB - 1))).astype(jnp.float32)

    n = 2 * NB
    t_c = jnp.concatenate([cols[0], src1], axis=0)
    d_dst = jnp.concatenate([cols[0], cols[1]], axis=0)
    d_src = jnp.concatenate([receive[0], from1], axis=0)
    fresh = jnp.concatenate([again, jnp.zeros_like(again)], axis=0)
    valid = (d_dst >= 2.0 * NB) & (fresh < 0.5)
    t_group = owner(t_c)
    group = jnp.where(valid, owner(d_dst) * CORES + jnp.where(d_src >= NB, 1.0, 0.0), -1000.0)
    lanes = ids((n, 128), 1)
    members = jnp.where((lanes == t_group) | (lanes == group + nprow), 1.0, 0.0)
    before = dot(hot(ids((n, n), 1) < ids((n, n), 0)), members.astype(jnp.bfloat16)) * members
    is_t = lanes < nprow
    t_rank = along(jnp.where(is_t, before, 0.0))
    d_rank = along(jnp.where(is_t, 0.0, before))
    slot_c = jnp.where(t_rank < CAP, t_group * CAP + t_rank, -1.0)
    key_c = jnp.where(valid & (d_rank < DCAP), group * DCAP + d_rank, -1.0)
    slot_out[...] = slot_c.astype(jnp.int32)
    packed = jnp.where(lanes == 0, slot_c, jnp.where(lanes == 1, local(t_c), jnp.where(lanes == 2, key_c, d_src)))
    packed = packed.T
    slot_r, local_r, key_r, src_r = (packed[k : k + 1, :] for k in range(4))
    mine = ids((CAP, 1), 0) + prow_f * CAP
    pick = along(jnp.where(slot_r == mine, local_r + 1.0, 0.0)) - 1.0
    sent = bdot(hot(pick == ids((CAP, n), 1)), tile[...])
    sent0[...] = sent[:, :NB]
    sent1[...] = sent[:, NB:]
    lane = ids((1, 128), 1)
    wanted = jnp.where(lane < MOVED, lane + prow_f * MOVED, -2.0)
    into = down(jnp.where(key_c == wanted, local(d_dst) + 1.0, 0.0)) - 1.0
    into_out[...] = into.astype(jnp.int32)
    most_t = jnp.max(t_rank) * (1.0 / CAP)
    most_d = jnp.max(jnp.where(valid, d_rank, 0.0)) * (1.0 / DCAP)
    rounds_out[0, 0] = jnp.where(jnp.maximum(most_t, most_d) > 1.0 - 0.25 / CAP, 2, 1).astype(jnp.int32)

    @pl.when(prow < CORES)
    def _():
        s = ids((MOVED, 1), 0)

        def one_chip(q, _):
            second = jnp.where(s >= DCAP, 1.0, 0.0)
            want = (2.0 * q.astype(jnp.float32) + second) * MOVED + core * DCAP + s - second * DCAP
            src = along(jnp.where(key_r == want, src_r + 1.0, 0.0)) - 1.0 - core * NB
            out = bdot(hot(src == ids((MOVED, NB), 1)), tile[:NB, :])
            here = pl.ds(pl.multiple_of(q * MOVED, MOVED), MOVED)
            spread0[here, :] = out[:, :NB]
            spread1[here, :] = out[:, NB:]
            return 0

        lax.fori_loop(0, nprow // 2, one_chip, 0)


def index_and_pack(pivots, tile, nprow):
    n = 2 * NB
    bf16 = jnp.bfloat16
    vmem = pl.BlockSpec(memory_space=pltpu.VMEM)
    return pl.pallas_call(
        lambda *refs: index_kernel(nprow, *refs),
        out_shape=(
            jax.ShapeDtypeStruct((CAP, NB), bf16), jax.ShapeDtypeStruct((CAP, NB), bf16),
            jax.ShapeDtypeStruct((nprow * DCAP, NB), bf16), jax.ShapeDtypeStruct((nprow * DCAP, NB), bf16),
            jax.ShapeDtypeStruct((n, 1), jnp.int32), jax.ShapeDtypeStruct((1, 128), jnp.int32),
            jax.ShapeDtypeStruct((1, 1), jnp.int32),
        ),
        in_specs=[vmem, vmem],
        out_specs=(vmem,) * 6 + (pl.BlockSpec(memory_space=pltpu.SMEM),),
        name="index_and_pack",
    )(pivots, tile)


def panel_tops_kernel(rows, moved, slot, small):
    pcol, prow = lax.axis_index("pcol"), lax.axis_index("prow")
    first = jnp.where(pcol == 0, NB, 0) + lax.rem(prow, CORES) * HALF
    first = pl.multiple_of(first, HALF)
    keys = slot[pl.ds(first, HALF), :]
    total = rows.shape[0]
    place = jnp.where(keys == lax.broadcasted_iota(jnp.int32, (HALF, total), 1), 1.0, 0.0).astype(jnp.bfloat16)
    part = bdot(place, rows[...])
    last = small.shape[1] - HALF - MOVED
    for x in range(NX):
        lanes = slice(x * LANES, (x + 1) * LANES)
        small[x, pl.ds(0, HALF), :] = part[:, lanes]
        small[x, pl.ds(HALF, MOVED), :] = moved[:, lanes]
        small[x, pl.ds(HALF + MOVED, last), :] = jnp.zeros((last, LANES), jnp.bfloat16)


def panel_tops(rows, moved, slot, nz):
    vmem = pl.BlockSpec(memory_space=pltpu.VMEM)
    return pl.pallas_call(
        panel_tops_kernel,
        out_shape=jax.ShapeDtypeStruct((NX, nz * PB, LANES), jnp.bfloat16),
        in_specs=[vmem] * 3,
        out_specs=vmem,
        name="panel_tops",
    )(rows, moved, slot)


def update_kernel(raw, extra, other, rows0, rows1, moved0, moved1, slot, into, tile, low_inv, up_inv,
                  out, top, low, up0, up1):
    pcol, prow = lax.axis_index("pcol"), lax.axis_index("prow")
    core = lax.rem(prow, CORES)
    f32 = jnp.float32
    step = NB // 2
    halves = (pl.ds(0, NB), pl.ds(NB, NB))
    total = rows0.shape[0]

    def spot(i):
        return pl.ds(pl.multiple_of(i * step, step), step)

    def place_rows(i, _):
        keys = slot[spot(i), :]
        place = jnp.where(keys == lax.broadcasted_iota(jnp.int32, (step, total), 1), 1.0, 0.0).astype(jnp.bfloat16)
        top[spot(i), halves[0]] = bdot(place, rows0[...])
        top[spot(i), halves[1]] = bdot(place, rows1[...])
        return 0

    lax.fori_loop(0, 4, place_rows, 0)
    l0, l1, u0, u1 = low_inv[0], low_inv[1], up_inv[0], up_inv[1]
    panel_tops = []
    for k in (0, 1):
        own = jnp.concatenate([extra[k, x, :HALF, :] for x in range(NX)], axis=1)
        far = jnp.concatenate([other[k, x] for x in range(NX)], axis=1)
        panel_tops.append(jnp.concatenate(
            [jnp.where(core == 0, own, far), jnp.where(core == 0, far, own)], axis=0))
    corner = bdot(panel_tops[0], u0)
    upper = bdot(l0, panel_tops[1])
    moved_panel = [
        jnp.concatenate([extra[k, x, HALF : HALF + MOVED, :] for x in range(NX)], axis=1) for k in (0, 1)
    ]
    for cols in halves:
        up0[:, cols] = bdot(l0, top[pl.ds(0, NB), cols])
        low[:, cols] = (top[pl.ds(NB, NB), cols].astype(f32) - dot(corner, up0[:, cols])).astype(jnp.bfloat16)
        up1[:, cols] = bdot(l1, low[:, cols])

    def update(i, _):
        here = spot(i)
        ids_c = lax.broadcasted_iota(jnp.int32, (step, MOVED), 0) + i * step
        match = jnp.where(ids_c == into[:, :MOVED], 1.0, 0.0)
        hit = jnp.max(match, axis=1, keepdims=True) > 0.5
        insert = match.astype(jnp.bfloat16)

        def with_moved(new, old):
            return jnp.where(hit, dot(insert, new), old.astype(f32)).astype(jnp.bfloat16)

        factor0 = bdot(with_moved(moved_panel[0], raw[0, here, :]), u0)
        panel1 = (with_moved(moved_panel[1], raw[1, here, :]).astype(f32) - dot(factor0, upper)).astype(jnp.bfloat16)
        factor1 = bdot(panel1, u1)
        for d, (cols, moved) in enumerate(zip(halves, (moved0, moved1))):
            new = with_moved(moved[...], tile[here, cols]).astype(f32)
            new = (new - dot(factor0, up0[:, cols])).astype(jnp.bfloat16).astype(f32)
            new = (new - dot(factor1, up1[:, cols])).astype(jnp.bfloat16)
            if d == 0:
                new = jnp.where(pcol == 0, factor0, jnp.where(pcol == 1, factor1, new))
            out[here, cols] = new
        return 0

    lax.fori_loop(0, 4, update, 0)
    heads = pl.ds(0, NB)

    @pl.when(prow == 0)
    def _():
        out[heads, halves[0]] = jnp.where(pcol == 0, top[heads, halves[0]], up0[:, halves[0]])
        out[heads, halves[1]] = up0[:, halves[1]]

    @pl.when(prow == 1)
    def _():
        out[heads, halves[0]] = jnp.where(
            pcol == 0, corner, jnp.where(pcol == 1, low[:, halves[0]], up1[:, halves[0]]))
        out[heads, halves[1]] = up1[:, halves[1]]


def update(*args):
    n = 2 * NB
    vmem = pl.BlockSpec(memory_space=pltpu.VMEM)
    bf16 = jnp.bfloat16
    return pl.pallas_call(
        update_kernel,
        out_shape=jax.ShapeDtypeStruct((n, n), bf16),
        in_specs=[vmem] * len(args),
        out_specs=vmem,
        scratch_shapes=[pltpu.VMEM((n, n), bf16)] + [pltpu.VMEM((NB, n), bf16)] * 3,
        name="update",
    )(*args)


def count_before(flags):
    n = flags.shape[0]
    ahead = jnp.arange(n)[None, :] < jnp.arange(n)[:, None]
    return jnp.sum((ahead & flags[None, :]).astype(jnp.int32), axis=1)


def pairing(sources, first_row):
    top_ids = first_row + jnp.arange(NB, dtype=jnp.int32)
    leftover = jnp.logical_not(jnp.any(sources[None, :] == top_ids[:, None], axis=1))
    left_rank = count_before(leftover)
    vacated = sources >= first_row + NB
    vac_rank = count_before(vacated)
    table = leftover[None, :] & (left_rank[None, :] == vac_rank[:, None])
    return jnp.sum(jnp.where(table, top_ids[None, :], 0), axis=1)


def lookup(keys, names, values):
    hit = keys[:, None] == names[None, :]
    found = jnp.sum(jnp.where(hit, values[None, :], 0), axis=1)
    return jnp.where(jnp.any(hit, axis=1), found, keys)


def rank_in(group):
    n = group.shape[0]
    ahead = jnp.arange(n)[None, :] < jnp.arange(n)[:, None]
    same = group[None, :] == group[:, None]
    return jnp.sum((same & ahead).astype(jnp.int32), axis=1)


def slot_values(keys, values, wanted):
    hit = wanted[:, None] == keys[None, :]
    return jnp.sum(jnp.where(hit, values[None, :] + 1, 0), axis=1) - 1


def one_hot(index, n):
    return (index[:, None] == jnp.arange(n, dtype=jnp.int32)[None, :]).astype(jnp.bfloat16)


def collect_rounds(tile, pivots, nprow, ny):
    prow = lax.axis_index("prow")
    core = lax.rem(prow, CORES)
    s0, s1 = pivots[0], pivots[1]
    receive0, receive1 = pairing(s0, 0), pairing(s1, NB)
    src1 = lookup(s1, s0, receive0)
    from1 = lookup(receive1, s0, receive0)
    again = jnp.any(s0[:, None] == s1[None, :], axis=1)
    big = jnp.int32(1 << 20)

    def owner(rows):
        return lax.rem(rows // NB, nprow)

    def local(rows):
        return rows // (NB * nprow) * NB + lax.rem(rows, NB)

    t_src = jnp.concatenate([s0, src1])
    t_owner = owner(t_src)
    t_rank = rank_in(t_owner)
    t_local = local(t_src)
    d_dst = jnp.concatenate([s0, s1])
    d_src = jnp.concatenate([receive0, from1])
    d_valid = (d_dst >= 2 * NB) & jnp.concatenate([jnp.logical_not(again), jnp.ones((NB,), jnp.bool_)])
    d_core = d_src // NB
    d_owner = owner(d_dst)
    d_rank = rank_in(jnp.where(d_valid, d_owner * CORES + d_core, -1))
    d_local = local(d_dst)
    rounds = jnp.maximum(jnp.max(t_rank) // CAP, jnp.max(jnp.where(d_valid, d_rank, 0)) // DCAP) + 1

    def body(state):
        r, top, now = state
        t_in = (t_rank // CAP) == r
        t_slot = t_owner * CAP + lax.rem(t_rank, CAP)
        t_key = jnp.where(t_in, t_slot, big)
        d_in = d_valid & ((d_rank // DCAP) == r)
        d_key = jnp.where(d_in, (d_owner * CORES + d_core) * DCAP + lax.rem(d_rank, DCAP), big)
        pick = one_hot(slot_values(t_key, t_local, prow * CAP + jnp.arange(CAP, dtype=jnp.int32)), 2 * NB)
        every = jnp.arange(nprow * DCAP, dtype=jnp.int32)
        wanted = (every // DCAP * CORES + core) * DCAP + lax.rem(every, DCAP)
        spread_sel = one_hot(slot_values(d_key, d_src - core * NB, wanted), NB)
        mine = prow * MOVED + jnp.arange(MOVED, dtype=jnp.int32)
        into = slot_values(d_key, d_local, mine)
        insert = (jnp.arange(2 * NB, dtype=jnp.int32)[:, None] == into[None, :]).astype(jnp.bfloat16)
        rows, moved = row_exchange(
            bdot(pick, tile).reshape(2, CAP // 2, 2 * NB),
            bdot(spread_sel, tile[:NB]).reshape(nprow, DCAP, 2 * NB), ny, 1)
        place = one_hot(jnp.where(t_in, t_slot, -1), nprow * CAP)
        top = top + bdot(place, rows.reshape(nprow * CAP, 2 * NB))
        new = bdot(insert, moved.reshape(MOVED, 2 * NB))
        return r + 1, top, jnp.where(jnp.any(insert > 0, axis=1)[:, None], new, now)

    _, top, now = lax.while_loop(
        lambda s: s[0] < rounds, body, (jnp.int32(0), jnp.zeros_like(tile), tile))
    return top, now


def per_device(matrix, pivots, lower_inverse, upper_inverse):
    nprow, npcol = lax.axis_size("prow"), lax.axis_size("pcol")
    ny, nz = nprow // CORES, npcol // NX
    n = 2 * NB
    tile = matrix.reshape(n, n)
    *packed, slot, into, rounds = index_and_pack(pivots, tile, nprow)

    def finish(tile, packed, slot, into, known, cids):
        sents = [v.reshape(2, CAP // 2, NB) for v in packed[:2]]
        spreads = [v.reshape(nprow, DCAP, NB) for v in packed[2:]]
        line, rows0, moved0 = first_exchange(tile, sents[0], spreads[0], ny, nz, cids[0])
        rows0, moved0 = rows0.reshape(nprow * CAP, NB), moved0.reshape(MOVED, NB)
        if known is not None:
            rows0, moved0 = known[0], jnp.zeros_like(moved0)
        small = panel_tops(rows0, moved0, slot, nz)
        raw, extra, other, rows1, moved1 = second_exchange(line, small, sents[1], spreads[1], ny, nz, cids[1])
        rows1, moved1 = rows1.reshape(nprow * CAP, NB), moved1.reshape(MOVED, NB)
        if known is not None:
            rows1, moved1 = known[1], jnp.zeros_like(moved1)
        return update(
            raw.reshape(2, n, NB), extra, other, rows0, rows1, moved0, moved1, slot, into, tile, lower_inverse, upper_inverse)

    def one_round(tile):
        return finish(tile, packed, slot, into, None, (0, 2))

    def many_rounds(tile):
        top, now = collect_rounds(tile, pivots, nprow, ny)
        top = jnp.pad(top, ((0, nprow * CAP - n), (0, 0)))
        empty = [jnp.zeros_like(v) for v in packed]
        order = jnp.arange(n, dtype=jnp.int32)[:, None]
        return finish(now, empty, order, jnp.full_like(into, -1), (top[:, :NB], top[:, NB:]), (3, 4))

    out = lax.cond(rounds[0, 0] > 1, many_rounds, one_round, tile)
    return out.reshape(matrix.shape)


def solution(mesh):
    return jax.shard_map(
        per_device,
        mesh=mesh,
        in_specs=(P(None, "prow", None, None, "pcol", None), P(), P(), P()),
        out_specs=P(None, "prow", None, None, "pcol", None),
        check_vma=False,
    )
```

```python
import jax
import jax.numpy as jnp
from jax import lax
from jax.experimental import pallas as pl
from jax.experimental.pallas import tpu as pltpu
from jax.sharding import PartitionSpec as P

NB = 512
CORES = 2
NX = 4
CAP = 96
DCAP = 56
MOVED = CORES * DCAP
HALF = NB // CORES
LANES = NB // NX
PA = 32
PB = 48
MESH = pl.DeviceIdType.MESH
T_Y, T_A0, T_A1, T_AD, T_BZ, T_BX, T_BXD, T_TOP = 4.5, 0.0, 2.5, 5.8, 3.5, 11.0, 4.0, 20.5
ANY = pl.BlockSpec(memory_space=pl.ANY)


class Ring:
    def __init__(self, n, pos, goto, item, send, recv, fresh=None, arrived=None):
        self.n, self.pos, self.goto, self.item = n, pos, goto, item
        self.send, self.recv = send, recv
        self.fresh, self.arrived = fresh, arrived
        self.got = [0, 0]

    def carries(self, way, hop, half):
        return hop < self.n // 2 or (hop == self.n // 2 and half == way)

    def copy(self, way, hop, half):
        step = 1 if way == 0 else -1
        index = lax.rem(self.pos + self.n - step * (hop - 1), self.n)
        target = lax.rem(self.pos + self.n + step, self.n)
        src = self.item(index, half)
        if hop == 1 and self.fresh is not None:
            src = self.fresh(half)
        return pltpu.make_async_remote_copy(
            src_ref=src,
            dst_ref=self.item(index, half),
            send_sem=self.send.at[way, hop - 1, half],
            recv_sem=self.recv.at[way, hop - 1, half],
            device_id=self.goto(target),
            device_id_type=MESH,
        )

    def landed(self, way, hop, half):
        step = 1 if way == 0 else -1
        index = lax.rem(self.pos + self.n - step * hop, self.n)
        ref = self.item(index, half)
        return index, ref, pltpu.make_async_remote_copy(
            src_ref=ref,
            dst_ref=ref,
            send_sem=self.send.at[way, hop - 1, half],
            recv_sem=self.recv.at[way, hop - 1, half],
            device_id=self.goto(lax.rem(self.pos + 1, self.n)),
            device_id_type=MESH,
        )

    def start(self, half):
        for way in (0, 1):
            self.copy(way, 1, half).start()

    def step(self, way, hop, half):
        index, ref, arrival = self.landed(way, hop, half)
        arrival.wait_recv()
        if self.carries(way, hop + 1, half):
            self.copy(way, hop + 1, half).start()
        self.got[half] += 1
        if self.arrived is not None:
            self.arrived(index, ref, way, hop, half)

    def events(self, t0, dt):
        out = []
        for half in (0, 1):
            for hop in range(1, self.n // 2 + 1):
                for way in (0, 1):
                    if self.carries(way, hop, half):
                        when = t0[half] + dt * hop
                        out.append((when, lambda w=way, h=hop, f=half: self.step(w, h, f)))
        return out

    def complete(self, half):
        assert self.got[half] == self.n - 1

    def drain(self):
        for half in (0, 1):
            for hop in range(1, self.n // 2 + 1):
                for way in (0, 1):
                    if self.carries(way, hop, half):
                        self.copy(way, hop, half).wait_send()


def run_events(events):
    for _, act in sorted(events, key=lambda e: e[0]):
        act()


class RowExchange:
    def __init__(self, ny, sent, spread, rows, moved, sems):
        self.ny, self.sent, self.spread, self.rows, self.moved = ny, sent, spread, rows, moved
        (self.rs, self.rr, self.fs, self.fr, self.os, self.orr, self.ls, self.es, self.er) = sems
        prow = lax.axis_index("prow")
        self.y, self.c = lax.div(prow, CORES), lax.rem(prow, CORES)
        self.partner = {"prow": self.y * CORES + 1 - self.c}
        self.ring = Ring(
            ny, self.y,
            lambda i: {"prow": i * CORES + self.c},
            lambda i, half: rows.at[i * CORES + self.c, half],
            self.rs, self.rr,
            fresh=lambda half: sent.at[half],
            arrived=self.forward,
        )
        self.forwards = []

    def barrier_peers(self):
        ids = [{"prow": lax.rem(self.y + k, self.ny) * CORES + c} for k in range(1, self.ny) for c in (0, 1)]
        return ids + [self.partner]

    def forward_copy(self, index, way, hop, half):
        return pltpu.make_async_remote_copy(
            src_ref=self.rows.at[index * CORES + self.c, half],
            dst_ref=self.rows.at[index * CORES + self.c, half],
            send_sem=self.fs.at[way, hop - 1, half],
            recv_sem=self.fr.at[way, hop - 1, half],
            device_id=self.partner,
            device_id_type=MESH,
        )

    def forward(self, index, ref, way, hop, half):
        copy = self.forward_copy(index, way, hop, half)
        copy.start()
        self.forwards.append((copy, index, way, hop, half))

    def own_copies(self):
        mine = self.rows.at[self.y * CORES + self.c]
        local = pltpu.make_async_copy(self.sent, mine, self.ls.at[0])
        across = pltpu.make_async_remote_copy(
            src_ref=self.sent, dst_ref=mine, send_sem=self.os, recv_sem=self.orr,
            device_id=self.partner, device_id_type=MESH,
        )
        return local, across

    def spread_copy(self, k, core):
        to = lax.rem(self.y + k, self.ny) * CORES + core
        return pltpu.make_async_remote_copy(
            src_ref=self.spread.at[to], dst_ref=self.moved.at[self.c],
            send_sem=self.es.at[k, core], recv_sem=self.er.at[self.c],
            device_id={"prow": to}, device_id_type=MESH,
        )

    def spread_partner(self):
        to = 1 - self.c
        return pltpu.make_async_remote_copy(
            src_ref=self.spread.at[to], dst_ref=self.moved.at[self.c],
            send_sem=self.es.at[0, 0], recv_sem=self.er.at[self.c],
            device_id=self.partner, device_id_type=MESH,
        )

    def spread_own(self):
        return pltpu.make_async_copy(self.spread.at[self.c], self.moved.at[self.c], self.er.at[self.c])

    def begin(self):
        for half in (0, 1):
            self.ring.start(half)
        for copy in self.own_copies():
            copy.start()

    def spread_some(self, ks):
        @pl.when(self.y == 0)
        def _():
            for k in ks:
                for core in (0, 1):
                    self.spread_copy(k, core).start()

    def spread_near(self):
        @pl.when(self.y == 0)
        def _():
            self.spread_partner().start()
            self.spread_own().start()

    def events(self, dt):
        half_n = self.ny // 2
        out = [(-1.0, self.begin), (3.9 * dt, self.spread_near)]
        order = [half_n] + [k for d in range(half_n - 1, 0, -1) for k in (d, self.ny - d)]
        for i, k in enumerate(order):
            out.append((0.1 + i * 0.5 * dt, lambda k=k: self.spread_some([k])))
        return out + self.ring.events([0.0, 0.3 * dt], dt)

    def finish(self):
        local, across = self.own_copies()
        local.wait()
        across.wait()
        self.ring.drain()
        for copy, index, way, hop, half in self.forwards:
            copy.wait_send()
        for copy, index, way, hop, half in self.forwards:
            ref = self.rows.at[index * CORES + 1 - self.c, half]
            pltpu.make_async_remote_copy(
                src_ref=ref, dst_ref=ref,
                send_sem=self.fs.at[way, hop - 1, half], recv_sem=self.fr.at[way, hop - 1, half],
                device_id=self.partner, device_id_type=MESH,
            ).wait_recv()
        for core in (0, 1):
            ref = self.moved.at[core]
            pltpu.make_async_copy(ref, ref, self.er.at[core]).wait()

        @pl.when(self.y == 0)
        def _():
            for k in range(1, self.ny):
                for core in (0, 1):
                    self.spread_copy(k, core).wait_send()
            self.spread_partner().wait_send()


def exchange_sems(ny):
    dma = pltpu.SemaphoreType.DMA
    return [
        dma((2, ny // 2, 2)), dma((2, ny // 2, 2)),
        dma((2, ny // 2, 2)), dma((2, ny // 2, 2)),
        dma, dma, dma((1,)), dma((ny, CORES)), dma((CORES,)),
    ]


def meet(peers):
    barrier = pltpu.get_barrier_semaphore()
    for peer in peers:
        pl.semaphore_signal(barrier, inc=1, device_id=peer, device_id_type=MESH)
    pl.semaphore_wait(barrier, len(peers))


def exchange_kernel(ny, sent, spread, rows, moved, *sems):
    ex = RowExchange(ny, sent, spread, rows, moved, sems)
    meet(ex.barrier_peers())
    run_events(ex.events(3.8))
    ex.finish()


def row_exchange(sent, spread, ny, cid):
    width = sent.shape[-1]
    return pl.pallas_call(
        lambda *refs: exchange_kernel(ny, *refs),
        out_shape=(
            jax.ShapeDtypeStruct((ny * CORES, 2, CAP // 2, width), jnp.bfloat16),
            jax.ShapeDtypeStruct((CORES, DCAP, width), jnp.bfloat16),
        ),
        in_specs=[ANY, ANY],
        out_specs=(ANY, ANY),
        scratch_shapes=exchange_sems(ny),
        compiler_params=pltpu.CompilerParams(collective_id=cid, has_side_effects=True),
        name="row_exchange",
    )(sent, spread)


def meet_with_roots(near, pcol, n, meanwhile=None):
    barrier = pltpu.get_barrier_semaphore()

    def signal(peer):
        pl.semaphore_signal(barrier, inc=1, device_id=peer, device_id_type=MESH)

    for root in (0, 1):
        @pl.when(pcol == root)
        def _():
            for k in range(1, n):
                signal({"pcol": lax.rem(pcol + k, n)})

        @pl.when(pcol != root)
        def _():
            signal({"pcol": root})

    for peer in near:
        signal(peer)
    if meanwhile is not None:
        meanwhile()

    @pl.when(pcol < 2)
    def _():
        pl.semaphore_wait(barrier, len(near) + n)

    @pl.when(pcol >= 2)
    def _():
        pl.semaphore_wait(barrier, len(near) + 2)


class Scatter:
    def __init__(self, pcol, n, piece, slot, send, recv):
        self.pcol, self.n, self.piece, self.slot, self.send, self.recv = pcol, n, piece, slot, send, recv

    def copy(self, k):
        to = lax.rem(self.pcol + k, self.n)
        return pltpu.make_async_remote_copy(
            src_ref=self.piece(to), dst_ref=self.slot(self.pcol, to),
            send_sem=self.send.at[k], recv_sem=self.recv.at[self.pcol],
            device_id={"pcol": to}, device_id_type=MESH)

    def start(self):
        @pl.when(self.pcol < 2)
        def _():
            for k in range(1, self.n):
                self.copy(k).start()
            pltpu.make_async_copy(
                self.piece(self.pcol), self.slot(self.pcol, self.pcol), self.recv.at[self.pcol]
            ).start()

    def landed(self, panel):
        ref = self.slot(panel, self.pcol)
        pltpu.make_async_copy(ref, ref, self.recv.at[panel]).wait()

    def drain(self):
        @pl.when(self.pcol < 2)
        def _():
            for k in range(1, self.n):
                self.copy(k).wait_send()


class Direct:
    def __init__(self, n, pos, goto, item, send, recv):
        self.n, self.pos, self.goto, self.item, self.send, self.recv = n, pos, goto, item, send, recv

    def copy(self, k, half):
        to = lax.rem(self.pos + k, self.n)
        return pltpu.make_async_remote_copy(
            src_ref=self.item(self.pos, half), dst_ref=self.item(self.pos, half),
            send_sem=self.send.at[k, half], recv_sem=self.recv.at[k, half],
            device_id=self.goto(to), device_id_type=MESH)

    def start(self):
        for half in (0, 1):
            self.start_half(half)

    def start_half(self, half):
        for k in sorted(range(1, self.n), key=lambda k: -min(k, self.n - k)):
            self.copy(k, half).start()

    def wait(self, half):
        for k in range(1, self.n):
            ref = self.item(lax.rem(self.pos + self.n - k, self.n), half)
            pltpu.make_async_copy(ref, ref, self.recv.at[k, half]).wait()

    def drain(self):
        for half in (0, 1):
            for k in range(1, self.n):
                self.copy(k, half).wait_send()


def first_kernel(ny, nz, nexch, *refs):
    tile, sent, spread, line, rows, moved = refs[:6]
    ex = RowExchange(ny, sent, spread, rows, moved, refs[6 : 6 + nexch])
    ss, sr, xs, xr = refs[6 + nexch :]
    pcol = lax.axis_index("pcol")
    n = nz * NX
    z, x = lax.div(pcol, NX), lax.rem(pcol, NX)
    scatter = Scatter(
        pcol, n,
        lambda to: tile.at[pl.ds(pl.multiple_of(to * PA, PA), PA), pl.ds(0, NB)],
        lambda panel, to: line.at[panel, lax.rem(to, NX)], ss, sr)
    gather = Direct(NX, x, lambda i: {"pcol": z * NX + i}, lambda i, h: line.at[h, i], xs, xr)
    near = ex.barrier_peers() + [{"pcol": z * NX + lax.rem(x + d, NX)} for d in range(1, NX)]
    meet_with_roots(near, pcol, n)

    def pass_on():
        for panel in (0, 1):
            scatter.landed(panel)
            gather.start_half(panel)

    run_events(ex.events(3.8) + [(-0.5, scatter.start), (13.0, pass_on)])
    ex.finish()
    for panel in (0, 1):
        gather.wait(panel)
    gather.drain()
    scatter.drain()


def first_exchange(tile, sent, spread, ny, nz, cid):
    width = sent.shape[-1]
    sems = exchange_sems(ny)
    dma = pltpu.SemaphoreType.DMA
    return pl.pallas_call(
        lambda *refs: first_kernel(ny, nz, len(sems), *refs),
        out_shape=(
            jax.ShapeDtypeStruct((2, NX, PA, NB), jnp.bfloat16),
            jax.ShapeDtypeStruct((ny * CORES, 2, CAP // 2, width), jnp.bfloat16),
            jax.ShapeDtypeStruct((CORES, DCAP, width), jnp.bfloat16),
        ),
        in_specs=[ANY] * 3,
        out_specs=(ANY,) * 3,
        scratch_shapes=sems + [dma((nz * NX,)), dma((2,)), dma((NX, 2)), dma((NX, 2))],
        compiler_params=pltpu.CompilerParams(collective_id=cid, has_side_effects=True),
        name="first_exchange",
    )(tile, sent, spread)


def second_kernel(ny, nz, nexch, *refs):
    line, rows_first, moved_first, slot_in, sent, spread, raw, extra, other, moved, top = refs[:11]
    rows, rows0, moved0, slot, made, small, fetch_sem, small_sem = refs[11:19]
    ex = RowExchange(ny, sent, spread, rows, moved, refs[19 : 19 + nexch])
    (azs, azr, bzs, bzr, bxs, bxr, ss, sr, ts, tr, to_s, to_r, own) = refs[19 + nexch :]
    total = rows0.shape[0]
    pcol = lax.axis_index("pcol")
    n = nz * NX
    z, x = lax.div(pcol, NX), lax.rem(pcol, NX)

    def to_x(i):
        return {"pcol": z * NX + i}

    def to_z(i):
        return {"pcol": i * NX + x}

    near = ex.barrier_peers()
    near += [to_x(lax.rem(x + d, NX)) for d in (1, NX - 1)]
    near += [to_z(lax.rem(z + d, nz)) for d in range(1, nz)]

    def place(start, size):
        keys = slot[pl.ds(pl.multiple_of(start, HALF), size), :]
        return jnp.where(
            keys == lax.broadcasted_iota(jnp.int32, (size, total), 1), 1.0, 0.0
        ).astype(jnp.bfloat16)

    def place_rows(source, cols):
        def chunk(i, _):
            here = pl.ds(pl.multiple_of(i * HALF, HALF), HALF)
            top[here, cols] = bdot(place(i * HALF, HALF), source())
            return 0

        lax.fori_loop(0, 2 * NB // HALF, chunk, 0)

    def meanwhile():
        fetches = [
            pltpu.make_async_copy(src, dst, fetch_sem.at[k])
            for k, (src, dst) in enumerate(((slot_in, slot), (moved_first, moved0), (rows_first, rows0)))
        ]
        for copy in fetches:
            copy.start()
        for copy in fetches:
            copy.wait()
        first = jnp.where(pcol == 0, NB, 0) + ex.c * HALF
        part = bdot(place(first, HALF), rows0[...])
        last = made.shape[1] - HALF - MOVED
        for k in range(NX):
            lanes = slice(k * LANES, (k + 1) * LANES)
            made[k, pl.ds(0, HALF), :] = part[:, lanes]
            made[k, pl.ds(HALF, MOVED), :] = moved0[:, lanes]
            made[k, pl.ds(HALF + MOVED, last), :] = jnp.zeros((last, LANES), jnp.bfloat16)
        place_rows(lambda: rows0[...], pl.ds(0, NB))
        handover = pltpu.make_async_copy(made, small, small_sem)
        handover.start()
        handover.wait()

    meet_with_roots(near, pcol, n, meanwhile)

    def across(index, way, hop, half):
        s, r = (ts.at[way, hop - 1, half], tr.at[way, hop - 1, half]) if hop else (to_s.at[half], to_r.at[half])
        return pltpu.make_async_remote_copy(
            src_ref=extra.at[half, index, pl.ds(0, HALF)], dst_ref=other.at[half, index],
            send_sem=s, recv_sem=r, device_id=ex.partner, device_id_type=MESH)

    crossing = []

    def cross(index, ref, way, hop, half):
        copy = across(index, way, hop, half)
        copy.start()
        crossing.append(copy)

    def band(i):
        return pl.ds(pl.multiple_of(i * PB, PB), PB)

    scatter = Scatter(
        pcol, n,
        lambda to: small.at[lax.rem(to, NX), band(lax.div(to, NX))],
        lambda panel, to: extra.at[panel, lax.rem(to, NX), band(lax.div(to, NX))], ss, sr)
    az = Ring(nz, z, to_z, lambda i, h: raw.at[h, i], azs, azr, fresh=lambda h: line.at[h])
    bz = Direct(nz, z, to_z, lambda i, h: extra.at[h, x, band(i)], bzs, bzr)
    bx = Ring(NX, x, to_x, lambda i, h: extra.at[h, i], bxs, bxr, arrived=cross)
    keep = [pltpu.make_async_copy(line.at[h], raw.at[h, z], own.at[h]) for h in (0, 1)]

    def begin_az():
        for half in (0, 1):
            az.start(half)
        for copy in keep:
            copy.start()

    def begin_bz():
        for half in (0, 1):
            scatter.landed(half)
            bz.start_half(half)

    def begin_bx(half):
        bz.wait(half)
        bx.start(half)
        cross(x, None, 0, 0, half)

    events = [(-2.0, scatter.start), (-0.9, begin_az)]
    events += ex.events(T_Y)
    events += az.events([T_A0, T_A1], T_AD)
    events += [(T_BZ, begin_bz)]
    events += [(T_BX + h * 0.4, lambda h=h: begin_bx(h)) for h in (0, 1)]
    events += bx.events([T_BX + 0.2, T_BX + 1.2], T_BXD)

    def last_rows():
        ex.finish()
        place_rows(lambda: rows[...].reshape(total, NB), pl.ds(NB, NB))

    events += [(T_TOP, last_rows)]
    run_events(events)
    for ring in (az, bx):
        for half in (0, 1):
            ring.complete(half)
        ring.drain()
    bz.drain()
    scatter.drain()
    for copy in crossing:
        copy.wait()
    for copy in keep:
        copy.wait()


def second_exchange(line, rows0, moved0, slot, sent, spread, ny, nz, cid):
    width = sent.shape[-1]
    dma = pltpu.SemaphoreType.DMA
    sems = exchange_sems(ny)
    zring, xring, zdirect = dma((2, nz // 2, 2)), dma((2, NX // 2, 2)), dma((nz, 2))
    return pl.pallas_call(
        lambda *refs: second_kernel(ny, nz, len(sems), *refs),
        out_shape=(
            jax.ShapeDtypeStruct((2, nz, NX, PA, NB), jnp.bfloat16),
            jax.ShapeDtypeStruct((2, NX, nz * PB, LANES), jnp.bfloat16),
            jax.ShapeDtypeStruct((2, NX, HALF, LANES), jnp.bfloat16),
            jax.ShapeDtypeStruct((CORES, DCAP, width), jnp.bfloat16),
            jax.ShapeDtypeStruct((2 * NB, 2 * width), jnp.bfloat16),
        ),
        in_specs=[ANY] * 6,
        out_specs=(ANY,) * 4 + (pl.BlockSpec(memory_space=pltpu.VMEM),),
        scratch_shapes=[
            pltpu.VMEM((ny * CORES, 2, CAP // 2, width), jnp.bfloat16),
            pltpu.VMEM(rows0.shape, jnp.bfloat16),
            pltpu.VMEM(moved0.shape, jnp.bfloat16),
            pltpu.VMEM(slot.shape, jnp.int32),
            pltpu.VMEM((NX, nz * PB, LANES), jnp.bfloat16),
            pltpu.VMEM((NX, nz * PB, LANES), jnp.bfloat16),
            dma((3,)),
            dma,
        ]
        + sems
        + [zring, zring, zdirect, zdirect, xring, xring]
        + [dma((nz * NX,)), dma((2,)), xring, xring, dma((2,)), dma((2,)), dma((2,))],
        compiler_params=pltpu.CompilerParams(collective_id=cid, has_side_effects=True),
        name="second_exchange",
    )(line, rows0, moved0, slot, sent, spread)


def dot(a, b):
    return jnp.dot(a, b, preferred_element_type=jnp.float32)


def bdot(a, b):
    return dot(a, b).astype(jnp.bfloat16)


def ids(shape, axis):
    return lax.broadcasted_iota(jnp.int32, shape, axis).astype(jnp.float32)


def to_row(col):
    n = col.shape[0]
    return jnp.sum(jnp.where(ids((n, n), 0) == ids((n, n), 1), col, 0.0), axis=0, keepdims=True)


def to_col(row):
    n = row.shape[1]
    return jnp.sum(jnp.where(ids((n, n), 0) == ids((n, n), 1), row, 0.0), axis=1, keepdims=True)


def along(table):
    return jnp.sum(table, axis=1, keepdims=True)


def down(table):
    return jnp.sum(table, axis=0, keepdims=True)


def hot(mask):
    return jnp.where(mask, 1.0, 0.0).astype(jnp.bfloat16)


def index_kernel(nprow, piv, tile, sent0, sent1, spread0, spread1, slot_out, into_out, rounds_out):
    prow = lax.axis_index("prow")
    core = lax.rem(prow, CORES).astype(jnp.float32)
    prow_f = prow.astype(jnp.float32)
    rows = [piv[k : k + 1, :].astype(jnp.float32) for k in (0, 1)]
    cols = [to_col(r) for r in rows]
    i0, i1 = ids((NB, NB), 0), ids((NB, NB), 1)
    receive = []
    for k in (0, 1):
        first = float(k * NB)
        top_c, top_r = ids((NB, 1), 0) + first, ids((1, NB), 1) + first
        left_c = 1.0 - along(jnp.where(rows[k] == top_c, 1.0, 0.0))
        left_r = 1.0 - down(jnp.where(cols[k] == top_r, 1.0, 0.0))
        rank_r = down(jnp.where(i0 < i1, left_c, 0.0))
        vac_r = jnp.where(rows[k] >= first + NB, 1.0, 0.0)
        vac_c = along(jnp.where(i1 < i0, vac_r, 0.0))
        receive.append(along(jnp.where((rank_r == vac_c) & (left_r > 0.5), top_r, 0.0)))
    receive0_r = to_row(receive[0])

    def lookup(keys):
        hit = keys == rows[0]
        found = along(jnp.where(hit, 1.0, 0.0))
        return jnp.where(found > 0.5, along(jnp.where(hit, receive0_r, 0.0)), keys)

    src1, from1 = lookup(cols[1]), lookup(receive[1])
    again = along(jnp.where(cols[0] == rows[1], 1.0, 0.0))

    def owner(v):
        return (lax.shift_right_logical(v.astype(jnp.int32), 9) & (nprow - 1)).astype(jnp.float32)

    def local(v):
        v = v.astype(jnp.int32)
        return (lax.shift_right_logical(v, 13) * NB + (v & (NB - 1))).astype(jnp.float32)

    n = 2 * NB
    t_c = jnp.concatenate([cols[0], src1], axis=0)
    d_dst = jnp.concatenate([cols[0], cols[1]], axis=0)
    d_src = jnp.concatenate([receive[0], from1], axis=0)
    fresh = jnp.concatenate([again, jnp.zeros_like(again)], axis=0)
    valid = (d_dst >= 2.0 * NB) & (fresh < 0.5)
    t_group = owner(t_c)
    group = jnp.where(valid, owner(d_dst) * CORES + jnp.where(d_src >= NB, 1.0, 0.0), -1000.0)
    lanes = ids((n, 128), 1)
    members = jnp.where((lanes == t_group) | (lanes == group + nprow), 1.0, 0.0)
    before = dot(hot(ids((n, n), 1) < ids((n, n), 0)), members.astype(jnp.bfloat16)) * members
    is_t = lanes < nprow
    t_rank = along(jnp.where(is_t, before, 0.0))
    d_rank = along(jnp.where(is_t, 0.0, before))
    slot_c = jnp.where(t_rank < CAP, t_group * CAP + t_rank, -1.0)
    key_c = jnp.where(valid & (d_rank < DCAP), group * DCAP + d_rank, -1.0)
    slot_out[...] = slot_c.astype(jnp.int32)
    packed = jnp.where(lanes == 0, slot_c, jnp.where(lanes == 1, local(t_c), jnp.where(lanes == 2, key_c, d_src)))
    packed = packed.T
    slot_r, local_r, key_r, src_r = (packed[k : k + 1, :] for k in range(4))
    mine = ids((CAP, 1), 0) + prow_f * CAP
    pick = along(jnp.where(slot_r == mine, local_r + 1.0, 0.0)) - 1.0
    sent = bdot(hot(pick == ids((CAP, n), 1)), tile[...])
    sent0[...] = sent[:, :NB]
    sent1[...] = sent[:, NB:]
    lane = ids((1, 128), 1)
    wanted = jnp.where(lane < MOVED, lane + prow_f * MOVED, -2.0)
    into = down(jnp.where(key_c == wanted, local(d_dst) + 1.0, 0.0)) - 1.0
    into_out[...] = into.astype(jnp.int32)
    most_t = jnp.max(t_rank) * (1.0 / CAP)
    most_d = jnp.max(jnp.where(valid, d_rank, 0.0)) * (1.0 / DCAP)
    rounds_out[0, 0] = jnp.where(jnp.maximum(most_t, most_d) > 1.0 - 0.25 / CAP, 2, 1).astype(jnp.int32)

    @pl.when(prow < CORES)
    def _():
        s = ids((MOVED, 1), 0)

        def one_chip(q, _):
            second = jnp.where(s >= DCAP, 1.0, 0.0)
            want = (2.0 * q.astype(jnp.float32) + second) * MOVED + core * DCAP + s - second * DCAP
            src = along(jnp.where(key_r == want, src_r + 1.0, 0.0)) - 1.0 - core * NB
            out = bdot(hot(src == ids((MOVED, NB), 1)), tile[:NB, :])
            here = pl.ds(pl.multiple_of(q * MOVED, MOVED), MOVED)
            spread0[here, :] = out[:, :NB]
            spread1[here, :] = out[:, NB:]
            return 0

        lax.fori_loop(0, nprow // 2, one_chip, 0)


def index_and_pack(pivots, tile, nprow):
    n = 2 * NB
    bf16 = jnp.bfloat16
    vmem = pl.BlockSpec(memory_space=pltpu.VMEM)
    return pl.pallas_call(
        lambda *refs: index_kernel(nprow, *refs),
        out_shape=(
            jax.ShapeDtypeStruct((CAP, NB), bf16), jax.ShapeDtypeStruct((CAP, NB), bf16),
            jax.ShapeDtypeStruct((nprow * DCAP, NB), bf16), jax.ShapeDtypeStruct((nprow * DCAP, NB), bf16),
            jax.ShapeDtypeStruct((n, 1), jnp.int32), jax.ShapeDtypeStruct((1, 128), jnp.int32),
            jax.ShapeDtypeStruct((1, 1), jnp.int32),
        ),
        in_specs=[vmem, vmem],
        out_specs=(vmem,) * 6 + (pl.BlockSpec(memory_space=pltpu.SMEM),),
        name="index_and_pack",
    )(pivots, tile)


def update_kernel(into, *refs):
    sources, out, held = refs[:9], refs[9], refs[10:19]
    low, up0, up1, sem = refs[19:]
    fetches = [pltpu.make_async_copy(src, dst, sem.at[k]) for k, (src, dst) in enumerate(zip(sources, held))]
    for copy in fetches:
        copy.start()
    low_inv, up_inv, top, extra, other, moved0, moved1, raw, tile = held
    pcol, prow = lax.axis_index("pcol"), lax.axis_index("prow")
    core = lax.rem(prow, CORES)
    f32 = jnp.float32
    step = NB // 2
    halves = (pl.ds(0, NB), pl.ds(NB, NB))

    def spot(i):
        return pl.ds(pl.multiple_of(i * step, step), step)

    for copy in fetches[:5]:
        copy.wait()
    l0, l1, u0, u1 = low_inv[0], low_inv[1], up_inv[0], up_inv[1]
    panel_tops = []
    for k in (0, 1):
        own = jnp.concatenate([extra[k, x, :HALF, :] for x in range(NX)], axis=1)
        far = jnp.concatenate([other[k, x] for x in range(NX)], axis=1)
        panel_tops.append(jnp.concatenate(
            [jnp.where(core == 0, own, far), jnp.where(core == 0, far, own)], axis=0))
    corner = bdot(panel_tops[0], u0)
    upper = bdot(l0, panel_tops[1])
    moved_panel = [
        jnp.concatenate([extra[k, x, HALF : HALF + MOVED, :] for x in range(NX)], axis=1) for k in (0, 1)
    ]
    for cols in halves:
        up0[:, cols] = bdot(l0, top[pl.ds(0, NB), cols])
        low[:, cols] = (top[pl.ds(NB, NB), cols].astype(f32) - dot(corner, up0[:, cols])).astype(jnp.bfloat16)
        up1[:, cols] = bdot(l1, low[:, cols])
    for copy in fetches[5:]:
        copy.wait()

    def update(i, _):
        here = spot(i)
        ids_c = lax.broadcasted_iota(jnp.int32, (step, MOVED), 0) + i * step
        match = jnp.where(ids_c == into[:, :MOVED], 1.0, 0.0)
        hit = jnp.max(match, axis=1, keepdims=True) > 0.5
        insert = match.astype(jnp.bfloat16)

        def with_moved(new, old):
            return jnp.where(hit, dot(insert, new), old.astype(f32)).astype(jnp.bfloat16)

        factor0 = bdot(with_moved(moved_panel[0], raw[0, here, :]), u0)
        panel1 = (with_moved(moved_panel[1], raw[1, here, :]).astype(f32) - dot(factor0, upper)).astype(jnp.bfloat16)
        factor1 = bdot(panel1, u1)
        for d, (cols, moved) in enumerate(zip(halves, (moved0, moved1))):
            new = with_moved(moved[...], tile[here, cols]).astype(f32)
            new = (new - dot(factor0, up0[:, cols])).astype(jnp.bfloat16).astype(f32)
            new = (new - dot(factor1, up1[:, cols])).astype(jnp.bfloat16)
            if d == 0:
                new = jnp.where(pcol == 0, factor0, jnp.where(pcol == 1, factor1, new))
            out[here, cols] = new
        return 0

    lax.fori_loop(0, 4, update, 0)
    heads = pl.ds(0, NB)

    @pl.when(prow == 0)
    def _():
        out[heads, halves[0]] = jnp.where(pcol == 0, top[heads, halves[0]], up0[:, halves[0]])
        out[heads, halves[1]] = up0[:, halves[1]]

    @pl.when(prow == 1)
    def _():
        out[heads, halves[0]] = jnp.where(
            pcol == 0, corner, jnp.where(pcol == 1, low[:, halves[0]], up1[:, halves[0]]))
        out[heads, halves[1]] = up1[:, halves[1]]


def update(into, *args):
    n = 2 * NB
    vmem = pl.BlockSpec(memory_space=pltpu.VMEM)
    bf16 = jnp.bfloat16
    return pl.pallas_call(
        update_kernel,
        out_shape=jax.ShapeDtypeStruct((n, n), bf16),
        in_specs=[vmem] + [ANY] * len(args),
        out_specs=vmem,
        scratch_shapes=[pltpu.VMEM(a.shape, bf16) for a in args]
        + [pltpu.VMEM((NB, n), bf16)] * 3 + [pltpu.SemaphoreType.DMA((len(args),))],
        name="update",
    )(into, *args)


def count_before(flags):
    n = flags.shape[0]
    ahead = jnp.arange(n)[None, :] < jnp.arange(n)[:, None]
    return jnp.sum((ahead & flags[None, :]).astype(jnp.int32), axis=1)


def pairing(sources, first_row):
    top_ids = first_row + jnp.arange(NB, dtype=jnp.int32)
    leftover = jnp.logical_not(jnp.any(sources[None, :] == top_ids[:, None], axis=1))
    left_rank = count_before(leftover)
    vacated = sources >= first_row + NB
    vac_rank = count_before(vacated)
    table = leftover[None, :] & (left_rank[None, :] == vac_rank[:, None])
    return jnp.sum(jnp.where(table, top_ids[None, :], 0), axis=1)


def lookup(keys, names, values):
    hit = keys[:, None] == names[None, :]
    found = jnp.sum(jnp.where(hit, values[None, :], 0), axis=1)
    return jnp.where(jnp.any(hit, axis=1), found, keys)


def rank_in(group):
    n = group.shape[0]
    ahead = jnp.arange(n)[None, :] < jnp.arange(n)[:, None]
    same = group[None, :] == group[:, None]
    return jnp.sum((same & ahead).astype(jnp.int32), axis=1)


def slot_values(keys, values, wanted):
    hit = wanted[:, None] == keys[None, :]
    return jnp.sum(jnp.where(hit, values[None, :] + 1, 0), axis=1) - 1


def one_hot(index, n):
    return (index[:, None] == jnp.arange(n, dtype=jnp.int32)[None, :]).astype(jnp.bfloat16)


def collect_rounds(tile, pivots, nprow, ny):
    prow = lax.axis_index("prow")
    core = lax.rem(prow, CORES)
    s0, s1 = pivots[0], pivots[1]
    receive0, receive1 = pairing(s0, 0), pairing(s1, NB)
    src1 = lookup(s1, s0, receive0)
    from1 = lookup(receive1, s0, receive0)
    again = jnp.any(s0[:, None] == s1[None, :], axis=1)
    big = jnp.int32(1 << 20)

    def owner(rows):
        return lax.rem(rows // NB, nprow)

    def local(rows):
        return rows // (NB * nprow) * NB + lax.rem(rows, NB)

    t_src = jnp.concatenate([s0, src1])
    t_owner = owner(t_src)
    t_rank = rank_in(t_owner)
    t_local = local(t_src)
    d_dst = jnp.concatenate([s0, s1])
    d_src = jnp.concatenate([receive0, from1])
    d_valid = (d_dst >= 2 * NB) & jnp.concatenate([jnp.logical_not(again), jnp.ones((NB,), jnp.bool_)])
    d_core = d_src // NB
    d_owner = owner(d_dst)
    d_rank = rank_in(jnp.where(d_valid, d_owner * CORES + d_core, -1))
    d_local = local(d_dst)
    rounds = jnp.maximum(jnp.max(t_rank) // CAP, jnp.max(jnp.where(d_valid, d_rank, 0)) // DCAP) + 1

    def body(state):
        r, top, now = state
        t_in = (t_rank // CAP) == r
        t_slot = t_owner * CAP + lax.rem(t_rank, CAP)
        t_key = jnp.where(t_in, t_slot, big)
        d_in = d_valid & ((d_rank // DCAP) == r)
        d_key = jnp.where(d_in, (d_owner * CORES + d_core) * DCAP + lax.rem(d_rank, DCAP), big)
        pick = one_hot(slot_values(t_key, t_local, prow * CAP + jnp.arange(CAP, dtype=jnp.int32)), 2 * NB)
        every = jnp.arange(nprow * DCAP, dtype=jnp.int32)
        wanted = (every // DCAP * CORES + core) * DCAP + lax.rem(every, DCAP)
        spread_sel = one_hot(slot_values(d_key, d_src - core * NB, wanted), NB)
        mine = prow * MOVED + jnp.arange(MOVED, dtype=jnp.int32)
        into = slot_values(d_key, d_local, mine)
        insert = (jnp.arange(2 * NB, dtype=jnp.int32)[:, None] == into[None, :]).astype(jnp.bfloat16)
        rows, moved = row_exchange(
            bdot(pick, tile).reshape(2, CAP // 2, 2 * NB),
            bdot(spread_sel, tile[:NB]).reshape(nprow, DCAP, 2 * NB), ny, 1)
        place = one_hot(jnp.where(t_in, t_slot, -1), nprow * CAP)
        top = top + bdot(place, rows.reshape(nprow * CAP, 2 * NB))
        new = bdot(insert, moved.reshape(MOVED, 2 * NB))
        return r + 1, top, jnp.where(jnp.any(insert > 0, axis=1)[:, None], new, now)

    _, top, now = lax.while_loop(
        lambda s: s[0] < rounds, body, (jnp.int32(0), jnp.zeros_like(tile), tile))
    return top, now


def per_device(matrix, pivots, lower_inverse, upper_inverse):
    nprow, npcol = lax.axis_size("prow"), lax.axis_size("pcol")
    ny, nz = nprow // CORES, npcol // NX
    n = 2 * NB
    tile = matrix.reshape(n, n)
    *packed, slot, into, rounds = index_and_pack(pivots, tile, nprow)

    def finish(tile, packed, slot, into, known, cids):
        sents = [v.reshape(2, CAP // 2, NB) for v in packed[:2]]
        spreads = [v.reshape(nprow, DCAP, NB) for v in packed[2:]]
        line, rows0, moved0 = first_exchange(tile, sents[0], spreads[0], ny, nz, cids[0])
        rows0, moved0 = rows0.reshape(nprow * CAP, NB), moved0.reshape(MOVED, NB)
        if known is not None:
            rows0, moved0 = jnp.pad(known[:, :NB], ((0, nprow * CAP - n), (0, 0))), jnp.zeros_like(moved0)
        raw, extra, other, moved1, top = second_exchange(
            line, rows0, moved0, slot, sents[1], spreads[1], ny, nz, cids[1])
        moved1 = moved1.reshape(MOVED, NB)
        if known is not None:
            moved1, top = jnp.zeros_like(moved1), known
        return update(
            into, lower_inverse, upper_inverse, top, extra, other, moved0, moved1, raw.reshape(2, n, NB), tile)

    def one_round(tile):
        return finish(tile, packed, slot, into, None, (0, 2))

    def many_rounds(tile):
        top, now = collect_rounds(tile, pivots, nprow, ny)
        empty = [jnp.zeros_like(v) for v in packed]
        order = jnp.arange(n, dtype=jnp.int32)[:, None]
        return finish(now, empty, order, jnp.full_like(into, -1), top, (3, 4))

    out = lax.cond(rounds[0, 0] > 1, many_rounds, one_round, tile)
    return out.reshape(matrix.shape)


def solution(mesh):
    return jax.shard_map(
        per_device,
        mesh=mesh,
        in_specs=(P(None, "prow", None, None, "pcol", None), P(), P(), P()),
        out_specs=P(None, "prow", None, None, "pcol", None),
        check_vma=False,
    )
```

```python
import jax
import jax.numpy as jnp
from jax import lax
from jax.experimental import pallas as pl
from jax.experimental.pallas import tpu as pltpu
from jax.sharding import PartitionSpec as P

NB = 512
CORES = 2
NX = 4
CAP = 96
DCAP = 56
MOVED = CORES * DCAP
HALF = NB // CORES
LANES = NB // NX
PA = 32
PB = 48
MESH = pl.DeviceIdType.MESH
T_Y, T_A0, T_A1, T_AD, T_BZ, T_BX, T_BXD, T_TOP, T_PLACE = 4.5, 0.0, 2.5, 5.8, 3.5, 11.0, 4.0, 20.5, 0.3
T_PASS, T_LINE = 13.0, 16.5
ANY = pl.BlockSpec(memory_space=pl.ANY)


class Ring:
    def __init__(self, n, pos, goto, item, send, recv, fresh=None, arrived=None, first=1):
        self.first = first
        self.n, self.pos, self.goto, self.item = n, pos, goto, item
        self.send, self.recv = send, recv
        self.fresh, self.arrived = fresh, arrived
        self.got = [0, 0]

    def carries(self, way, hop, half):
        return hop < self.n // 2 or (hop == self.n // 2 and half == way)

    def copy(self, way, hop, half):
        step = 1 if way == 0 else -1
        index = lax.rem(self.pos + self.n - step * (hop - 1), self.n)
        target = lax.rem(self.pos + self.n + step, self.n)
        src = self.item(index, half)
        if hop == self.first and self.fresh is not None:
            src = self.fresh(way, half)
        return pltpu.make_async_remote_copy(
            src_ref=src,
            dst_ref=self.item(index, half),
            send_sem=self.send.at[way, hop - 1, half],
            recv_sem=self.recv.at[way, hop - 1, half],
            device_id=self.goto(target),
            device_id_type=MESH,
        )

    def landed(self, way, hop, half):
        step = 1 if way == 0 else -1
        index = lax.rem(self.pos + self.n - step * hop, self.n)
        ref = self.item(index, half)
        return index, ref, pltpu.make_async_remote_copy(
            src_ref=ref,
            dst_ref=ref,
            send_sem=self.send.at[way, hop - 1, half],
            recv_sem=self.recv.at[way, hop - 1, half],
            device_id=self.goto(lax.rem(self.pos + 1, self.n)),
            device_id_type=MESH,
        )

    def start(self, half):
        for way in (0, 1):
            self.copy(way, self.first, half).start()

    def step(self, way, hop, half):
        index, ref, arrival = self.landed(way, hop, half)
        arrival.wait_recv()
        if self.carries(way, hop + 1, half):
            self.copy(way, hop + 1, half).start()
        self.got[half] += 1
        if self.arrived is not None:
            self.arrived(index, ref, way, hop, half)

    def events(self, t0, dt):
        out = []
        for half in (0, 1):
            for hop in range(self.first, self.n // 2 + 1):
                for way in (0, 1):
                    if self.carries(way, hop, half):
                        when = t0[half] + dt * (hop - self.first + 1)
                        out.append((when, lambda w=way, h=hop, f=half: self.step(w, h, f)))
        return out

    def complete(self, half):
        assert self.got[half] == self.n + 1 - 2 * self.first

    def drain(self):
        for half in (0, 1):
            for hop in range(self.first, self.n // 2 + 1):
                for way in (0, 1):
                    if self.carries(way, hop, half):
                        self.copy(way, hop, half).wait_send()


def run_events(events):
    for _, act in sorted(events, key=lambda e: e[0]):
        act()


class RowExchange:
    def __init__(self, ny, sent, spread, rows, moved, sems):
        self.ny, self.sent, self.spread, self.rows, self.moved = ny, sent, spread, rows, moved
        (self.rs, self.rr, self.fs, self.fr, self.os, self.orr, self.ls, self.es, self.er) = sems
        prow = lax.axis_index("prow")
        self.y, self.c = lax.div(prow, CORES), lax.rem(prow, CORES)
        self.partner = {"prow": self.y * CORES + 1 - self.c}
        self.ring = Ring(
            ny, self.y,
            lambda i: {"prow": i * CORES + self.c},
            lambda i, half: rows.at[i * CORES + self.c, half],
            self.rs, self.rr,
            fresh=lambda way, half: sent.at[half],
            arrived=self.forward,
        )
        self.forwards = []

    def barrier_peers(self):
        ids = [{"prow": lax.rem(self.y + k, self.ny) * CORES + c} for k in range(1, self.ny) for c in (0, 1)]
        return ids + [self.partner]

    def forward_copy(self, index, way, hop, half):
        return pltpu.make_async_remote_copy(
            src_ref=self.rows.at[index * CORES + self.c, half],
            dst_ref=self.rows.at[index * CORES + self.c, half],
            send_sem=self.fs.at[way, hop - 1, half],
            recv_sem=self.fr.at[way, hop - 1, half],
            device_id=self.partner,
            device_id_type=MESH,
        )

    def forward(self, index, ref, way, hop, half):
        copy = self.forward_copy(index, way, hop, half)
        copy.start()
        self.forwards.append((copy, index, way, hop, half))

    def own_copies(self):
        mine = self.rows.at[self.y * CORES + self.c]
        local = pltpu.make_async_copy(self.sent, mine, self.ls.at[0])
        across = pltpu.make_async_remote_copy(
            src_ref=self.sent, dst_ref=mine, send_sem=self.os, recv_sem=self.orr,
            device_id=self.partner, device_id_type=MESH,
        )
        return local, across

    def spread_copy(self, k, core):
        to = lax.rem(self.y + k, self.ny) * CORES + core
        return pltpu.make_async_remote_copy(
            src_ref=self.spread.at[to], dst_ref=self.moved.at[self.c],
            send_sem=self.es.at[k, core], recv_sem=self.er.at[self.c],
            device_id={"prow": to}, device_id_type=MESH,
        )

    def spread_partner(self):
        to = 1 - self.c
        return pltpu.make_async_remote_copy(
            src_ref=self.spread.at[to], dst_ref=self.moved.at[self.c],
            send_sem=self.es.at[0, 0], recv_sem=self.er.at[self.c],
            device_id=self.partner, device_id_type=MESH,
        )

    def spread_own(self):
        return pltpu.make_async_copy(self.spread.at[self.c], self.moved.at[self.c], self.er.at[self.c])

    def begin(self):
        for half in (0, 1):
            self.ring.start(half)
        for copy in self.own_copies():
            copy.start()

    def spread_some(self, ks):
        @pl.when(self.y == 0)
        def _():
            for k in ks:
                for core in (0, 1):
                    self.spread_copy(k, core).start()

    def spread_near(self):
        @pl.when(self.y == 0)
        def _():
            self.spread_partner().start()
            self.spread_own().start()

    def events(self, dt):
        half_n = self.ny // 2
        out = [(-1.0, self.begin), (3.9 * dt, self.spread_near)]
        order = [half_n] + [k for d in range(half_n - 1, 0, -1) for k in (d, self.ny - d)]
        for i, k in enumerate(order):
            out.append((0.1 + i * 0.5 * dt, lambda k=k: self.spread_some([k])))
        return out + self.ring.events([0.0, 0.3 * dt], dt)

    def finish(self):
        local, across = self.own_copies()
        local.wait()
        across.wait()
        self.ring.drain()
        for copy, index, way, hop, half in self.forwards:
            copy.wait_send()
        for copy, index, way, hop, half in self.forwards:
            ref = self.rows.at[index * CORES + 1 - self.c, half]
            pltpu.make_async_remote_copy(
                src_ref=ref, dst_ref=ref,
                send_sem=self.fs.at[way, hop - 1, half], recv_sem=self.fr.at[way, hop - 1, half],
                device_id=self.partner, device_id_type=MESH,
            ).wait_recv()
        for core in (0, 1):
            ref = self.moved.at[core]
            pltpu.make_async_copy(ref, ref, self.er.at[core]).wait()

        @pl.when(self.y == 0)
        def _():
            for k in range(1, self.ny):
                for core in (0, 1):
                    self.spread_copy(k, core).wait_send()
            self.spread_partner().wait_send()


def exchange_sems(ny):
    dma = pltpu.SemaphoreType.DMA
    return [
        dma((2, ny // 2, 2)), dma((2, ny // 2, 2)),
        dma((2, ny // 2, 2)), dma((2, ny // 2, 2)),
        dma, dma, dma((1,)), dma((ny, CORES)), dma((CORES,)),
    ]


def meet(peers):
    barrier = pltpu.get_barrier_semaphore()
    for peer in peers:
        pl.semaphore_signal(barrier, inc=1, device_id=peer, device_id_type=MESH)
    pl.semaphore_wait(barrier, len(peers))


def exchange_kernel(ny, sent, spread, rows, moved, *sems):
    ex = RowExchange(ny, sent, spread, rows, moved, sems)
    meet(ex.barrier_peers())
    run_events(ex.events(3.8))
    ex.finish()


def row_exchange(sent, spread, ny, cid):
    width = sent.shape[-1]
    return pl.pallas_call(
        lambda *refs: exchange_kernel(ny, *refs),
        out_shape=(
            jax.ShapeDtypeStruct((ny * CORES, 2, CAP // 2, width), jnp.bfloat16),
            jax.ShapeDtypeStruct((CORES, DCAP, width), jnp.bfloat16),
        ),
        in_specs=[ANY, ANY],
        out_specs=(ANY, ANY),
        scratch_shapes=exchange_sems(ny),
        compiler_params=pltpu.CompilerParams(collective_id=cid, has_side_effects=True),
        name="row_exchange",
    )(sent, spread)


def meet_with_roots(near, pcol, n, meanwhile=None):
    barrier = pltpu.get_barrier_semaphore()

    def signal(peer):
        pl.semaphore_signal(barrier, inc=1, device_id=peer, device_id_type=MESH)

    for root in (0, 1):
        @pl.when(pcol == root)
        def _():
            for k in range(1, n):
                signal({"pcol": lax.rem(pcol + k, n)})

        @pl.when(pcol != root)
        def _():
            signal({"pcol": root})

    for peer in near:
        signal(peer)
    if meanwhile is not None:
        meanwhile()

    @pl.when(pcol < 2)
    def _():
        pl.semaphore_wait(barrier, len(near) + n)

    @pl.when(pcol >= 2)
    def _():
        pl.semaphore_wait(barrier, len(near) + 2)


class Scatter:
    def __init__(self, pcol, n, piece, slot, send, recv):
        self.pcol, self.n, self.piece, self.slot, self.send, self.recv = pcol, n, piece, slot, send, recv

    def copy(self, k):
        to = lax.rem(self.pcol + k, self.n)
        return pltpu.make_async_remote_copy(
            src_ref=self.piece(to), dst_ref=self.slot(self.pcol, to),
            send_sem=self.send.at[k], recv_sem=self.recv.at[self.pcol],
            device_id={"pcol": to}, device_id_type=MESH)

    def start(self):
        @pl.when(self.pcol < 2)
        def _():
            for k in range(1, self.n):
                self.copy(k).start()
            pltpu.make_async_copy(
                self.piece(self.pcol), self.slot(self.pcol, self.pcol), self.recv.at[self.pcol]
            ).start()

    def landed(self, panel):
        ref = self.slot(panel, self.pcol)
        pltpu.make_async_copy(ref, ref, self.recv.at[panel]).wait()

    def drain(self):
        @pl.when(self.pcol < 2)
        def _():
            for k in range(1, self.n):
                self.copy(k).wait_send()


class Direct:
    def __init__(self, n, pos, goto, item, send, recv):
        self.n, self.pos, self.goto, self.item, self.send, self.recv = n, pos, goto, item, send, recv

    def copy(self, k, half):
        to = lax.rem(self.pos + k, self.n)
        return pltpu.make_async_remote_copy(
            src_ref=self.item(self.pos, half), dst_ref=self.item(self.pos, half),
            send_sem=self.send.at[k, half], recv_sem=self.recv.at[k, half],
            device_id=self.goto(to), device_id_type=MESH)

    def start(self):
        for half in (0, 1):
            self.start_half(half)

    def start_half(self, half):
        for k in sorted(range(1, self.n), key=lambda k: -min(k, self.n - k)):
            self.copy(k, half).start()

    def wait(self, half):
        for k in range(1, self.n):
            ref = self.item(lax.rem(self.pos + self.n - k, self.n), half)
            pltpu.make_async_copy(ref, ref, self.recv.at[k, half]).wait()

    def drain(self):
        for half in (0, 1):
            for k in range(1, self.n):
                self.copy(k, half).wait_send()


def first_kernel(ny, nz, nexch, *refs):
    tile, sent, spread, line, beside, rows, moved = refs[:7]
    ex = RowExchange(ny, sent, spread, rows, moved, refs[7 : 7 + nexch])
    ss, sr, xs, xr, zs, zr = refs[7 + nexch :]
    pcol = lax.axis_index("pcol")
    n = nz * NX
    z, x = lax.div(pcol, NX), lax.rem(pcol, NX)
    scatter = Scatter(
        pcol, n,
        lambda to: tile.at[pl.ds(pl.multiple_of(to * PA, PA), PA), pl.ds(0, NB)],
        lambda panel, to: line.at[panel, lax.rem(to, NX)], ss, sr)
    gather = Direct(NX, x, lambda i: {"pcol": z * NX + i}, lambda i, h: line.at[h, i], xs, xr)
    near = ex.barrier_peers() + [{"pcol": z * NX + lax.rem(x + d, NX)} for d in range(1, NX)]
    around = [{"pcol": lax.rem(z + d, nz) * NX + x} for d in (1, nz - 1)]
    near += around

    def next_line(way, half):
        return pltpu.make_async_remote_copy(
            src_ref=line.at[half], dst_ref=beside.at[way, half],
            send_sem=zs.at[way, half], recv_sem=zr.at[way, half],
            device_id=around[way], device_id_type=MESH)

    def send_lines():
        for half in (0, 1):
            gather.wait(half)
            for way in (0, 1):
                next_line(way, half).start()

    meet_with_roots(near, pcol, n)

    def pass_on():
        for panel in (0, 1):
            scatter.landed(panel)
            gather.start_half(panel)

    run_events(ex.events(3.8) + [(-0.5, scatter.start), (T_PASS, pass_on), (T_LINE, send_lines)])
    ex.finish()
    for half in (0, 1):
        for way in (0, 1):
            next_line(way, half).wait()
    gather.drain()
    scatter.drain()


def first_exchange(tile, sent, spread, ny, nz, cid):
    width = sent.shape[-1]
    sems = exchange_sems(ny)
    dma = pltpu.SemaphoreType.DMA
    return pl.pallas_call(
        lambda *refs: first_kernel(ny, nz, len(sems), *refs),
        out_shape=(
            jax.ShapeDtypeStruct((2, NX, PA, NB), jnp.bfloat16),
            jax.ShapeDtypeStruct((2, 2, NX, PA, NB), jnp.bfloat16),
            jax.ShapeDtypeStruct((ny * CORES, 2, CAP // 2, width), jnp.bfloat16),
            jax.ShapeDtypeStruct((CORES, DCAP, width), jnp.bfloat16),
        ),
        in_specs=[ANY] * 3,
        out_specs=(ANY,) * 4,
        scratch_shapes=sems
        + [dma((nz * NX,)), dma((2,)), dma((NX, 2)), dma((NX, 2)), dma((2, 2)), dma((2, 2))],
        compiler_params=pltpu.CompilerParams(collective_id=cid, has_side_effects=True),
        name="first_exchange",
    )(tile, sent, spread)


def second_kernel(ny, nz, nexch, *refs):
    beside, rows_first, moved_first, slot_in, sent, spread, raw, extra, other, moved, top = refs[:11]
    rows, rows0, moved0, slot, made, small, fetch_sem, small_sem = refs[11:19]
    ex = RowExchange(ny, sent, spread, rows, moved, refs[19 : 19 + nexch])
    (azs, azr, bzs, bzr, bxs, bxr, ss, sr, ts, tr, to_s, to_r) = refs[19 + nexch :]
    total = rows0.shape[0]
    pcol = lax.axis_index("pcol")
    n = nz * NX
    z, x = lax.div(pcol, NX), lax.rem(pcol, NX)

    def to_x(i):
        return {"pcol": z * NX + i}

    def to_z(i):
        return {"pcol": i * NX + x}

    near = ex.barrier_peers()
    near += [to_x(lax.rem(x + d, NX)) for d in (1, NX - 1)]
    near += [to_z(lax.rem(z + d, nz)) for d in range(1, nz)]

    def place(start, size):
        keys = slot[pl.ds(pl.multiple_of(start, HALF), size), :]
        return jnp.where(
            keys == lax.broadcasted_iota(jnp.int32, (size, total), 1), 1.0, 0.0
        ).astype(jnp.bfloat16)

    def place_rows(source, cols):
        def chunk(i, _):
            here = pl.ds(pl.multiple_of(i * HALF, HALF), HALF)
            top[here, cols] = bdot(place(i * HALF, HALF), source())
            return 0

        lax.fori_loop(0, 2 * NB // HALF, chunk, 0)

    def meanwhile():
        fetches = [
            pltpu.make_async_copy(src, dst, fetch_sem.at[k])
            for k, (src, dst) in enumerate(((slot_in, slot), (moved_first, moved0), (rows_first, rows0)))
        ]
        for copy in fetches:
            copy.start()
        for copy in fetches:
            copy.wait()
        first = jnp.where(pcol == 0, NB, 0) + ex.c * HALF
        part = bdot(place(first, HALF), rows0[...])
        last = made.shape[1] - HALF - MOVED
        for k in range(NX):
            lanes = slice(k * LANES, (k + 1) * LANES)
            made[k, pl.ds(0, HALF), :] = part[:, lanes]
            made[k, pl.ds(HALF, MOVED), :] = moved0[:, lanes]
            made[k, pl.ds(HALF + MOVED, last), :] = jnp.zeros((last, LANES), jnp.bfloat16)
        handover = pltpu.make_async_copy(made, small, small_sem)
        handover.start()
        handover.wait()

    meet_with_roots(near, pcol, n, meanwhile)

    def across(index, way, hop, half):
        s, r = (ts.at[way, hop - 1, half], tr.at[way, hop - 1, half]) if hop else (to_s.at[half], to_r.at[half])
        return pltpu.make_async_remote_copy(
            src_ref=extra.at[half, index, pl.ds(0, HALF)], dst_ref=other.at[half, index],
            send_sem=s, recv_sem=r, device_id=ex.partner, device_id_type=MESH)

    crossing = []

    def cross(index, ref, way, hop, half):
        copy = across(index, way, hop, half)
        copy.start()
        crossing.append(copy)

    def band(i):
        return pl.ds(pl.multiple_of(i * PB, PB), PB)

    scatter = Scatter(
        pcol, n,
        lambda to: small.at[lax.rem(to, NX), band(lax.div(to, NX))],
        lambda panel, to: extra.at[panel, lax.rem(to, NX), band(lax.div(to, NX))], ss, sr)
    az = Ring(nz, z, to_z, lambda i, h: raw.at[h, i], azs, azr,
              fresh=lambda way, h: beside.at[way, h], first=2)
    bz = Direct(nz, z, to_z, lambda i, h: extra.at[h, x, band(i)], bzs, bzr)
    bx = Ring(NX, x, to_x, lambda i, h: extra.at[h, i], bxs, bxr, arrived=cross)

    def begin_az():
        for half in (0, 1):
            for way in (0, 1):
                if az.carries(way, 2, half):
                    az.copy(way, 2, half).start()

    def begin_bz():
        for half in (0, 1):
            scatter.landed(half)
            bz.start_half(half)

    def begin_bx(half):
        bz.wait(half)
        bx.start(half)
        cross(x, None, 0, 0, half)

    events = [(-2.0, scatter.start), (-0.9, begin_az)]
    events += ex.events(T_Y)
    events += az.events([T_A0, T_A1], T_AD)
    events += [(T_BZ, begin_bz)]
    events += [(T_BX + h * 0.4, lambda h=h: begin_bx(h)) for h in (0, 1)]
    events += bx.events([T_BX + 0.2, T_BX + 1.2], T_BXD)

    def last_rows():
        ex.finish()
        place_rows(lambda: rows[...].reshape(total, NB), pl.ds(NB, NB))

    events += [(T_TOP, last_rows), (T_PLACE, lambda: place_rows(lambda: rows0[...], pl.ds(0, NB)))]
    run_events(events)
    for ring in (az, bx):
        for half in (0, 1):
            ring.complete(half)
        ring.drain()
    bz.drain()
    scatter.drain()
    for copy in crossing:
        copy.wait()


def second_exchange(beside, rows0, moved0, slot, sent, spread, ny, nz, cid):
    width = sent.shape[-1]
    dma = pltpu.SemaphoreType.DMA
    sems = exchange_sems(ny)
    zring, xring, zdirect = dma((2, nz // 2, 2)), dma((2, NX // 2, 2)), dma((nz, 2))
    return pl.pallas_call(
        lambda *refs: second_kernel(ny, nz, len(sems), *refs),
        out_shape=(
            jax.ShapeDtypeStruct((2, nz, NX, PA, NB), jnp.bfloat16),
            jax.ShapeDtypeStruct((2, NX, nz * PB, LANES), jnp.bfloat16),
            jax.ShapeDtypeStruct((2, NX, HALF, LANES), jnp.bfloat16),
            jax.ShapeDtypeStruct((CORES, DCAP, width), jnp.bfloat16),
            jax.ShapeDtypeStruct((2 * NB, 2 * width), jnp.bfloat16),
        ),
        in_specs=[ANY] * 6,
        out_specs=(ANY,) * 4 + (pl.BlockSpec(memory_space=pltpu.VMEM),),
        scratch_shapes=[
            pltpu.VMEM((ny * CORES, 2, CAP // 2, width), jnp.bfloat16),
            pltpu.VMEM(rows0.shape, jnp.bfloat16),
            pltpu.VMEM(moved0.shape, jnp.bfloat16),
            pltpu.VMEM(slot.shape, jnp.int32),
            pltpu.VMEM((NX, nz * PB, LANES), jnp.bfloat16),
            pltpu.VMEM((NX, nz * PB, LANES), jnp.bfloat16),
            dma((3,)),
            dma,
        ]
        + sems
        + [zring, zring, zdirect, zdirect, xring, xring]
        + [dma((nz * NX,)), dma((2,)), xring, xring, dma((2,)), dma((2,))],
        compiler_params=pltpu.CompilerParams(collective_id=cid, has_side_effects=True),
        name="second_exchange",
    )(beside, rows0, moved0, slot, sent, spread)


def dot(a, b):
    return jnp.dot(a, b, preferred_element_type=jnp.float32)


def bdot(a, b):
    return dot(a, b).astype(jnp.bfloat16)


def ids(shape, axis):
    return lax.broadcasted_iota(jnp.int32, shape, axis).astype(jnp.float32)


def to_row(col):
    n = col.shape[0]
    return jnp.sum(jnp.where(ids((n, n), 0) == ids((n, n), 1), col, 0.0), axis=0, keepdims=True)


def to_col(row):
    n = row.shape[1]
    return jnp.sum(jnp.where(ids((n, n), 0) == ids((n, n), 1), row, 0.0), axis=1, keepdims=True)


def along(table):
    return jnp.sum(table, axis=1, keepdims=True)


def down(table):
    return jnp.sum(table, axis=0, keepdims=True)


def hot(mask):
    return jnp.where(mask, 1.0, 0.0).astype(jnp.bfloat16)


def index_kernel(nprow, piv, tile, sent0, sent1, spread0, spread1, slot_out, into_out, rounds_out):
    prow = lax.axis_index("prow")
    core = lax.rem(prow, CORES).astype(jnp.float32)
    prow_f = prow.astype(jnp.float32)
    rows = [piv[k : k + 1, :].astype(jnp.float32) for k in (0, 1)]
    cols = [to_col(r) for r in rows]
    i0, i1 = ids((NB, NB), 0), ids((NB, NB), 1)
    receive = []
    for k in (0, 1):
        first = float(k * NB)
        top_c, top_r = ids((NB, 1), 0) + first, ids((1, NB), 1) + first
        left_c = 1.0 - along(jnp.where(rows[k] == top_c, 1.0, 0.0))
        left_r = 1.0 - down(jnp.where(cols[k] == top_r, 1.0, 0.0))
        rank_r = down(jnp.where(i0 < i1, left_c, 0.0))
        vac_r = jnp.where(rows[k] >= first + NB, 1.0, 0.0)
        vac_c = along(jnp.where(i1 < i0, vac_r, 0.0))
        receive.append(along(jnp.where((rank_r == vac_c) & (left_r > 0.5), top_r, 0.0)))
    receive0_r = to_row(receive[0])

    def lookup(keys):
        hit = keys == rows[0]
        found = along(jnp.where(hit, 1.0, 0.0))
        return jnp.where(found > 0.5, along(jnp.where(hit, receive0_r, 0.0)), keys)

    src1, from1 = lookup(cols[1]), lookup(receive[1])
    again = along(jnp.where(cols[0] == rows[1], 1.0, 0.0))

    def owner(v):
        return (lax.shift_right_logical(v.astype(jnp.int32), 9) & (nprow - 1)).astype(jnp.float32)

    def local(v):
        v = v.astype(jnp.int32)
        return (lax.shift_right_logical(v, 13) * NB + (v & (NB - 1))).astype(jnp.float32)

    n = 2 * NB
    t_c = jnp.concatenate([cols[0], src1], axis=0)
    d_dst = jnp.concatenate([cols[0], cols[1]], axis=0)
    d_src = jnp.concatenate([receive[0], from1], axis=0)
    fresh = jnp.concatenate([again, jnp.zeros_like(again)], axis=0)
    valid = (d_dst >= 2.0 * NB) & (fresh < 0.5)
    t_group = owner(t_c)
    group = jnp.where(valid, owner(d_dst) * CORES + jnp.where(d_src >= NB, 1.0, 0.0), -1000.0)
    lanes = ids((n, 128), 1)
    members = jnp.where((lanes == t_group) | (lanes == group + nprow), 1.0, 0.0)
    before = dot(hot(ids((n, n), 1) < ids((n, n), 0)), members.astype(jnp.bfloat16)) * members
    is_t = lanes < nprow
    t_rank = along(jnp.where(is_t, before, 0.0))
    d_rank = along(jnp.where(is_t, 0.0, before))
    slot_c = jnp.where(t_rank < CAP, t_group * CAP + t_rank, -1.0)
    key_c = jnp.where(valid & (d_rank < DCAP), group * DCAP + d_rank, -1.0)
    slot_out[...] = slot_c.astype(jnp.int32)
    packed = jnp.where(lanes == 0, slot_c, jnp.where(lanes == 1, local(t_c), jnp.where(lanes == 2, key_c, d_src)))
    packed = packed.T
    slot_r, local_r, key_r, src_r = (packed[k : k + 1, :] for k in range(4))
    mine = ids((CAP, 1), 0) + prow_f * CAP
    pick = along(jnp.where(slot_r == mine, local_r + 1.0, 0.0)) - 1.0
    sent = bdot(hot(pick == ids((CAP, n), 1)), tile[...])
    sent0[...] = sent[:, :NB]
    sent1[...] = sent[:, NB:]
    lane = ids((1, 128), 1)
    wanted = jnp.where(lane < MOVED, lane + prow_f * MOVED, -2.0)
    into = down(jnp.where(key_c == wanted, local(d_dst) + 1.0, 0.0)) - 1.0
    into_out[...] = into.astype(jnp.int32)
    most_t = jnp.max(t_rank) * (1.0 / CAP)
    most_d = jnp.max(jnp.where(valid, d_rank, 0.0)) * (1.0 / DCAP)
    rounds_out[0, 0] = jnp.where(jnp.maximum(most_t, most_d) > 1.0 - 0.25 / CAP, 2, 1).astype(jnp.int32)

    @pl.when(prow < CORES)
    def _():
        s = ids((MOVED, 1), 0)

        def one_chip(q, _):
            second = jnp.where(s >= DCAP, 1.0, 0.0)
            want = (2.0 * q.astype(jnp.float32) + second) * MOVED + core * DCAP + s - second * DCAP
            src = along(jnp.where(key_r == want, src_r + 1.0, 0.0)) - 1.0 - core * NB
            out = bdot(hot(src == ids((MOVED, NB), 1)), tile[:NB, :])
            here = pl.ds(pl.multiple_of(q * MOVED, MOVED), MOVED)
            spread0[here, :] = out[:, :NB]
            spread1[here, :] = out[:, NB:]
            return 0

        lax.fori_loop(0, nprow // 2, one_chip, 0)


def index_and_pack(pivots, tile, nprow):
    n = 2 * NB
    bf16 = jnp.bfloat16
    vmem = pl.BlockSpec(memory_space=pltpu.VMEM)
    return pl.pallas_call(
        lambda *refs: index_kernel(nprow, *refs),
        out_shape=(
            jax.ShapeDtypeStruct((CAP, NB), bf16), jax.ShapeDtypeStruct((CAP, NB), bf16),
            jax.ShapeDtypeStruct((nprow * DCAP, NB), bf16), jax.ShapeDtypeStruct((nprow * DCAP, NB), bf16),
            jax.ShapeDtypeStruct((n, 1), jnp.int32), jax.ShapeDtypeStruct((1, 128), jnp.int32),
            jax.ShapeDtypeStruct((1, 1), jnp.int32),
        ),
        in_specs=[vmem, vmem],
        out_specs=(vmem,) * 6 + (pl.BlockSpec(memory_space=pltpu.SMEM),),
        name="index_and_pack",
    )(pivots, tile)


def update_kernel(into, *refs):
    sources, (raw_in, line, beside), out, held, raw = refs[:8], refs[8:11], refs[11], refs[12:20], refs[20]
    low, up0, up1, sem = refs[21:]
    nz = raw.shape[1]
    z = lax.div(lax.axis_index("pcol"), NX)
    pairs = list(zip(sources, held))
    for k in range(nz):
        at = lax.rem(z + k, nz)
        src = line if k == 0 else beside.at[1] if k == 1 else beside.at[0] if k == nz - 1 else raw_in.at[:, at]
        pairs.append((src, raw.at[:, at]))
    fetches = [pltpu.make_async_copy(src, dst, sem.at[k]) for k, (src, dst) in enumerate(pairs)]
    for copy in fetches:
        copy.start()
    low_inv, up_inv, top, extra, other, moved0, moved1, tile = held
    pcol, prow = lax.axis_index("pcol"), lax.axis_index("prow")
    core = lax.rem(prow, CORES)
    f32 = jnp.float32
    step = NB // 2
    halves = (pl.ds(0, NB), pl.ds(NB, NB))

    def spot(i):
        return pl.ds(pl.multiple_of(i * step, step), step)

    for copy in fetches[:5]:
        copy.wait()
    l0, l1, u0, u1 = low_inv[0], low_inv[1], up_inv[0], up_inv[1]
    panel_tops = []
    for k in (0, 1):
        own = jnp.concatenate([extra[k, x, :HALF, :] for x in range(NX)], axis=1)
        far = jnp.concatenate([other[k, x] for x in range(NX)], axis=1)
        panel_tops.append(jnp.concatenate(
            [jnp.where(core == 0, own, far), jnp.where(core == 0, far, own)], axis=0))
    corner = bdot(panel_tops[0], u0)
    upper = bdot(l0, panel_tops[1])
    moved_panel = [
        jnp.concatenate([extra[k, x, HALF : HALF + MOVED, :] for x in range(NX)], axis=1) for k in (0, 1)
    ]
    for cols in halves:
        up0[:, cols] = bdot(l0, top[pl.ds(0, NB), cols])
        low[:, cols] = (top[pl.ds(NB, NB), cols].astype(f32) - dot(corner, up0[:, cols])).astype(jnp.bfloat16)
        up1[:, cols] = bdot(l1, low[:, cols])
    for copy in fetches[5:]:
        copy.wait()

    def update(i, _):
        here = spot(i)
        ids_c = lax.broadcasted_iota(jnp.int32, (step, MOVED), 0) + i * step
        match = jnp.where(ids_c == into[:, :MOVED], 1.0, 0.0)
        hit = jnp.max(match, axis=1, keepdims=True) > 0.5
        insert = match.astype(jnp.bfloat16)

        lines = pl.ds(i * (step // raw.shape[2]), step // raw.shape[2])

        def with_moved(new, old):
            return jnp.where(hit, dot(insert, new), old.astype(f32)).astype(jnp.bfloat16)

        factor0 = bdot(with_moved(moved_panel[0], raw[0, lines].reshape(step, NB)), u0)
        panel1 = (with_moved(moved_panel[1], raw[1, lines].reshape(step, NB)).astype(f32) - dot(factor0, upper)).astype(jnp.bfloat16)
        factor1 = bdot(panel1, u1)
        for d, (cols, moved) in enumerate(zip(halves, (moved0, moved1))):
            new = with_moved(moved[...], tile[here, cols]).astype(f32)
            new = (new - dot(factor0, up0[:, cols])).astype(jnp.bfloat16).astype(f32)
            new = (new - dot(factor1, up1[:, cols])).astype(jnp.bfloat16)
            if d == 0:
                new = jnp.where(pcol == 0, factor0, jnp.where(pcol == 1, factor1, new))
            out[here, cols] = new
        return 0

    lax.fori_loop(0, 4, update, 0)
    heads = pl.ds(0, NB)

    @pl.when(prow == 0)
    def _():
        out[heads, halves[0]] = jnp.where(pcol == 0, top[heads, halves[0]], up0[:, halves[0]])
        out[heads, halves[1]] = up0[:, halves[1]]

    @pl.when(prow == 1)
    def _():
        out[heads, halves[0]] = jnp.where(
            pcol == 0, corner, jnp.where(pcol == 1, low[:, halves[0]], up1[:, halves[0]]))
        out[heads, halves[1]] = up1[:, halves[1]]


def update(into, *args):
    n = 2 * NB
    vmem = pl.BlockSpec(memory_space=pltpu.VMEM)
    bf16 = jnp.bfloat16
    held = [pltpu.VMEM(a.shape, bf16) for a in args[:9]]
    return pl.pallas_call(
        update_kernel,
        out_shape=jax.ShapeDtypeStruct((n, n), bf16),
        in_specs=[vmem] + [ANY] * len(args),
        out_specs=vmem,
        scratch_shapes=held
        + [pltpu.VMEM((NB, n), bf16)] * 3 + [pltpu.SemaphoreType.DMA((8 + args[8].shape[1],))],
        name="update",
    )(into, *args)


def count_before(flags):
    n = flags.shape[0]
    ahead = jnp.arange(n)[None, :] < jnp.arange(n)[:, None]
    return jnp.sum((ahead & flags[None, :]).astype(jnp.int32), axis=1)


def pairing(sources, first_row):
    top_ids = first_row + jnp.arange(NB, dtype=jnp.int32)
    leftover = jnp.logical_not(jnp.any(sources[None, :] == top_ids[:, None], axis=1))
    left_rank = count_before(leftover)
    vacated = sources >= first_row + NB
    vac_rank = count_before(vacated)
    table = leftover[None, :] & (left_rank[None, :] == vac_rank[:, None])
    return jnp.sum(jnp.where(table, top_ids[None, :], 0), axis=1)


def lookup(keys, names, values):
    hit = keys[:, None] == names[None, :]
    found = jnp.sum(jnp.where(hit, values[None, :], 0), axis=1)
    return jnp.where(jnp.any(hit, axis=1), found, keys)


def rank_in(group):
    n = group.shape[0]
    ahead = jnp.arange(n)[None, :] < jnp.arange(n)[:, None]
    same = group[None, :] == group[:, None]
    return jnp.sum((same & ahead).astype(jnp.int32), axis=1)


def slot_values(keys, values, wanted):
    hit = wanted[:, None] == keys[None, :]
    return jnp.sum(jnp.where(hit, values[None, :] + 1, 0), axis=1) - 1


def one_hot(index, n):
    return (index[:, None] == jnp.arange(n, dtype=jnp.int32)[None, :]).astype(jnp.bfloat16)


def collect_rounds(tile, pivots, nprow, ny):
    prow = lax.axis_index("prow")
    core = lax.rem(prow, CORES)
    s0, s1 = pivots[0], pivots[1]
    receive0, receive1 = pairing(s0, 0), pairing(s1, NB)
    src1 = lookup(s1, s0, receive0)
    from1 = lookup(receive1, s0, receive0)
    again = jnp.any(s0[:, None] == s1[None, :], axis=1)
    big = jnp.int32(1 << 20)

    def owner(rows):
        return lax.rem(rows // NB, nprow)

    def local(rows):
        return rows // (NB * nprow) * NB + lax.rem(rows, NB)

    t_src = jnp.concatenate([s0, src1])
    t_owner = owner(t_src)
    t_rank = rank_in(t_owner)
    t_local = local(t_src)
    d_dst = jnp.concatenate([s0, s1])
    d_src = jnp.concatenate([receive0, from1])
    d_valid = (d_dst >= 2 * NB) & jnp.concatenate([jnp.logical_not(again), jnp.ones((NB,), jnp.bool_)])
    d_core = d_src // NB
    d_owner = owner(d_dst)
    d_rank = rank_in(jnp.where(d_valid, d_owner * CORES + d_core, -1))
    d_local = local(d_dst)
    rounds = jnp.maximum(jnp.max(t_rank) // CAP, jnp.max(jnp.where(d_valid, d_rank, 0)) // DCAP) + 1

    def body(state):
        r, top, now = state
        t_in = (t_rank // CAP) == r
        t_slot = t_owner * CAP + lax.rem(t_rank, CAP)
        t_key = jnp.where(t_in, t_slot, big)
        d_in = d_valid & ((d_rank // DCAP) == r)
        d_key = jnp.where(d_in, (d_owner * CORES + d_core) * DCAP + lax.rem(d_rank, DCAP), big)
        pick = one_hot(slot_values(t_key, t_local, prow * CAP + jnp.arange(CAP, dtype=jnp.int32)), 2 * NB)
        every = jnp.arange(nprow * DCAP, dtype=jnp.int32)
        wanted = (every // DCAP * CORES + core) * DCAP + lax.rem(every, DCAP)
        spread_sel = one_hot(slot_values(d_key, d_src - core * NB, wanted), NB)
        mine = prow * MOVED + jnp.arange(MOVED, dtype=jnp.int32)
        into = slot_values(d_key, d_local, mine)
        insert = (jnp.arange(2 * NB, dtype=jnp.int32)[:, None] == into[None, :]).astype(jnp.bfloat16)
        rows, moved = row_exchange(
            bdot(pick, tile).reshape(2, CAP // 2, 2 * NB),
            bdot(spread_sel, tile[:NB]).reshape(nprow, DCAP, 2 * NB), ny, 1)
        place = one_hot(jnp.where(t_in, t_slot, -1), nprow * CAP)
        top = top + bdot(place, rows.reshape(nprow * CAP, 2 * NB))
        new = bdot(insert, moved.reshape(MOVED, 2 * NB))
        return r + 1, top, jnp.where(jnp.any(insert > 0, axis=1)[:, None], new, now)

    _, top, now = lax.while_loop(
        lambda s: s[0] < rounds, body, (jnp.int32(0), jnp.zeros_like(tile), tile))
    return top, now


def per_device(matrix, pivots, lower_inverse, upper_inverse):
    nprow, npcol = lax.axis_size("prow"), lax.axis_size("pcol")
    ny, nz = nprow // CORES, npcol // NX
    n = 2 * NB
    tile = matrix.reshape(n, n)
    *packed, slot, into, rounds = index_and_pack(pivots, tile, nprow)

    def finish(tile, packed, slot, into, known, cids):
        sents = [v.reshape(2, CAP // 2, NB) for v in packed[:2]]
        spreads = [v.reshape(nprow, DCAP, NB) for v in packed[2:]]
        line, beside, rows0, moved0 = first_exchange(tile, sents[0], spreads[0], ny, nz, cids[0])
        rows0, moved0 = rows0.reshape(nprow * CAP, NB), moved0.reshape(MOVED, NB)
        if known is not None:
            rows0, moved0 = jnp.pad(known[:, :NB], ((0, nprow * CAP - n), (0, 0))), jnp.zeros_like(moved0)
        raw, extra, other, moved1, top = second_exchange(
            beside, rows0, moved0, slot, sents[1], spreads[1], ny, nz, cids[1])
        moved1 = moved1.reshape(MOVED, NB)
        if known is not None:
            moved1, top = jnp.zeros_like(moved1), known
        return update(
            into, lower_inverse, upper_inverse, top, extra, other, moved0, moved1, tile,
            raw.reshape(2, nz, NX * PA, NB), line.reshape(2, NX * PA, NB), beside.reshape(2, 2, NX * PA, NB))

    def one_round(tile):
        return finish(tile, packed, slot, into, None, (0, 2))

    def many_rounds(tile):
        top, now = collect_rounds(tile, pivots, nprow, ny)
        empty = [jnp.zeros_like(v) for v in packed]
        order = jnp.arange(n, dtype=jnp.int32)[:, None]
        return finish(now, empty, order, jnp.full_like(into, -1), top, (3, 4))

    out = lax.cond(rounds[0, 0] > 1, many_rounds, one_round, tile)
    return out.reshape(matrix.shape)


def solution(mesh):
    return jax.shard_map(
        per_device,
        mesh=mesh,
        in_specs=(P(None, "prow", None, None, "pcol", None), P(), P(), P()),
        out_specs=P(None, "prow", None, None, "pcol", None),
        check_vma=False,
    )
```

```python
import jax
import jax.numpy as jnp
from jax import lax
from jax.experimental import pallas as pl
from jax.experimental.pallas import tpu as pltpu
from jax.sharding import PartitionSpec as P

NB = 512
CORES = 2
NX = 4
CAP = 96
DCAP = 56
MOVED = CORES * DCAP
HALF = NB // CORES
LANES = NB // NX
PA = 32
PB = 48
MESH = pl.DeviceIdType.MESH
T_Y, T_A0, T_A1, T_AD, T_BZ, T_BX, T_BXD, T_TOP, T_PLACE = 4.5, 0.0, 2.5, 5.8, 3.5, 11.0, 4.0, 20.5, 0.3
T_PASS, T_LINE = 9.5, 12.8
ANY = pl.BlockSpec(memory_space=pl.ANY)


class Ring:
    def __init__(self, n, pos, goto, item, send, recv, fresh=None, arrived=None, first=1):
        self.first = first
        self.n, self.pos, self.goto, self.item = n, pos, goto, item
        self.send, self.recv = send, recv
        self.fresh, self.arrived = fresh, arrived
        self.got = [0, 0]

    def carries(self, way, hop, half):
        return hop < self.n // 2 or (hop == self.n // 2 and half == way)

    def copy(self, way, hop, half):
        step = 1 if way == 0 else -1
        index = lax.rem(self.pos + self.n - step * (hop - 1), self.n)
        target = lax.rem(self.pos + self.n + step, self.n)
        src = self.item(index, half)
        if hop == self.first and self.fresh is not None:
            src = self.fresh(way, half)
        return pltpu.make_async_remote_copy(
            src_ref=src,
            dst_ref=self.item(index, half),
            send_sem=self.send.at[way, hop - 1, half],
            recv_sem=self.recv.at[way, hop - 1, half],
            device_id=self.goto(target),
            device_id_type=MESH,
        )

    def landed(self, way, hop, half):
        step = 1 if way == 0 else -1
        index = lax.rem(self.pos + self.n - step * hop, self.n)
        ref = self.item(index, half)
        return index, ref, pltpu.make_async_remote_copy(
            src_ref=ref,
            dst_ref=ref,
            send_sem=self.send.at[way, hop - 1, half],
            recv_sem=self.recv.at[way, hop - 1, half],
            device_id=self.goto(lax.rem(self.pos + 1, self.n)),
            device_id_type=MESH,
        )

    def start(self, half):
        for way in (0, 1):
            self.copy(way, self.first, half).start()

    def step(self, way, hop, half):
        index, ref, arrival = self.landed(way, hop, half)
        arrival.wait_recv()
        if self.carries(way, hop + 1, half):
            self.copy(way, hop + 1, half).start()
        self.got[half] += 1
        if self.arrived is not None:
            self.arrived(index, ref, way, hop, half)

    def events(self, t0, dt):
        out = []
        for half in (0, 1):
            for hop in range(self.first, self.n // 2 + 1):
                for way in (0, 1):
                    if self.carries(way, hop, half):
                        when = t0[half] + dt * (hop - self.first + 1)
                        out.append((when, lambda w=way, h=hop, f=half: self.step(w, h, f)))
        return out

    def complete(self, half):
        assert self.got[half] == self.n + 1 - 2 * self.first

    def drain(self):
        for half in (0, 1):
            for hop in range(self.first, self.n // 2 + 1):
                for way in (0, 1):
                    if self.carries(way, hop, half):
                        self.copy(way, hop, half).wait_send()


def run_events(events):
    for _, act in sorted(events, key=lambda e: e[0]):
        act()


class RowExchange:
    def __init__(self, ny, sent, spread, rows, moved, sems):
        self.ny, self.sent, self.spread, self.rows, self.moved = ny, sent, spread, rows, moved
        (self.rs, self.rr, self.fs, self.fr, self.os, self.orr, self.ls, self.es, self.er) = sems
        prow = lax.axis_index("prow")
        self.y, self.c = lax.div(prow, CORES), lax.rem(prow, CORES)
        self.partner = {"prow": self.y * CORES + 1 - self.c}
        self.ring = Ring(
            ny, self.y,
            lambda i: {"prow": i * CORES + self.c},
            lambda i, half: rows.at[i * CORES + self.c, half],
            self.rs, self.rr,
            fresh=lambda way, half: sent.at[half],
            arrived=self.forward,
        )
        self.forwards = []

    def barrier_peers(self):
        ids = [{"prow": lax.rem(self.y + k, self.ny) * CORES + c} for k in range(1, self.ny) for c in (0, 1)]
        return ids + [self.partner]

    def forward_copy(self, index, way, hop, half):
        return pltpu.make_async_remote_copy(
            src_ref=self.rows.at[index * CORES + self.c, half],
            dst_ref=self.rows.at[index * CORES + self.c, half],
            send_sem=self.fs.at[way, hop - 1, half],
            recv_sem=self.fr.at[way, hop - 1, half],
            device_id=self.partner,
            device_id_type=MESH,
        )

    def forward(self, index, ref, way, hop, half):
        copy = self.forward_copy(index, way, hop, half)
        copy.start()
        self.forwards.append((copy, index, way, hop, half))

    def own_copies(self):
        mine = self.rows.at[self.y * CORES + self.c]
        local = pltpu.make_async_copy(self.sent, mine, self.ls.at[0])
        across = pltpu.make_async_remote_copy(
            src_ref=self.sent, dst_ref=mine, send_sem=self.os, recv_sem=self.orr,
            device_id=self.partner, device_id_type=MESH,
        )
        return local, across

    def spread_copy(self, k, core):
        to = lax.rem(self.y + k, self.ny) * CORES + core
        return pltpu.make_async_remote_copy(
            src_ref=self.spread.at[to], dst_ref=self.moved.at[self.c],
            send_sem=self.es.at[k, core], recv_sem=self.er.at[self.c],
            device_id={"prow": to}, device_id_type=MESH,
        )

    def spread_partner(self):
        to = 1 - self.c
        return pltpu.make_async_remote_copy(
            src_ref=self.spread.at[to], dst_ref=self.moved.at[self.c],
            send_sem=self.es.at[0, 0], recv_sem=self.er.at[self.c],
            device_id=self.partner, device_id_type=MESH,
        )

    def spread_own(self):
        return pltpu.make_async_copy(self.spread.at[self.c], self.moved.at[self.c], self.er.at[self.c])

    def begin(self):
        for half in (0, 1):
            self.ring.start(half)
        for copy in self.own_copies():
            copy.start()

    def spread_some(self, ks):
        @pl.when(self.y == 0)
        def _():
            for k in ks:
                for core in (0, 1):
                    self.spread_copy(k, core).start()

    def spread_near(self):
        @pl.when(self.y == 0)
        def _():
            self.spread_partner().start()
            self.spread_own().start()

    def events(self, dt):
        half_n = self.ny // 2
        out = [(-1.0, self.begin), (3.9 * dt, self.spread_near)]
        order = [half_n] + [k for d in range(half_n - 1, 0, -1) for k in (d, self.ny - d)]
        for i, k in enumerate(order):
            out.append((0.1 + i * 0.5 * dt, lambda k=k: self.spread_some([k])))
        return out + self.ring.events([0.0, 0.3 * dt], dt)

    def finish(self):
        local, across = self.own_copies()
        local.wait()
        across.wait()
        self.ring.drain()
        for copy, index, way, hop, half in self.forwards:
            copy.wait_send()
        for copy, index, way, hop, half in self.forwards:
            ref = self.rows.at[index * CORES + 1 - self.c, half]
            pltpu.make_async_remote_copy(
                src_ref=ref, dst_ref=ref,
                send_sem=self.fs.at[way, hop - 1, half], recv_sem=self.fr.at[way, hop - 1, half],
                device_id=self.partner, device_id_type=MESH,
            ).wait_recv()
        for core in (0, 1):
            ref = self.moved.at[core]
            pltpu.make_async_copy(ref, ref, self.er.at[core]).wait()

        @pl.when(self.y == 0)
        def _():
            for k in range(1, self.ny):
                for core in (0, 1):
                    self.spread_copy(k, core).wait_send()
            self.spread_partner().wait_send()


def exchange_sems(ny):
    dma = pltpu.SemaphoreType.DMA
    return [
        dma((2, ny // 2, 2)), dma((2, ny // 2, 2)),
        dma((2, ny // 2, 2)), dma((2, ny // 2, 2)),
        dma, dma, dma((1,)), dma((ny, CORES)), dma((CORES,)),
    ]


def meet(peers):
    barrier = pltpu.get_barrier_semaphore()
    for peer in peers:
        pl.semaphore_signal(barrier, inc=1, device_id=peer, device_id_type=MESH)
    pl.semaphore_wait(barrier, len(peers))


def exchange_kernel(ny, sent, spread, rows, moved, *sems):
    ex = RowExchange(ny, sent, spread, rows, moved, sems)
    meet(ex.barrier_peers())
    run_events(ex.events(3.8))
    ex.finish()


def row_exchange(sent, spread, ny, cid):
    width = sent.shape[-1]
    return pl.pallas_call(
        lambda *refs: exchange_kernel(ny, *refs),
        out_shape=(
            jax.ShapeDtypeStruct((ny * CORES, 2, CAP // 2, width), jnp.bfloat16),
            jax.ShapeDtypeStruct((CORES, DCAP, width), jnp.bfloat16),
        ),
        in_specs=[ANY, ANY],
        out_specs=(ANY, ANY),
        scratch_shapes=exchange_sems(ny),
        compiler_params=pltpu.CompilerParams(collective_id=cid, has_side_effects=True),
        name="row_exchange",
    )(sent, spread)


def meet_with_roots(near, pcol, n, meanwhile=None):
    barrier = pltpu.get_barrier_semaphore()

    def signal(peer):
        pl.semaphore_signal(barrier, inc=1, device_id=peer, device_id_type=MESH)

    for root in (0, 1):
        @pl.when(pcol == root)
        def _():
            for k in range(1, n):
                signal({"pcol": lax.rem(pcol + k, n)})

        @pl.when(pcol != root)
        def _():
            signal({"pcol": root})

    for peer in near:
        signal(peer)
    if meanwhile is not None:
        meanwhile()

    @pl.when(pcol < 2)
    def _():
        pl.semaphore_wait(barrier, len(near) + n)

    @pl.when(pcol >= 2)
    def _():
        pl.semaphore_wait(barrier, len(near) + 2)


class Scatter:
    def __init__(self, pcol, n, piece, slot, send, recv):
        self.pcol, self.n, self.piece, self.slot, self.send, self.recv = pcol, n, piece, slot, send, recv

    def copy(self, k):
        to = lax.rem(self.pcol + k, self.n)
        return pltpu.make_async_remote_copy(
            src_ref=self.piece(to), dst_ref=self.slot(self.pcol, to),
            send_sem=self.send.at[k], recv_sem=self.recv.at[self.pcol],
            device_id={"pcol": to}, device_id_type=MESH)

    def start(self):
        @pl.when(self.pcol < 2)
        def _():
            for k in range(1, self.n):
                self.copy(k).start()
            pltpu.make_async_copy(
                self.piece(self.pcol), self.slot(self.pcol, self.pcol), self.recv.at[self.pcol]
            ).start()

    def landed(self, panel):
        ref = self.slot(panel, self.pcol)
        pltpu.make_async_copy(ref, ref, self.recv.at[panel]).wait()

    def drain(self):
        @pl.when(self.pcol < 2)
        def _():
            for k in range(1, self.n):
                self.copy(k).wait_send()


class Direct:
    def __init__(self, n, pos, goto, item, send, recv):
        self.n, self.pos, self.goto, self.item, self.send, self.recv = n, pos, goto, item, send, recv

    def copy(self, k, half):
        to = lax.rem(self.pos + k, self.n)
        return pltpu.make_async_remote_copy(
            src_ref=self.item(self.pos, half), dst_ref=self.item(self.pos, half),
            send_sem=self.send.at[k, half], recv_sem=self.recv.at[k, half],
            device_id=self.goto(to), device_id_type=MESH)

    def start(self):
        for half in (0, 1):
            self.start_half(half)

    def start_half(self, half):
        for k in sorted(range(1, self.n), key=lambda k: -min(k, self.n - k)):
            self.copy(k, half).start()

    def wait(self, half):
        for k in range(1, self.n):
            ref = self.item(lax.rem(self.pos + self.n - k, self.n), half)
            pltpu.make_async_copy(ref, ref, self.recv.at[k, half]).wait()

    def drain(self):
        for half in (0, 1):
            for k in range(1, self.n):
                self.copy(k, half).wait_send()


def first_kernel(ny, nz, nexch, *refs):
    tile, sent, spread, line, beside, rows, moved = refs[:7]
    ex = RowExchange(ny, sent, spread, rows, moved, refs[7 : 7 + nexch])
    ss, sr, xs, xr, zs, zr = refs[7 + nexch :]
    pcol = lax.axis_index("pcol")
    n = nz * NX
    z, x = lax.div(pcol, NX), lax.rem(pcol, NX)
    scatter = Scatter(
        pcol, n,
        lambda to: tile.at[pl.ds(pl.multiple_of(to * PA, PA), PA), pl.ds(0, NB)],
        lambda panel, to: line.at[panel, lax.rem(to, NX)], ss, sr)
    gather = Direct(NX, x, lambda i: {"pcol": z * NX + i}, lambda i, h: line.at[h, i], xs, xr)
    near = ex.barrier_peers() + [{"pcol": z * NX + lax.rem(x + d, NX)} for d in range(1, NX)]
    around = [{"pcol": lax.rem(z + d, nz) * NX + x} for d in (1, nz - 1)]
    near += around

    def next_line(way, half):
        return pltpu.make_async_remote_copy(
            src_ref=line.at[half], dst_ref=beside.at[way, half],
            send_sem=zs.at[way, half], recv_sem=zr.at[way, half],
            device_id=around[way], device_id_type=MESH)

    def send_lines():
        for half in (0, 1):
            gather.wait(half)
            for way in (0, 1):
                next_line(way, half).start()

    meet_with_roots(near, pcol, n)

    def pass_on():
        for panel in (0, 1):
            scatter.landed(panel)
            gather.start_half(panel)

    run_events(ex.events(3.8) + [(-0.5, scatter.start), (T_PASS, pass_on), (T_LINE, send_lines)])
    ex.finish()
    for half in (0, 1):
        for way in (0, 1):
            next_line(way, half).wait()
    gather.drain()
    scatter.drain()


def first_exchange(tile, sent, spread, ny, nz, cid):
    width = sent.shape[-1]
    sems = exchange_sems(ny)
    dma = pltpu.SemaphoreType.DMA
    return pl.pallas_call(
        lambda *refs: first_kernel(ny, nz, len(sems), *refs),
        out_shape=(
            jax.ShapeDtypeStruct((2, NX, PA, NB), jnp.bfloat16),
            jax.ShapeDtypeStruct((2, 2, NX, PA, NB), jnp.bfloat16),
            jax.ShapeDtypeStruct((ny * CORES, 2, CAP // 2, width), jnp.bfloat16),
            jax.ShapeDtypeStruct((CORES, DCAP, width), jnp.bfloat16),
        ),
        in_specs=[ANY] * 3,
        out_specs=(ANY,) * 4,
        scratch_shapes=sems
        + [dma((nz * NX,)), dma((2,)), dma((NX, 2)), dma((NX, 2)), dma((2, 2)), dma((2, 2))],
        compiler_params=pltpu.CompilerParams(collective_id=cid, has_side_effects=True),
        name="first_exchange",
    )(tile, sent, spread)


def second_kernel(ny, nz, nexch, *refs):
    beside, rows_first, moved_first, slot_in, sent, spread, raw, extra, other, moved, top = refs[:11]
    rows, rows0, moved0, slot, made, small, fetch_sem, small_sem = refs[11:19]
    ex = RowExchange(ny, sent, spread, rows, moved, refs[19 : 19 + nexch])
    (azs, azr, bzs, bzr, bxs, bxr, ss, sr, ts, tr, to_s, to_r) = refs[19 + nexch :]
    total = rows0.shape[0]
    pcol = lax.axis_index("pcol")
    n = nz * NX
    z, x = lax.div(pcol, NX), lax.rem(pcol, NX)

    def to_x(i):
        return {"pcol": z * NX + i}

    def to_z(i):
        return {"pcol": i * NX + x}

    near = ex.barrier_peers()
    near += [to_x(lax.rem(x + d, NX)) for d in (1, NX - 1)]
    near += [to_z(lax.rem(z + d, nz)) for d in range(1, nz)]

    def place(start, size):
        keys = slot[pl.ds(pl.multiple_of(start, HALF), size), :]
        return jnp.where(
            keys == lax.broadcasted_iota(jnp.int32, (size, total), 1), 1.0, 0.0
        ).astype(jnp.bfloat16)

    def place_rows(source, cols):
        def chunk(i, _):
            here = pl.ds(pl.multiple_of(i * HALF, HALF), HALF)
            top[here, cols] = bdot(place(i * HALF, HALF), source())
            return 0

        lax.fori_loop(0, 2 * NB // HALF, chunk, 0)

    def meanwhile():
        fetches = [
            pltpu.make_async_copy(src, dst, fetch_sem.at[k])
            for k, (src, dst) in enumerate(((slot_in, slot), (moved_first, moved0), (rows_first, rows0)))
        ]
        for copy in fetches:
            copy.start()
        for copy in fetches:
            copy.wait()
        first = jnp.where(pcol == 0, NB, 0) + ex.c * HALF
        part = bdot(place(first, HALF), rows0[...])
        last = made.shape[1] - HALF - MOVED
        for k in range(NX):
            lanes = slice(k * LANES, (k + 1) * LANES)
            made[k, pl.ds(0, HALF), :] = part[:, lanes]
            made[k, pl.ds(HALF, MOVED), :] = moved0[:, lanes]
            made[k, pl.ds(HALF + MOVED, last), :] = jnp.zeros((last, LANES), jnp.bfloat16)
        handover = pltpu.make_async_copy(made, small, small_sem)
        handover.start()
        handover.wait()

    meet_with_roots(near, pcol, n, meanwhile)

    def across(index, way, hop, half):
        s, r = (ts.at[way, hop - 1, half], tr.at[way, hop - 1, half]) if hop else (to_s.at[half], to_r.at[half])
        return pltpu.make_async_remote_copy(
            src_ref=extra.at[half, index, pl.ds(0, HALF)], dst_ref=other.at[half, index],
            send_sem=s, recv_sem=r, device_id=ex.partner, device_id_type=MESH)

    crossing = []

    def cross(index, ref, way, hop, half):
        copy = across(index, way, hop, half)
        copy.start()
        crossing.append(copy)

    def band(i):
        return pl.ds(pl.multiple_of(i * PB, PB), PB)

    scatter = Scatter(
        pcol, n,
        lambda to: small.at[lax.rem(to, NX), band(lax.div(to, NX))],
        lambda panel, to: extra.at[panel, lax.rem(to, NX), band(lax.div(to, NX))], ss, sr)
    az = Ring(nz, z, to_z, lambda i, h: raw.at[h, i], azs, azr,
              fresh=lambda way, h: beside.at[way, h], first=2)
    bz = Direct(nz, z, to_z, lambda i, h: extra.at[h, x, band(i)], bzs, bzr)
    bx = Ring(NX, x, to_x, lambda i, h: extra.at[h, i], bxs, bxr, arrived=cross)

    def begin_az():
        for half in (0, 1):
            for way in (0, 1):
                if az.carries(way, 2, half):
                    az.copy(way, 2, half).start()

    def begin_bz():
        for half in (0, 1):
            scatter.landed(half)
            bz.start_half(half)

    def begin_bx(half):
        bz.wait(half)
        bx.start(half)
        cross(x, None, 0, 0, half)

    events = [(-2.0, scatter.start), (-0.9, begin_az)]
    events += ex.events(T_Y)
    events += az.events([T_A0, T_A1], T_AD)
    events += [(T_BZ, begin_bz)]
    events += [(T_BX + h * 0.4, lambda h=h: begin_bx(h)) for h in (0, 1)]
    events += bx.events([T_BX + 0.2, T_BX + 1.2], T_BXD)

    def last_rows():
        ex.finish()
        place_rows(lambda: rows[...].reshape(total, NB), pl.ds(NB, NB))

    events += [(T_TOP, last_rows), (T_PLACE, lambda: place_rows(lambda: rows0[...], pl.ds(0, NB)))]
    run_events(events)
    for ring in (az, bx):
        for half in (0, 1):
            ring.complete(half)
        ring.drain()
    bz.drain()
    scatter.drain()
    for copy in crossing:
        copy.wait()


def second_exchange(beside, rows0, moved0, slot, sent, spread, ny, nz, cid):
    width = sent.shape[-1]
    dma = pltpu.SemaphoreType.DMA
    sems = exchange_sems(ny)
    zring, xring, zdirect = dma((2, nz // 2, 2)), dma((2, NX // 2, 2)), dma((nz, 2))
    return pl.pallas_call(
        lambda *refs: second_kernel(ny, nz, len(sems), *refs),
        out_shape=(
            jax.ShapeDtypeStruct((2, nz, NX, PA, NB), jnp.bfloat16),
            jax.ShapeDtypeStruct((2, NX, nz * PB, LANES), jnp.bfloat16),
            jax.ShapeDtypeStruct((2, NX, HALF, LANES), jnp.bfloat16),
            jax.ShapeDtypeStruct((CORES, DCAP, width), jnp.bfloat16),
            jax.ShapeDtypeStruct((2 * NB, 2 * width), jnp.bfloat16),
        ),
        in_specs=[ANY] * 6,
        out_specs=(ANY,) * 4 + (pl.BlockSpec(memory_space=pltpu.VMEM),),
        scratch_shapes=[
            pltpu.VMEM((ny * CORES, 2, CAP // 2, width), jnp.bfloat16),
            pltpu.VMEM(rows0.shape, jnp.bfloat16),
            pltpu.VMEM(moved0.shape, jnp.bfloat16),
            pltpu.VMEM(slot.shape, jnp.int32),
            pltpu.VMEM((NX, nz * PB, LANES), jnp.bfloat16),
            pltpu.VMEM((NX, nz * PB, LANES), jnp.bfloat16),
            dma((3,)),
            dma,
        ]
        + sems
        + [zring, zring, zdirect, zdirect, xring, xring]
        + [dma((nz * NX,)), dma((2,)), xring, xring, dma((2,)), dma((2,))],
        compiler_params=pltpu.CompilerParams(collective_id=cid, has_side_effects=True),
        name="second_exchange",
    )(beside, rows0, moved0, slot, sent, spread)


def dot(a, b):
    return jnp.dot(a, b, preferred_element_type=jnp.float32)


def bdot(a, b):
    return dot(a, b).astype(jnp.bfloat16)


def ids(shape, axis):
    return lax.broadcasted_iota(jnp.int32, shape, axis).astype(jnp.float32)


def to_row(col):
    n = col.shape[0]
    return jnp.sum(jnp.where(ids((n, n), 0) == ids((n, n), 1), col, 0.0), axis=0, keepdims=True)


def to_col(row):
    n = row.shape[1]
    return jnp.sum(jnp.where(ids((n, n), 0) == ids((n, n), 1), row, 0.0), axis=1, keepdims=True)


def along(table):
    return jnp.sum(table, axis=1, keepdims=True)


def down(table):
    return jnp.sum(table, axis=0, keepdims=True)


def hot(mask):
    return jnp.where(mask, 1.0, 0.0).astype(jnp.bfloat16)


def index_kernel(nprow, piv, tile, sent0, sent1, spread0, spread1, slot_out, into_out, rounds_out):
    prow = lax.axis_index("prow")
    core = lax.rem(prow, CORES).astype(jnp.float32)
    prow_f = prow.astype(jnp.float32)
    rows = [piv[k : k + 1, :].astype(jnp.float32) for k in (0, 1)]
    cols = [to_col(r) for r in rows]
    i0, i1 = ids((NB, NB), 0), ids((NB, NB), 1)
    receive = []
    for k in (0, 1):
        first = float(k * NB)
        top_c, top_r = ids((NB, 1), 0) + first, ids((1, NB), 1) + first
        left_c = 1.0 - along(jnp.where(rows[k] == top_c, 1.0, 0.0))
        left_r = 1.0 - down(jnp.where(cols[k] == top_r, 1.0, 0.0))
        rank_r = down(jnp.where(i0 < i1, left_c, 0.0))
        vac_r = jnp.where(rows[k] >= first + NB, 1.0, 0.0)
        vac_c = along(jnp.where(i1 < i0, vac_r, 0.0))
        receive.append(along(jnp.where((rank_r == vac_c) & (left_r > 0.5), top_r, 0.0)))
    receive0_r = to_row(receive[0])

    def lookup(keys):
        hit = keys == rows[0]
        found = along(jnp.where(hit, 1.0, 0.0))
        return jnp.where(found > 0.5, along(jnp.where(hit, receive0_r, 0.0)), keys)

    src1, from1 = lookup(cols[1]), lookup(receive[1])
    again = along(jnp.where(cols[0] == rows[1], 1.0, 0.0))

    def owner(v):
        return (lax.shift_right_logical(v.astype(jnp.int32), 9) & (nprow - 1)).astype(jnp.float32)

    def local(v):
        v = v.astype(jnp.int32)
        return (lax.shift_right_logical(v, 13) * NB + (v & (NB - 1))).astype(jnp.float32)

    n = 2 * NB
    t_c = jnp.concatenate([cols[0], src1], axis=0)
    d_dst = jnp.concatenate([cols[0], cols[1]], axis=0)
    d_src = jnp.concatenate([receive[0], from1], axis=0)
    fresh = jnp.concatenate([again, jnp.zeros_like(again)], axis=0)
    valid = (d_dst >= 2.0 * NB) & (fresh < 0.5)
    t_group = owner(t_c)
    group = jnp.where(valid, owner(d_dst) * CORES + jnp.where(d_src >= NB, 1.0, 0.0), -1000.0)
    lanes = ids((n, 128), 1)
    members = jnp.where((lanes == t_group) | (lanes == group + nprow), 1.0, 0.0)
    before = dot(hot(ids((n, n), 1) < ids((n, n), 0)), members.astype(jnp.bfloat16)) * members
    is_t = lanes < nprow
    t_rank = along(jnp.where(is_t, before, 0.0))
    d_rank = along(jnp.where(is_t, 0.0, before))
    slot_c = jnp.where(t_rank < CAP, t_group * CAP + t_rank, -1.0)
    key_c = jnp.where(valid & (d_rank < DCAP), group * DCAP + d_rank, -1.0)
    slot_out[...] = slot_c.astype(jnp.int32)
    packed = jnp.where(lanes == 0, slot_c, jnp.where(lanes == 1, local(t_c), jnp.where(lanes == 2, key_c, d_src)))
    packed = packed.T
    slot_r, local_r, key_r, src_r = (packed[k : k + 1, :] for k in range(4))
    mine = ids((CAP, 1), 0) + prow_f * CAP
    pick = along(jnp.where(slot_r == mine, local_r + 1.0, 0.0)) - 1.0
    sent = bdot(hot(pick == ids((CAP, n), 1)), tile[...])
    sent0[...] = sent[:, :NB]
    sent1[...] = sent[:, NB:]
    lane = ids((1, 128), 1)
    wanted = jnp.where(lane < MOVED, lane + prow_f * MOVED, -2.0)
    into = down(jnp.where(key_c == wanted, local(d_dst) + 1.0, 0.0)) - 1.0
    into_out[...] = into.astype(jnp.int32)
    most_t = jnp.max(t_rank) * (1.0 / CAP)
    most_d = jnp.max(jnp.where(valid, d_rank, 0.0)) * (1.0 / DCAP)
    rounds_out[0, 0] = jnp.where(jnp.maximum(most_t, most_d) > 1.0 - 0.25 / CAP, 2, 1).astype(jnp.int32)

    @pl.when(prow < CORES)
    def _():
        s = ids((MOVED, 1), 0)

        def one_chip(q, _):
            second = jnp.where(s >= DCAP, 1.0, 0.0)
            want = (2.0 * q.astype(jnp.float32) + second) * MOVED + core * DCAP + s - second * DCAP
            src = along(jnp.where(key_r == want, src_r + 1.0, 0.0)) - 1.0 - core * NB
            out = bdot(hot(src == ids((MOVED, NB), 1)), tile[:NB, :])
            here = pl.ds(pl.multiple_of(q * MOVED, MOVED), MOVED)
            spread0[here, :] = out[:, :NB]
            spread1[here, :] = out[:, NB:]
            return 0

        lax.fori_loop(0, nprow // 2, one_chip, 0)


def index_and_pack(pivots, tile, nprow):
    n = 2 * NB
    bf16 = jnp.bfloat16
    vmem = pl.BlockSpec(memory_space=pltpu.VMEM)
    return pl.pallas_call(
        lambda *refs: index_kernel(nprow, *refs),
        out_shape=(
            jax.ShapeDtypeStruct((CAP, NB), bf16), jax.ShapeDtypeStruct((CAP, NB), bf16),
            jax.ShapeDtypeStruct((nprow * DCAP, NB), bf16), jax.ShapeDtypeStruct((nprow * DCAP, NB), bf16),
            jax.ShapeDtypeStruct((n, 1), jnp.int32), jax.ShapeDtypeStruct((1, 128), jnp.int32),
            jax.ShapeDtypeStruct((1, 1), jnp.int32),
        ),
        in_specs=[vmem, vmem],
        out_specs=(vmem,) * 6 + (pl.BlockSpec(memory_space=pltpu.SMEM),),
        name="index_and_pack",
    )(pivots, tile)


def update_kernel(into, *refs):
    sources, (raw_in, line, beside), out, held, raw = refs[:8], refs[8:11], refs[11], refs[12:20], refs[20]
    low, up0, up1, sem = refs[21:]
    nz = raw.shape[1]
    z = lax.div(lax.axis_index("pcol"), NX)
    pairs = list(zip(sources, held))
    for k in range(nz):
        at = lax.rem(z + k, nz)
        src = line if k == 0 else beside.at[1] if k == 1 else beside.at[0] if k == nz - 1 else raw_in.at[:, at]
        pairs.append((src, raw.at[:, at]))
    fetches = [pltpu.make_async_copy(src, dst, sem.at[k]) for k, (src, dst) in enumerate(pairs)]
    for copy in fetches:
        copy.start()
    low_inv, up_inv, top, extra, other, moved0, moved1, tile = held
    pcol, prow = lax.axis_index("pcol"), lax.axis_index("prow")
    core = lax.rem(prow, CORES)
    f32 = jnp.float32
    step = NB // 2
    halves = (pl.ds(0, NB), pl.ds(NB, NB))

    def spot(i):
        return pl.ds(pl.multiple_of(i * step, step), step)

    for copy in fetches[:5]:
        copy.wait()
    l0, l1, u0, u1 = low_inv[0], low_inv[1], up_inv[0], up_inv[1]
    panel_tops = []
    for k in (0, 1):
        own = jnp.concatenate([extra[k, x, :HALF, :] for x in range(NX)], axis=1)
        far = jnp.concatenate([other[k, x] for x in range(NX)], axis=1)
        panel_tops.append(jnp.concatenate(
            [jnp.where(core == 0, own, far), jnp.where(core == 0, far, own)], axis=0))
    corner = bdot(panel_tops[0], u0)
    upper = bdot(l0, panel_tops[1])
    moved_panel = [
        jnp.concatenate([extra[k, x, HALF : HALF + MOVED, :] for x in range(NX)], axis=1) for k in (0, 1)
    ]
    for cols in halves:
        up0[:, cols] = bdot(l0, top[pl.ds(0, NB), cols])
        low[:, cols] = (top[pl.ds(NB, NB), cols].astype(f32) - dot(corner, up0[:, cols])).astype(jnp.bfloat16)
        up1[:, cols] = bdot(l1, low[:, cols])
    for copy in fetches[5:]:
        copy.wait()

    def update(i, _):
        here = spot(i)
        ids_c = lax.broadcasted_iota(jnp.int32, (step, MOVED), 0) + i * step
        match = jnp.where(ids_c == into[:, :MOVED], 1.0, 0.0)
        hit = jnp.max(match, axis=1, keepdims=True) > 0.5
        insert = match.astype(jnp.bfloat16)

        lines = pl.ds(i * (step // raw.shape[2]), step // raw.shape[2])

        def with_moved(new, old):
            return jnp.where(hit, dot(insert, new), old.astype(f32)).astype(jnp.bfloat16)

        factor0 = bdot(with_moved(moved_panel[0], raw[0, lines].reshape(step, NB)), u0)
        panel1 = (with_moved(moved_panel[1], raw[1, lines].reshape(step, NB)).astype(f32) - dot(factor0, upper)).astype(jnp.bfloat16)
        factor1 = bdot(panel1, u1)
        for d, (cols, moved) in enumerate(zip(halves, (moved0, moved1))):
            new = with_moved(moved[...], tile[here, cols]).astype(f32)
            new = (new - dot(factor0, up0[:, cols])).astype(jnp.bfloat16).astype(f32)
            new = (new - dot(factor1, up1[:, cols])).astype(jnp.bfloat16)
            if d == 0:
                new = jnp.where(pcol == 0, factor0, jnp.where(pcol == 1, factor1, new))
            out[here, cols] = new
        return 0

    lax.fori_loop(0, 4, update, 0)
    heads = pl.ds(0, NB)

    @pl.when(prow == 0)
    def _():
        out[heads, halves[0]] = jnp.where(pcol == 0, top[heads, halves[0]], up0[:, halves[0]])
        out[heads, halves[1]] = up0[:, halves[1]]

    @pl.when(prow == 1)
    def _():
        out[heads, halves[0]] = jnp.where(
            pcol == 0, corner, jnp.where(pcol == 1, low[:, halves[0]], up1[:, halves[0]]))
        out[heads, halves[1]] = up1[:, halves[1]]


def update(into, *args):
    n = 2 * NB
    vmem = pl.BlockSpec(memory_space=pltpu.VMEM)
    bf16 = jnp.bfloat16
    held = [pltpu.VMEM(a.shape, bf16) for a in args[:9]]
    return pl.pallas_call(
        update_kernel,
        out_shape=jax.ShapeDtypeStruct((n, n), bf16),
        in_specs=[vmem] + [ANY] * len(args),
        out_specs=vmem,
        scratch_shapes=held
        + [pltpu.VMEM((NB, n), bf16)] * 3 + [pltpu.SemaphoreType.DMA((8 + args[8].shape[1],))],
        name="update",
    )(into, *args)


def count_before(flags):
    n = flags.shape[0]
    ahead = jnp.arange(n)[None, :] < jnp.arange(n)[:, None]
    return jnp.sum((ahead & flags[None, :]).astype(jnp.int32), axis=1)


def pairing(sources, first_row):
    top_ids = first_row + jnp.arange(NB, dtype=jnp.int32)
    leftover = jnp.logical_not(jnp.any(sources[None, :] == top_ids[:, None], axis=1))
    left_rank = count_before(leftover)
    vacated = sources >= first_row + NB
    vac_rank = count_before(vacated)
    table = leftover[None, :] & (left_rank[None, :] == vac_rank[:, None])
    return jnp.sum(jnp.where(table, top_ids[None, :], 0), axis=1)


def lookup(keys, names, values):
    hit = keys[:, None] == names[None, :]
    found = jnp.sum(jnp.where(hit, values[None, :], 0), axis=1)
    return jnp.where(jnp.any(hit, axis=1), found, keys)


def rank_in(group):
    n = group.shape[0]
    ahead = jnp.arange(n)[None, :] < jnp.arange(n)[:, None]
    same = group[None, :] == group[:, None]
    return jnp.sum((same & ahead).astype(jnp.int32), axis=1)


def slot_values(keys, values, wanted):
    hit = wanted[:, None] == keys[None, :]
    return jnp.sum(jnp.where(hit, values[None, :] + 1, 0), axis=1) - 1


def one_hot(index, n):
    return (index[:, None] == jnp.arange(n, dtype=jnp.int32)[None, :]).astype(jnp.bfloat16)


def collect_rounds(tile, pivots, nprow, ny):
    prow = lax.axis_index("prow")
    core = lax.rem(prow, CORES)
    s0, s1 = pivots[0], pivots[1]
    receive0, receive1 = pairing(s0, 0), pairing(s1, NB)
    src1 = lookup(s1, s0, receive0)
    from1 = lookup(receive1, s0, receive0)
    again = jnp.any(s0[:, None] == s1[None, :], axis=1)
    big = jnp.int32(1 << 20)

    def owner(rows):
        return lax.rem(rows // NB, nprow)

    def local(rows):
        return rows // (NB * nprow) * NB + lax.rem(rows, NB)

    t_src = jnp.concatenate([s0, src1])
    t_owner = owner(t_src)
    t_rank = rank_in(t_owner)
    t_local = local(t_src)
    d_dst = jnp.concatenate([s0, s1])
    d_src = jnp.concatenate([receive0, from1])
    d_valid = (d_dst >= 2 * NB) & jnp.concatenate([jnp.logical_not(again), jnp.ones((NB,), jnp.bool_)])
    d_core = d_src // NB
    d_owner = owner(d_dst)
    d_rank = rank_in(jnp.where(d_valid, d_owner * CORES + d_core, -1))
    d_local = local(d_dst)
    rounds = jnp.maximum(jnp.max(t_rank) // CAP, jnp.max(jnp.where(d_valid, d_rank, 0)) // DCAP) + 1

    def body(state):
        r, top, now = state
        t_in = (t_rank // CAP) == r
        t_slot = t_owner * CAP + lax.rem(t_rank, CAP)
        t_key = jnp.where(t_in, t_slot, big)
        d_in = d_valid & ((d_rank // DCAP) == r)
        d_key = jnp.where(d_in, (d_owner * CORES + d_core) * DCAP + lax.rem(d_rank, DCAP), big)
        pick = one_hot(slot_values(t_key, t_local, prow * CAP + jnp.arange(CAP, dtype=jnp.int32)), 2 * NB)
        every = jnp.arange(nprow * DCAP, dtype=jnp.int32)
        wanted = (every // DCAP * CORES + core) * DCAP + lax.rem(every, DCAP)
        spread_sel = one_hot(slot_values(d_key, d_src - core * NB, wanted), NB)
        mine = prow * MOVED + jnp.arange(MOVED, dtype=jnp.int32)
        into = slot_values(d_key, d_local, mine)
        insert = (jnp.arange(2 * NB, dtype=jnp.int32)[:, None] == into[None, :]).astype(jnp.bfloat16)
        rows, moved = row_exchange(
            bdot(pick, tile).reshape(2, CAP // 2, 2 * NB),
            bdot(spread_sel, tile[:NB]).reshape(nprow, DCAP, 2 * NB), ny, 1)
        place = one_hot(jnp.where(t_in, t_slot, -1), nprow * CAP)
        top = top + bdot(place, rows.reshape(nprow * CAP, 2 * NB))
        new = bdot(insert, moved.reshape(MOVED, 2 * NB))
        return r + 1, top, jnp.where(jnp.any(insert > 0, axis=1)[:, None], new, now)

    _, top, now = lax.while_loop(
        lambda s: s[0] < rounds, body, (jnp.int32(0), jnp.zeros_like(tile), tile))
    return top, now


def per_device(matrix, pivots, lower_inverse, upper_inverse):
    nprow, npcol = lax.axis_size("prow"), lax.axis_size("pcol")
    ny, nz = nprow // CORES, npcol // NX
    n = 2 * NB
    tile = matrix.reshape(n, n)
    *packed, slot, into, rounds = index_and_pack(pivots, tile, nprow)

    def finish(tile, packed, slot, into, known, cids):
        sents = [v.reshape(2, CAP // 2, NB) for v in packed[:2]]
        spreads = [v.reshape(nprow, DCAP, NB) for v in packed[2:]]
        line, beside, rows0, moved0 = first_exchange(tile, sents[0], spreads[0], ny, nz, cids[0])
        rows0, moved0 = rows0.reshape(nprow * CAP, NB), moved0.reshape(MOVED, NB)
        if known is not None:
            rows0, moved0 = jnp.pad(known[:, :NB], ((0, nprow * CAP - n), (0, 0))), jnp.zeros_like(moved0)
        raw, extra, other, moved1, top = second_exchange(
            beside, rows0, moved0, slot, sents[1], spreads[1], ny, nz, cids[1])
        moved1 = moved1.reshape(MOVED, NB)
        if known is not None:
            moved1, top = jnp.zeros_like(moved1), known
        return update(
            into, lower_inverse, upper_inverse, top, extra, other, moved0, moved1, tile,
            raw.reshape(2, nz, NX * PA, NB), line.reshape(2, NX * PA, NB), beside.reshape(2, 2, NX * PA, NB))

    def one_round(tile):
        return finish(tile, packed, slot, into, None, (0, 2))

    def many_rounds(tile):
        top, now = collect_rounds(tile, pivots, nprow, ny)
        empty = [jnp.zeros_like(v) for v in packed]
        order = jnp.arange(n, dtype=jnp.int32)[:, None]
        return finish(now, empty, order, jnp.full_like(into, -1), top, (3, 4))

    out = lax.cond(rounds[0, 0] > 1, many_rounds, one_round, tile)
    return out.reshape(matrix.shape)


def solution(mesh):
    return jax.shard_map(
        per_device,
        mesh=mesh,
        in_specs=(P(None, "prow", None, None, "pcol", None), P(), P(), P()),
        out_specs=P(None, "prow", None, None, "pcol", None),
        check_vma=False,
    )
```
